32 devices in a mesh: row: 8 (over y, x, core), col: 4 (over z).
Axes of the slice: x: 2, y: 2, z: 4, core: 2. Of those that a mesh axis runs over, the one named last changes fastest.
Arguments:
- mask: float32 [4096, 4096], P('row', 'col'), may hold values from -6 to 6
- target: bfloat16 [4096, 4096], P('row', 'col'), may hold values from 0 to 1
- live: int32 [8, 8], P('row', 'col'), may hold values from 0 to 1, as said below
- pupils: float32 [2, 12, 144, 144], replicated, may hold values from -8 to 8
- weights: float32 [12], replicated, may hold values from 0.1 to 1
Outputs:
- updated_mask: float32 [4096, 4096], P('row', 'col')
The draws below stay inside these ranges and needn't reach their ends.
Inputs may be any that keep to these rules, and one draw needn't show every extreme that they name: In each tile row exactly 2 tiles are live and the others are 0; all 2 tiles of at least one device of the row are live.
All inputs are finite; a program needn't handle non-finite values.
Results may differ from the reference program's by a relative error of at most 0.013.
Values may be sent and summed in bfloat16 or wider, within the bound.
No kernel may reach another device: no remote copies, remote signals or barrier semaphores. Data moves between devices by JAX's collectives and lax.ppermute only.
A program may use at most 128 MiB of HBM per device.

```python
import math
import jax
import jax.numpy as jnp
from jax import lax

TILE = 512
AMBIT = 128
KC = 144
KERNELS = 12
SLOTS = 2
TROWS = 8
GROUP = 4
TCOLS = 8
LIVE_ROW = 2
HEIGHT = 4096
WIDTH = 4096


def draw_live(key, part):
    key_scores, key_holder = jax.random.split(key)
    columns = jnp.arange(TCOLS, dtype=jnp.int32)
    scores = jax.random.randint(key_scores, (TROWS, TCOLS), 0, 1 << 20, dtype=jnp.int32) * TCOLS + columns[None, :]
    chosen = jax.random.randint(key_holder, (TROWS, 1), 0, GROUP, dtype=jnp.int32)
    holder = columns[None, :] // SLOTS
    scores = scores + jnp.where(holder == chosen, 1 << 26, 0).astype(jnp.int32)
    cutoff = lax.top_k(scores, LIVE_ROW)[0][:, -1:]
    return (scores >= cutoff).astype(jnp.int32)


def shard_levels(own_key, shape, shards, least, largest):
    loudness, own = 1.0, jax.random.fold_in(own_key, 6)
    for dim, parts in shards:
        steps = jnp.exp(jax.random.uniform(jax.random.fold_in(own, dim), (parts,), jnp.float32, least / len(shards), largest / len(shards)))
        loudness = loudness * jnp.repeat(steps, shape[dim] // parts).reshape([-1 if axis == dim else 1 for axis in range(len(shape))])
    return loudness


def gaussian(stream_key, shape, width, bound, cuts=(), held_as=jnp.bfloat16):
    values = width * jax.random.normal(stream_key, shape, jnp.float32)
    if cuts:
        values = values * shard_levels(stream_key, shape, cuts, -0.22, 0.18)
    return jnp.clip(values, -bound, bound).astype(held_as)


def setup_inputs(seed: int = 0) -> dict:
    arg_keys = jax.random.split(jax.random.key(seed), 6)
    mask = gaussian(arg_keys[0], (HEIGHT, WIDTH), 1.0, 6.0, ((0, 8), (1, 4)), jnp.float32)
    target = jnp.clip(1.0 * jax.random.uniform(arg_keys[1], (HEIGHT, WIDTH), jnp.float32) ** shard_levels(arg_keys[1], (HEIGHT, WIDTH), ((0, 8), (1, 4)), -0.2, 0.2), 0.0, 1.0).astype(jnp.bfloat16)
    live = draw_live(jax.random.fold_in(arg_keys[5], 71), 0)
    pupils = gaussian(arg_keys[3], (2, KERNELS, KC, KC), 1.75, 8.0, (), jnp.float32)
    weights = jnp.clip(jnp.exp(jax.random.uniform(arg_keys[4], (KERNELS,), jnp.float32, math.log(0.1), math.log(1.0))), 0.1, 1.0)
    return dict(mask=mask, target=target, live=live, pupils=pupils, weights=weights)


steepness = 4.0
threshold_level = 1.0
step_rate = 8.0

def matmul(leading, trailing):
    return jnp.dot(leading, trailing, preferred_element_type=jnp.float32)

def contract_first(leading, trailing):
    return lax.dot_general(leading, trailing, (((0,), (0,)), ((), ())), preferred_element_type=jnp.float32)

def contract_last(leading, trailing):
    return lax.dot_general(leading, trailing, (((1,), (1,)), ((), ())), preferred_element_type=jnp.float32)

def cosine_pair(freq_count, pixel_count, offset, period):
    frequency = jnp.arange(freq_count, dtype=jnp.int32) - freq_count // 2
    pixels = jnp.arange(pixel_count, dtype=jnp.int32) + offset
    phases = jnp.mod(frequency[:, None] * pixels[None, :], period).astype(jnp.float32)
    angles = phases * (2.0 * math.pi / period)
    factor = 1.0 / math.sqrt(period)
    return ((jnp.cos(angles) * factor).astype(jnp.bfloat16), (jnp.sin(angles) * factor).astype(jnp.bfloat16))

def transform_tables(spectrum_size, tile_size, ambit_size):
    extent = tile_size + 2 * ambit_size
    outer_cos, outer_sin = cosine_pair(spectrum_size, extent, 0, extent)
    forward = jnp.concatenate([outer_cos, outer_sin], axis=0)
    inner_cos, inner_sin = cosine_pair(spectrum_size, tile_size, ambit_size, extent)
    inverse = jnp.concatenate([inner_cos, inner_sin], axis=0)
    rotate = jnp.concatenate([jnp.concatenate([inner_cos, inner_sin], axis=1), jnp.concatenate([-inner_sin, inner_cos], axis=1)], axis=0)
    return (forward, inverse, rotate)

def spectrum(extended, forward):
    spectrum_size = forward.shape[0] // 2
    partial_rows = matmul(forward, extended).astype(jnp.bfloat16)
    blocks = contract_last(partial_rows, forward)
    real_spectrum = blocks[:spectrum_size, :spectrum_size] - blocks[spectrum_size:, spectrum_size:]
    imaginary_spectrum = -(blocks[:spectrum_size, spectrum_size:] + blocks[spectrum_size:, :spectrum_size])
    return jnp.stack([real_spectrum, imaginary_spectrum]).astype(jnp.bfloat16)

def spectral_gradient(spectra, goal_tile, live_flag, pupils, weights, inverse, rotate):
    real_spectrum = spectra[0].astype(jnp.float32)
    imaginary_spectrum = spectra[1].astype(jnp.float32)
    tile_size = inverse.shape[1]
    spectrum_size = real_spectrum.shape[0]

    def forward_kernel(intensity, inputs):
        pupil_real, pupil_imaginary, weight = inputs
        wave_real = pupil_real * real_spectrum - pupil_imaginary * imaginary_spectrum
        wave_imaginary = pupil_real * imaginary_spectrum + pupil_imaginary * real_spectrum
        amplitude = jnp.concatenate([jnp.concatenate([wave_real, -wave_imaginary], axis=1), jnp.concatenate([wave_imaginary, wave_real], axis=1)], axis=0).astype(jnp.bfloat16)
        section_one = matmul(amplitude, inverse).astype(jnp.bfloat16)
        field_pair = contract_first(rotate, section_one)
        energy = field_pair[:tile_size] ** 2 + field_pair[tile_size:] ** 2
        return (intensity + weight * energy, field_pair.astype(jnp.bfloat16))
    initial = jnp.zeros((tile_size, tile_size), jnp.float32)
    intensity, fields = lax.scan(forward_kernel, initial, (pupils[0], pupils[1], weights))
    resist = jax.nn.sigmoid(steepness * (intensity - threshold_level))
    slope_map = live_flag * (resist - goal_tile.astype(jnp.float32)) * steepness * resist * (1.0 - resist)
    doubled = jnp.concatenate([slope_map, slope_map], axis=0)

    def backward_kernel(totals, inputs):
        pupil_real, pupil_imaginary, weight, field_pair = inputs
        cotangent = (2.0 * weight * doubled * field_pair.astype(jnp.float32)).astype(jnp.bfloat16)
        section_back = matmul(rotate, cotangent).astype(jnp.bfloat16)
        wave_back = contract_last(section_back, inverse)
        adjoint_real = wave_back[:spectrum_size, :spectrum_size] + wave_back[spectrum_size:, spectrum_size:]
        adjoint_imaginary = wave_back[spectrum_size:, :spectrum_size] - wave_back[:spectrum_size, spectrum_size:]
        total_real = totals[0] + pupil_real * adjoint_real + pupil_imaginary * adjoint_imaginary
        total_imaginary = totals[1] - pupil_imaginary * adjoint_real + pupil_real * adjoint_imaginary
        return ((total_real, total_imaginary), None)
    empty_spec = jnp.zeros((spectrum_size, spectrum_size), jnp.float32)
    sums, unused = lax.scan(backward_kernel, (empty_spec, empty_spec), (pupils[0], pupils[1], weights, fields))
    return jnp.stack([sums[0], sums[1]]).astype(jnp.bfloat16)

def pixel_gradient(gradient, forward):
    adjoint_real = gradient[0]
    adjoint_imaginary = gradient[1]
    upper_rows = jnp.concatenate([adjoint_real, -adjoint_imaginary], axis=1)
    lower_rows = jnp.concatenate([-adjoint_imaginary, -adjoint_real], axis=1)
    blocks = jnp.concatenate([upper_rows, lower_rows], axis=0)
    partial_rows = matmul(blocks, forward).astype(jnp.bfloat16)
    return contract_first(forward, partial_rows)

def tile_gradient(extended, goal_tile, live_flag, pupils, weights, forward, inverse, rotate):
    spectra = spectrum(extended, forward)
    gradient = spectral_gradient(spectra, goal_tile, live_flag, pupils, weights, inverse, rotate)
    return pixel_gradient(gradient, forward)

def reference(mask, target, live, pupils, weights):
    forward, inverse, rotate = transform_tables(KC, TILE, AMBIT)
    padded = jnp.pad(mask.astype(jnp.bfloat16), AMBIT)
    tile_rows = live.shape[0]
    tile_cols = live.shape[1]
    extent = TILE + 2 * AMBIT

    def one_tile(total, index):
        row_index = (index // tile_cols).astype(jnp.int32)
        col_index = (index % tile_cols).astype(jnp.int32)
        row_start = (row_index * TILE).astype(jnp.int32)
        col_start = (col_index * TILE).astype(jnp.int32)
        extended = lax.dynamic_slice(padded, (row_start, col_start), (extent, extent))
        goal_tile = lax.dynamic_slice(target, (row_start, col_start), (TILE, TILE))
        live_flag = live[row_index, col_index]

        def compute():
            return tile_gradient(extended, goal_tile, live_flag.astype(jnp.float32), pupils, weights, forward, inverse, rotate)

        def skipped():
            return jnp.zeros((extent, extent), jnp.float32)
        piece = lax.cond(live_flag > 0, compute, skipped)
        current = lax.dynamic_slice(total, (row_start, col_start), (extent, extent))
        return (lax.dynamic_update_slice(total, current + piece, (row_start, col_start)), None)
    initial = jnp.zeros(padded.shape, jnp.float32)
    total, unused = lax.scan(one_tile, initial, jnp.arange(tile_rows * tile_cols, dtype=jnp.int32))
    gradient = total[AMBIT:AMBIT + mask.shape[0], AMBIT:AMBIT + mask.shape[1]]
    return mask - step_rate * gradient
```

```python
from functools import partial
import math

import jax
import jax.numpy as jnp
import numpy as np
from jax import lax
from jax.experimental import pallas as pl
from jax.experimental.pallas import tpu as pltpu
from jax.sharding import PartitionSpec as P

AMBIT = 128

steepness = 4.0
threshold_level = 1.0
step_rate = 8.0

VMEM_LIMIT = 60 * 1024 * 1024


def round_up(value, unit):
    return -(-value // unit) * unit


def shifted(block, axis, step):
    count = lax.axis_size(axis)
    pairs = [(i, i + step) for i in range(count) if 0 <= i + step < count]
    return lax.ppermute(block, axis, pairs)


def dot(leading, trailing):
    return jnp.dot(leading, trailing, preferred_element_type=jnp.float32)


def half_tables(half, rows, extent):
    frequency = np.arange(half + 1, dtype=np.int64)
    pixels = np.arange(extent, dtype=np.int64)
    phases = np.mod(frequency[:, None] * pixels[None, :], extent).astype(np.float32)
    angles = phases * np.float32(2.0 * math.pi / extent)
    factor = np.float32(1.0 / math.sqrt(extent))
    table = np.zeros((2 * rows, extent), np.float32)
    table[: half + 1] = np.cos(angles) * factor
    table[rows : rows + half + 1] = np.sin(angles) * factor
    return table


def pick_tables(half, rows, lanes):
    size = 2 * half
    row_pick = np.zeros((2 * rows, size), np.float32)
    col_pick = np.zeros((size, 2 * lanes), np.float32)
    for index in range(half):
        row_pick[index, half + index] = 1.0
        col_pick[half + index, index] = 1.0
        row_pick[rows + half - index, index] = 1.0
        col_pick[index, lanes + half - index] = 1.0
    return row_pick, col_pick


def vmem(count):
    return [pl.BlockSpec(memory_space=pltpu.VMEM)] * count


def call(kernel, outs, specs, scratch=(), cost=None, **kwargs):
    return pl.pallas_call(
        kernel,
        out_shape=outs,
        in_specs=specs,
        out_specs=jax.tree.map(lambda _: pl.BlockSpec(memory_space=pltpu.VMEM), outs),
        scratch_shapes=list(scratch),
        cost_estimate=cost,
        compiler_params=pltpu.CompilerParams(vmem_limit_bytes=VMEM_LIMIT),
        **kwargs,
    )


def pupil_kernel(rows, lanes, pupils_ref, weights_ref, row_ref, col_ref, out_ref):
    kernels = pupils_ref.shape[1]

    def one(k, carry):
        scale = jnp.sqrt(jnp.full((1, 1), weights_ref[k], jnp.float32))

        def picked(part):
            values = pupils_ref[part, k] * scale
            high = values.astype(jnp.bfloat16)
            low = (values - high.astype(jnp.float32)).astype(jnp.bfloat16)
            total = None
            for piece in (high, low):
                columns = dot(piece, col_ref[...]).astype(jnp.bfloat16)
                term = dot(row_ref[...], columns)
                total = term if total is None else total + term
            return total

        for part in range(2):
            full = picked(part)
            pos_pos, pos_neg = full[:rows, :lanes], full[:rows, lanes:]
            neg_pos, neg_neg = full[rows:, :lanes], full[rows:, lanes:]
            out_ref[k, 0 + part] = (pos_pos + neg_neg).astype(jnp.bfloat16)
            out_ref[k, 2 + part] = (pos_pos - neg_neg).astype(jnp.bfloat16)
            out_ref[k, 4 + part] = (pos_neg + neg_pos).astype(jnp.bfloat16)
            out_ref[k, 6 + part] = (pos_neg - neg_pos).astype(jnp.bfloat16)
        return carry

    lax.fori_loop(0, kernels, one, 0)


def middle_kernel(mask_ref, table_ref, out_ref):
    tile = mask_ref.shape[0]
    out_ref[...] = dot(
        table_ref[:, AMBIT : AMBIT + tile], mask_ref[...].astype(jnp.bfloat16)
    )


def partial_kernel(mid_ref, top_ref, bottom_ref, table_ref, own_ref, low_ref, high_ref):
    extent = table_ref.shape[1]
    width = mid_ref.shape[1]
    total = mid_ref[...] + dot(table_ref[:, :AMBIT], top_ref[...])
    total = total + dot(table_ref[:, extent - AMBIT :], bottom_ref[...])
    total = total.astype(jnp.bfloat16)
    own_ref[...] = total
    low_ref[...] = total[:, :AMBIT]
    high_ref[...] = total[:, width - AMBIT :]


def core_kernel(
    rows,
    lanes,
    slots,
    live_ref,
    own_ref,
    left_ref,
    right_ref,
    goal_ref,
    pupil_ref,
    row_ref,
    row_t_ref,
    col_ref,
    col_t_ref,
    *rest,
):
    outs = rest[:slots]
    ext_ref, amp_ref, sec_ref, field_ref, total_ref, slope_ref, back_ref, wave_ref, sum_ref = rest[
        slots:
    ]
    width = own_ref.shape[1]
    tile = goal_ref.shape[0]
    extent = row_ref.shape[1]
    kernels = pupil_ref.shape[0]
    inner = slice(AMBIT, AMBIT + tile)
    ext_ref[:, :AMBIT] = left_ref[...]
    ext_ref[:, AMBIT : AMBIT + width] = own_ref[...]
    ext_ref[:, AMBIT + width :] = right_ref[...]

    def pupil(k, index):
        return pupil_ref[k, index].astype(jnp.float32)

    for slot in range(slots):
        out_ref = outs[slot]
        live = live_ref[0, slot] > 0

        @pl.when(jnp.logical_not(live))
        def _():
            out_ref[...] = jnp.zeros_like(out_ref)

        @pl.when(live)
        def _():
            spec = dot(ext_ref[:, slot * tile : slot * tile + extent], col_t_ref[...])
            cc, cs = spec[:rows, :lanes], spec[:rows, lanes:]
            sc, ss = spec[rows:, :lanes], spec[rows:, lanes:]
            sum_ref[0] = cc - ss
            sum_ref[1] = sc + cs
            sum_ref[2] = cc + ss
            sum_ref[3] = sc - cs

            def amplitude(k, carry):
                u, v, m, n = sum_ref[0], sum_ref[1], sum_ref[2], sum_ref[3]
                pr, pi, mr, mi = (pupil(k, index) for index in range(4))
                big_re = pr * u + mi * v
                big_im = pi * u - mr * v
                small_re = mr * u + pi * v
                small_im = mi * u - pr * v
                pr, pi, mr, mi = (pupil(k, index) for index in range(4, 8))
                big_re2 = pr * m + mi * n
                big_im2 = pi * m - mr * n
                small_re2 = mr * m + pi * n
                small_im2 = mi * m - pr * n
                base = pl.multiple_of(k * 4 * rows, 16)

                def put(place, left, right):
                    where = pl.ds(base + place * rows, rows)
                    amp_ref[where, :lanes] = left.astype(jnp.bfloat16)
                    amp_ref[where, lanes:] = right.astype(jnp.bfloat16)

                put(0, big_re + big_re2, small_im2 - small_im)
                put(1, -(small_im + small_im2), big_re2 - big_re)
                put(2, big_im + big_im2, small_re - small_re2)
                put(3, small_re + small_re2, big_im2 - big_im)
                return carry

            lax.fori_loop(0, kernels, amplitude, 0)

            def section(k, carry):
                where = pl.ds(pl.multiple_of(k * 4 * rows, 16), 4 * rows)
                sec_ref[where] = dot(amp_ref[where], col_ref[:, inner]).astype(jnp.bfloat16)
                return carry

            lax.fori_loop(0, kernels, section, 0)
            total_ref[...] = jnp.zeros_like(total_ref)

            def field(k, carry):
                where_re = pl.ds(pl.multiple_of(k * 4 * rows, 16), 2 * rows)
                where_im = pl.ds(pl.multiple_of(k * 4 * rows + 2 * rows, 16), 2 * rows)
                real = dot(row_t_ref[inner], sec_ref[where_re])
                imag = dot(row_t_ref[inner], sec_ref[where_im])
                total_ref[...] += real * real + imag * imag
                field_ref[k, 0] = real.astype(jnp.bfloat16)
                field_ref[k, 1] = imag.astype(jnp.bfloat16)
                return carry

            lax.fori_loop(0, kernels, field, 0)
            resist = 1.0 / (1.0 + jnp.exp(-steepness * (total_ref[...] - threshold_level)))
            goal = goal_ref[:, slot * tile : (slot + 1) * tile].astype(jnp.float32)
            slope = (resist - goal) * (2.0 * steepness) * resist * (1.0 - resist)
            slope_ref[...] = slope.astype(jnp.bfloat16)

            def back(k, carry):
                for part in range(2):
                    cotangent = slope_ref[...] * field_ref[k, part]
                    where = pl.ds(pl.multiple_of((k * 2 + part) * 2 * rows, 16), 2 * rows)
                    back_ref[where] = dot(row_ref[:, inner], cotangent).astype(jnp.bfloat16)
                return carry

            lax.fori_loop(0, kernels, back, 0)

            def wave(k, carry):
                where = pl.ds(pl.multiple_of(k * 4 * rows, 16), 4 * rows)
                wave_ref[where] = dot(back_ref[where], col_t_ref[inner])
                return carry

            lax.fori_loop(0, kernels, wave, 0)
            sum_ref[...] = jnp.zeros_like(sum_ref)

            def adjoint(k, carry):
                base = pl.multiple_of(k * 4 * rows, 8)

                def quarters(place):
                    cos_rows = pl.ds(base + place * 2 * rows, rows)
                    sin_rows = pl.ds(base + place * 2 * rows + rows, rows)
                    return (
                        wave_ref[cos_rows, :lanes],
                        wave_ref[cos_rows, lanes:],
                        wave_ref[sin_rows, :lanes],
                        wave_ref[sin_rows, lanes:],
                    )

                rcc, rcs, rsc, rss = quarters(0)
                icc, ics, isc, iss = quarters(1)
                ur, ui, vr, vi = rcc - rss, icc - iss, rsc + rcs, isc + ics
                pr, pi, mr, mi = (pupil(k, index) for index in range(4))
                sum_ref[0] += pr * ur + pi * ui + mr * vi - mi * vr
                sum_ref[1] += mr * ui - mi * ur - pr * vr - pi * vi
                ur, ui, vr, vi = rcc + rss, icc + iss, rsc - rcs, isc - ics
                pr, pi, mr, mi = (pupil(k, index) for index in range(4, 8))
                sum_ref[2] += pr * ur + pi * ui + mr * vi - mi * vr
                sum_ref[3] += mr * ui - mi * ur - pr * vr - pi * vi
                return carry

            lax.fori_loop(0, kernels, adjoint, 0)
            out_ref[:rows, :lanes] = (sum_ref[0] + sum_ref[2]).astype(jnp.bfloat16)
            out_ref[:rows, lanes:] = (sum_ref[3] - sum_ref[1]).astype(jnp.bfloat16)
            out_ref[rows:, :lanes] = (-(sum_ref[1] + sum_ref[3])).astype(jnp.bfloat16)
            out_ref[rows:, lanes:] = (sum_ref[2] - sum_ref[0]).astype(jnp.bfloat16)


def returned_kernel(tile, slots, *refs):
    spectral = refs[: slots + 2]
    row_t_ref, col_ref, out_ref, up_ref, down_ref = refs[slots + 2 : slots + 7]
    sum_ref = refs[slots + 7]
    width = out_ref.shape[1]
    extent = row_t_ref.shape[0]
    sum_ref[...] = jnp.zeros_like(sum_ref)
    for place, ref in zip(range(-1, slots + 1), spectral):
        start = place * tile - AMBIT
        low, high = max(0, start), min(width, start + extent)
        sum_ref[:, low:high] += dot(ref[...], col_ref[:, low - start : high - start])
    mixed = sum_ref[...].astype(jnp.bfloat16)
    out_ref[...] = mixed
    up_ref[...] = dot(row_t_ref[:AMBIT], mixed).astype(jnp.bfloat16)
    down_ref[...] = dot(row_t_ref[extent - AMBIT :], mixed).astype(jnp.bfloat16)


def update_kernel(mask_ref, mixed_ref, row_t_ref, out_ref):
    tile = mask_ref.shape[0]
    out_ref[...] = mask_ref[...] - step_rate * dot(
        row_t_ref[AMBIT : AMBIT + tile], mixed_ref[...]
    )


def body(mask, target, live, pupils, weights):
    tile, width = mask.shape
    slots = live.shape[1]
    kernels, size = pupils.shape[1], pupils.shape[2]
    half = size // 2
    rows, lanes = round_up(half + 1, 16), round_up(half + 1, 128)
    extent = tile + 2 * AMBIT
    row_np = half_tables(half, rows, extent)
    col_np = half_tables(half, lanes, extent)
    row_pick, col_pick = (
        jnp.asarray(pick, jnp.bfloat16) for pick in pick_tables(half, rows, lanes)
    )
    row_table, row_table_t = jnp.asarray(row_np, jnp.bfloat16), jnp.asarray(row_np.T, jnp.bfloat16)
    col_table, col_table_t = jnp.asarray(col_np, jnp.bfloat16), jnp.asarray(col_np.T, jnp.bfloat16)
    bf16, f32 = jnp.bfloat16, jnp.float32
    shape = jax.ShapeDtypeStruct
    smem = pl.BlockSpec(memory_space=pltpu.SMEM)

    def cost(us):
        return pl.CostEstimate(
            flops=int(us * 5e8), bytes_accessed=int(us * 1e6), transcendentals=0
        )

    top = shifted(mask[tile - AMBIT :].astype(bf16), "row", 1)
    bottom = shifted(mask[:AMBIT].astype(bf16), "row", -1)
    middle = call(middle_kernel, shape((2 * rows, width), f32), vmem(2), cost=cost(2))(
        mask, row_table
    )
    quads = call(
        partial(pupil_kernel, rows, lanes),
        shape((kernels, 8, rows, lanes), bf16),
        [*vmem(1), smem, *vmem(2)],
        cost=cost(5),
    )(pupils, weights, row_pick, col_pick)
    own, low, high = call(
        partial_kernel,
        (
            shape((2 * rows, width), bf16),
            shape((2 * rows, AMBIT), bf16),
            shape((2 * rows, AMBIT), bf16),
        ),
        vmem(4),
        cost=cost(1),
    )(middle, top, bottom, row_table)
    left = shifted(high, "col", 1)
    right = shifted(low, "col", -1)
    spectral = call(
        partial(core_kernel, rows, lanes, slots),
        tuple(shape((2 * rows, 2 * lanes), bf16) for _ in range(slots)),
        [smem, *vmem(9)],
        scratch=[
            pltpu.VMEM((2 * rows, width + 2 * AMBIT), bf16),
            pltpu.VMEM((kernels * 4 * rows, 2 * lanes), bf16),
            pltpu.VMEM((kernels * 4 * rows, tile), bf16),
            pltpu.VMEM((kernels, 2, tile, tile), bf16),
            pltpu.VMEM((tile, tile), f32),
            pltpu.VMEM((tile, tile), bf16),
            pltpu.VMEM((kernels * 4 * rows, tile), bf16),
            pltpu.VMEM((kernels * 4 * rows, 2 * lanes), f32),
            pltpu.VMEM((4, rows, lanes), f32),
        ],
        cost=cost(20),
    )(live, own, left, right, target, quads, row_table, row_table_t, col_table, col_table_t)
    before = shifted(spectral[-1], "col", 1)
    after = shifted(spectral[0], "col", -1)
    mixed, up, down = call(
        partial(returned_kernel, tile, slots),
        (shape((2 * rows, width), bf16), shape((AMBIT, width), bf16), shape((AMBIT, width), bf16)),
        vmem(slots + 4),
        scratch=[pltpu.VMEM((2 * rows, width), f32)],
        cost=cost(1),
    )(before, *spectral, after, row_table_t, col_table)
    from_above = shifted(down, "row", 1)
    from_below = shifted(up, "row", -1)
    base = call(update_kernel, shape((tile, width), f32), vmem(3), cost=cost(2))(
        mask, mixed, row_table_t
    )
    return call_rims(base, from_above, from_below)


def rims_kernel(above_ref, below_ref, base_ref, out_ref):
    @pl.when(pl.program_id(0) == 0)
    def _():
        out_ref[...] = base_ref[...] - step_rate * above_ref[...].astype(jnp.float32)

    @pl.when(pl.program_id(0) > 0)
    def _():
        out_ref[...] = base_ref[...] - step_rate * below_ref[...].astype(jnp.float32)


def call_rims(base, from_above, from_below):
    tile, width = base.shape
    last = tile // AMBIT - 1
    edge = pl.BlockSpec((AMBIT, width), lambda i: (0, 0))
    moving = pl.BlockSpec((AMBIT, width), lambda i: (i * last, 0))
    return pl.pallas_call(
        rims_kernel,
        out_shape=jax.ShapeDtypeStruct((tile, width), jnp.float32),
        grid=(2,),
        in_specs=[edge, edge, moving],
        out_specs=moving,
        input_output_aliases={2: 0},
    )(from_above, from_below, base)


def solution(mesh):
    placed = (P("row", "col"), P("row", "col"), P("row", "col"), P(), P())
    return jax.shard_map(
        body, mesh=mesh, in_specs=placed, out_specs=P("row", "col"), check_vma=False
    )
```

```python
from functools import partial
import math

import jax
import jax.numpy as jnp
import numpy as np
from jax import lax
from jax.experimental import pallas as pl
from jax.experimental.pallas import tpu as pltpu
from jax.sharding import PartitionSpec as P

AMBIT = 128
LANE = 128

steepness = 4.0
threshold_level = 1.0
step_rate = 8.0

MIB = 1024 * 1024


def round_up(value, unit):
    return -(-value // unit) * unit


def moved(block, axis, target_of):
    count = lax.axis_size(axis)
    pairs = [(i, target_of(i)) for i in range(count)]
    return lax.ppermute(block, axis, [(i, j) for i, j in pairs if j is not None and 0 <= j < count])


def dot(leading, trailing):
    return jnp.dot(leading, trailing, preferred_element_type=jnp.float32)


def half_tables(half, rows, extent):
    frequency = np.arange(half + 1, dtype=np.int64)
    pixels = np.arange(extent, dtype=np.int64)
    phases = np.mod(frequency[:, None] * pixels[None, :], extent).astype(np.float32)
    angles = phases * np.float32(2.0 * math.pi / extent)
    factor = np.float32(1.0 / math.sqrt(extent))
    table = np.zeros((2 * rows, extent), np.float32)
    table[: half + 1] = np.cos(angles) * factor
    table[rows : rows + half + 1] = np.sin(angles) * factor
    return table


def pick_tables(half, rows, lanes):
    size = 2 * half
    row_pick = np.zeros((2 * rows, size), np.float32)
    col_pick = np.zeros((size, 2 * lanes), np.float32)
    for index in range(half):
        row_pick[index, half + index] = 1.0
        col_pick[half + index, index] = 1.0
        row_pick[rows + half - index, index] = 1.0
        col_pick[index, lanes + half - index] = 1.0
    return row_pick, col_pick


def vmem(count):
    return [pl.BlockSpec(memory_space=pltpu.VMEM)] * count


def call(kernel, outs, specs, scratch=(), limit=16, us=1, **kwargs):
    return pl.pallas_call(
        kernel,
        out_shape=outs,
        in_specs=specs,
        out_specs=jax.tree.map(lambda _: pl.BlockSpec(memory_space=pltpu.VMEM), outs),
        scratch_shapes=list(scratch),
        cost_estimate=pl.CostEstimate(
            flops=int(us * 5e8), bytes_accessed=int(us * 1e6), transcendentals=0
        ),
        compiler_params=pltpu.CompilerParams(vmem_limit_bytes=limit * MIB),
        **kwargs,
    )


def pupil_steps(rows, lanes, first, last, pupils_ref, weights_ref, row_ref, col_ref, out_ref):
    for k in range(first, last):
        scale = jnp.sqrt(jnp.full((1, 1), weights_ref[k] * (0.5 * steepness), jnp.float32))
        for part in range(2):
            values = (pupils_ref[part, k] * scale).astype(jnp.bfloat16)
            columns = dot(values, col_ref[...]).astype(jnp.bfloat16)
            full = dot(row_ref[...], columns)
            pos_pos, pos_neg = full[:rows, :lanes], full[:rows, lanes:]
            neg_pos, neg_neg = full[rows:, :lanes], full[rows:, lanes:]
            out_ref[k, 0 + part] = (pos_pos + neg_neg).astype(jnp.bfloat16)
            out_ref[k, 2 + part] = (pos_pos - neg_neg).astype(jnp.bfloat16)
            out_ref[k, 4 + part] = (pos_neg + neg_pos).astype(jnp.bfloat16)
            out_ref[k, 6 + part] = (pos_neg - neg_pos).astype(jnp.bfloat16)


def edges_kernel(low_ref, high_ref, first_ref, last_ref):
    first_ref[...] = low_ref[...].astype(jnp.bfloat16)
    last_ref[...] = high_ref[...].astype(jnp.bfloat16)


def early_kernel(
    rows, lanes, count, mask_ref, table_ref, pupils_ref, weights_ref, row_ref, col_ref, mid_ref, out_ref
):
    tile = mask_ref.shape[0]
    mid_ref[...] = dot(
        table_ref[:, AMBIT : AMBIT + tile], mask_ref[...].astype(jnp.bfloat16)
    )
    pupil_steps(rows, lanes, 0, count, pupils_ref, weights_ref, row_ref, col_ref, out_ref)


def partial_kernel(
    rows, lanes, live_ref, mid_ref, top_ref, bottom_ref, table_ref, col_t_ref, own_ref, low_ref, high_ref, main_ref
):
    extent = table_ref.shape[1]
    width = mid_ref.shape[1]
    tile = extent - 2 * AMBIT
    total = mid_ref[...] + dot(table_ref[:, :AMBIT], top_ref[...])
    total = total + dot(table_ref[:, extent - AMBIT :], bottom_ref[...])
    total = total.astype(jnp.bfloat16)
    own_ref[...] = total[:, : tile + AMBIT]
    low_ref[...] = total[:, :AMBIT]
    high_ref[...] = total[:, width - AMBIT :]
    main = dot(total[:, tile - AMBIT :], col_t_ref[: tile + AMBIT])
    shape = main.shape
    flag = (lax.broadcasted_iota(jnp.int32, shape, 0) == shape[0] - 1) & (
        lax.broadcasted_iota(jnp.int32, shape, 1) == shape[1] - 1
    )
    live = live_ref[0, live_ref.shape[1] - 1].astype(jnp.float32)
    main_ref[...] = jnp.where(flag, live, main).astype(jnp.bfloat16)


def late_kernel(
    rows, lanes, first, last, own_ref, col_t_ref, quads_ref, pupils_ref, weights_ref, row_ref, col_ref, base_ref, out_ref
):
    out_ref[:first] = quads_ref[...]
    base_ref[...] = dot(own_ref[...], col_t_ref[AMBIT:])
    pupil_steps(rows, lanes, first, last, pupils_ref, weights_ref, row_ref, col_ref, out_ref)


def core_kernel(
    rows,
    lanes,
    live_ref,
    base_ref,
    left_ref,
    main_ref,
    low_ref,
    right_ref,
    goal_ref,
    other_ref,
    pupil_ref,
    row_ref,
    row_t_ref,
    col_ref,
    col_t_ref,
    out_ref,
    other_out_ref,
    spec_ref,
    amp_ref,
    sec_ref,
    field_ref,
    total_ref,
    slope_ref,
    back_ref,
    sum_ref,
    ans_ref,
):
    tile = goal_ref.shape[0]
    extent = row_ref.shape[1]
    kernels = pupil_ref.shape[0]
    halves = [slice(start, start + 2 * LANE) for start in range(0, tile, 2 * LANE)]
    inner = slice(AMBIT, AMBIT + tile)
    odd = lax.rem(lax.axis_index("col"), 2) == 1
    spec_ref[0] = base_ref[...] + dot(left_ref[...], col_t_ref[:AMBIT])
    rim = jnp.where(odd, low_ref[...], right_ref[...])
    spec_ref[1] = main_ref[...].astype(jnp.float32) + dot(rim, col_t_ref[extent - AMBIT :])
    other_live = jnp.max(main_ref[2 * rows - 16 :, 2 * lanes - LANE :].astype(jnp.float32)[15:, LANE - 1 :])
    out_ref[...] = jnp.zeros_like(out_ref)
    other_out_ref[...] = jnp.zeros_like(other_out_ref)

    def work(item, carry):
        live = jnp.where(item == 0, live_ref[0, 0].astype(jnp.float32), other_live) > 0.0

        @pl.when(live)
        def _():
            spec = spec_ref[item]
            cc, cs = spec[:rows, :lanes], spec[:rows, lanes:]
            sc, ss = spec[rows:, :lanes], spec[rows:, lanes:]
            sum_ref[0] = cc - ss
            sum_ref[1] = sc + cs
            sum_ref[2] = cc + ss
            sum_ref[3] = sc - cs

            def pupil(k, index):
                return pupil_ref[k, index].astype(jnp.float32)

            def section(k, buf):
                u, v, m, n = sum_ref[0], sum_ref[1], sum_ref[2], sum_ref[3]
                pr, pi, mr, mi = (pupil(k, index) for index in range(4))
                big_re = pr * u + mi * v
                big_im = pi * u - mr * v
                small_re = mr * u + pi * v
                small_im = mi * u - pr * v
                pr, pi, mr, mi = (pupil(k, index) for index in range(4, 8))
                big_re2 = pr * m + mi * n
                big_im2 = pi * m - mr * n
                small_re2 = mr * m + pi * n
                small_im2 = mi * m - pr * n

                def pair(place, left, right):
                    where = slice(place * rows, (place + 1) * rows)
                    amp_ref[buf, where, :lanes] = left.astype(jnp.bfloat16)
                    amp_ref[buf, where, lanes:] = right.astype(jnp.bfloat16)

                pair(0, big_re + big_re2, small_im2 - small_im)
                pair(1, -(small_im + small_im2), big_re2 - big_re)
                pair(2, big_im + big_im2, small_re - small_re2)
                pair(3, small_re + small_re2, big_im2 - big_im)
                sec_ref[buf] = dot(amp_ref[buf], col_ref[:, inner]).astype(jnp.bfloat16)

            def field(ks, bufs):
                for where in halves:
                    energy = None
                    for k, buf in zip(ks, bufs):
                        real = dot(row_t_ref[inner], sec_ref[buf, : 2 * rows, where])
                        imag = dot(row_t_ref[inner], sec_ref[buf, 2 * rows :, where])
                        field_ref[k, 0, :, where] = real.astype(jnp.bfloat16)
                        field_ref[k, 1, :, where] = imag.astype(jnp.bfloat16)
                        term = real * real + imag * imag
                        energy = term if energy is None else energy + term
                    total_ref[:, where] += energy

            section(0, 0)
            total_ref[...] = jnp.zeros_like(total_ref)

            def forward(i, carry):
                k = 2 * i
                field((k,), (0,))
                section(k + 1, 1)
                field((k + 1,), (1,))
                section(jnp.minimum(k + 2, kernels - 1), 0)
                return carry

            lax.fori_loop(0, kernels // 2, forward, 0)

            def slopes(ref):
                for where in halves:
                    level = jnp.tanh(total_ref[:, where] - 0.5 * steepness * threshold_level)
                    excess = 0.5 * level + 0.5 - ref[:, where].astype(jnp.float32)
                    slope_ref[:, where] = (excess * (1.0 - level * level)).astype(jnp.bfloat16)

            @pl.when(item == 0)
            def _():
                slopes(goal_ref)

            @pl.when(item > 0)
            def _():
                slopes(other_ref)

            def back(k, buf):
                for where in halves:
                    for part in range(2):
                        cotangent = slope_ref[:, where] * field_ref[k, part, :, where]
                        place = slice(part * 2 * rows, (part + 1) * 2 * rows)
                        back_ref[buf, place, where] = dot(row_ref[:, inner], cotangent).astype(
                            jnp.bfloat16
                        )

            def adjoint(k, buf):
                wave = dot(back_ref[buf], col_t_ref[inner])
                rcc, rcs = wave[:rows, :lanes], wave[:rows, lanes:]
                rsc, rss = wave[rows : 2 * rows, :lanes], wave[rows : 2 * rows, lanes:]
                icc, ics = wave[2 * rows : 3 * rows, :lanes], wave[2 * rows : 3 * rows, lanes:]
                isc, iss = wave[3 * rows :, :lanes], wave[3 * rows :, lanes:]
                ur, ui, vr, vi = rcc - rss, icc - iss, rsc + rcs, isc + ics
                pr, pi, mr, mi = (pupil(k, index) for index in range(4))
                ans_ref[0] += pr * ur + pi * ui + mr * vi - mi * vr
                ans_ref[1] += mr * ui - mi * ur - pr * vr - pi * vi
                ur, ui, vr, vi = rcc + rss, icc + iss, rsc - rcs, isc - ics
                pr, pi, mr, mi = (pupil(k, index) for index in range(4, 8))
                ans_ref[2] += pr * ur + pi * ui + mr * vi - mi * vr
                ans_ref[3] += mr * ui - mi * ur - pr * vr - pi * vi

            ans_ref[...] = jnp.zeros_like(ans_ref)
            back(0, 0)

            def backward(i, carry):
                k = 2 * i
                adjoint(k, 0)
                back(k + 1, 1)
                adjoint(k + 1, 1)
                back(jnp.minimum(k + 2, kernels - 1), 0)
                return carry

            lax.fori_loop(0, kernels // 2, backward, 0)

            def answer(ref):
                ref[:rows, :lanes] = (ans_ref[0] + ans_ref[2]).astype(jnp.bfloat16)
                ref[:rows, lanes:] = (ans_ref[3] - ans_ref[1]).astype(jnp.bfloat16)
                ref[rows:, :lanes] = (-(ans_ref[1] + ans_ref[3])).astype(jnp.bfloat16)
                ref[rows:, lanes:] = (ans_ref[2] - ans_ref[0]).astype(jnp.bfloat16)

            @pl.when(item == 0)
            def _():
                answer(out_ref)

            @pl.when(item > 0)
            def _():
                answer(other_out_ref)

        return carry

    lax.fori_loop(0, 2, work, 0)


def returned_kernel(
    tile, mine_ref, second_ref, after_ref, before_ref, other_ref, row_t_ref, col_ref, out_ref, up_ref, down_ref, sum_ref
):
    width = out_ref.shape[1]
    extent = row_t_ref.shape[0]
    odd = lax.rem(lax.axis_index("col"), 2) == 1
    before = jnp.where(odd, other_ref[...], before_ref[...])
    sum_ref[...] = jnp.zeros_like(sum_ref)
    for place, value in zip(range(-1, 3), (before, mine_ref[...], second_ref[...], after_ref[...])):
        start = place * tile - AMBIT
        low, high = max(0, start), min(width, start + extent)
        sum_ref[:, low:high] += dot(value, col_ref[:, low - start : high - start])
    mixed = sum_ref[...].astype(jnp.bfloat16)
    out_ref[...] = mixed
    up_ref[...] = dot(row_t_ref[:AMBIT], mixed).astype(jnp.bfloat16)
    down_ref[...] = dot(row_t_ref[extent - AMBIT :], mixed).astype(jnp.bfloat16)


def update_kernel(mask_ref, mixed_ref, row_t_ref, out_ref, rims_ref, stage_ref, sem):
    tile = mask_ref.shape[0]
    stage_ref[...] = mask_ref[...] - step_rate * dot(
        row_t_ref[AMBIT : AMBIT + tile], mixed_ref[...]
    )
    inner = pl.ds(AMBIT, tile - 2 * AMBIT)
    copy = pltpu.make_async_copy(stage_ref.at[inner], out_ref.at[inner], sem)
    copy.start()
    rims_ref[:AMBIT] = stage_ref[:AMBIT]
    rims_ref[AMBIT:] = stage_ref[tile - AMBIT :]
    copy.wait()


def rims_kernel(above_ref, below_ref, rims_ref, base_ref, out_ref, stage_ref, sems):
    tile = out_ref.shape[0]
    copies = []
    for index, (rim_ref, start) in enumerate(((above_ref, 0), (below_ref, tile - AMBIT))):
        where = pl.ds(index * AMBIT, AMBIT)
        stage_ref[where] = rims_ref[where] - step_rate * rim_ref[...].astype(jnp.float32)
        copy = pltpu.make_async_copy(
            stage_ref.at[where], out_ref.at[pl.ds(start, AMBIT)], sems.at[index]
        )
        copy.start()
        copies.append(copy)
    for copy in copies:
        copy.wait()


def body(mask, target, live, pupils, weights):
    tile, width = mask.shape
    kernels, size = pupils.shape[1], pupils.shape[2]
    half = size // 2
    rows, lanes = round_up(half + 1, 16), round_up(half + 2, LANE)
    extent = tile + 2 * AMBIT
    row_np = half_tables(half, rows, extent)
    col_np = half_tables(half, lanes, extent)
    row_pick, col_pick = (
        jnp.asarray(pick, jnp.bfloat16) for pick in pick_tables(half, rows, lanes)
    )
    row_table, row_table_t = jnp.asarray(row_np, jnp.bfloat16), jnp.asarray(row_np.T, jnp.bfloat16)
    col_table, col_table_t = jnp.asarray(col_np, jnp.bfloat16), jnp.asarray(col_np.T, jnp.bfloat16)
    bf16, f32 = jnp.bfloat16, jnp.float32
    shape = jax.ShapeDtypeStruct
    smem = pl.BlockSpec(memory_space=pltpu.SMEM)
    early = kernels // 2

    def paired(index):
        return index + 1 - 2 * (index % 2)

    edge = shape((AMBIT, width), bf16)
    first, last = pl.pallas_call(
        edges_kernel,
        out_shape=(edge, edge),
        grid=(1,),
        in_specs=[
            pl.BlockSpec((AMBIT, width), lambda i: (0, 0)),
            pl.BlockSpec((AMBIT, width), lambda i: (tile // AMBIT - 1, 0)),
        ],
        out_specs=(pl.BlockSpec(memory_space=pltpu.VMEM), pl.BlockSpec(memory_space=pltpu.VMEM)),
        compiler_params=pltpu.CompilerParams(vmem_limit_bytes=8 * MIB),
    )(mask, mask)
    top = moved(last, "row", lambda i: i + 1)
    bottom = moved(first, "row", lambda i: i - 1)
    other_goal = moved(target[:, tile:], "col", paired)
    middle, quads = call(
        partial(early_kernel, rows, lanes, early),
        (shape((2 * rows, width), f32), shape((early, 8, rows, lanes), bf16)),
        [*vmem(3), smem, *vmem(2)],
        us=4,
    )(mask, row_table, pupils, weights, row_pick, col_pick)
    own, low, high, main = call(
        partial(partial_kernel, rows, lanes),
        (
            shape((2 * rows, tile + AMBIT), bf16),
            shape((2 * rows, AMBIT), bf16),
            shape((2 * rows, AMBIT), bf16),
            shape((2 * rows, 2 * lanes), bf16),
        ),
        [smem, *vmem(5)],
    )(live, middle, top, bottom, row_table, col_table_t)
    left = moved(high, "col", lambda i: i + 1)
    other_main = moved(main, "col", paired)
    right = moved(low, "col", lambda i: i - 2 if i % 2 == 0 else None)
    base, all_quads = call(
        partial(late_kernel, rows, lanes, early, kernels),
        (shape((2 * rows, 2 * lanes), f32), shape((kernels, 8, rows, lanes), bf16)),
        [*vmem(4), smem, *vmem(2)],
        us=4,
    )(own, col_table_t, quads, pupils, weights, row_pick, col_pick)
    answer = shape((2 * rows, 2 * lanes), bf16)
    mine, other = call(
        partial(core_kernel, rows, lanes),
        (answer, answer),
        [smem, *vmem(12)],
        scratch=[
            pltpu.VMEM((2, 2 * rows, 2 * lanes), f32),
            pltpu.VMEM((2, 4 * rows, 2 * lanes), bf16),
            pltpu.VMEM((2, 4 * rows, tile), bf16),
            pltpu.VMEM((kernels, 2, tile, tile), bf16),
            pltpu.VMEM((tile, tile), f32),
            pltpu.VMEM((tile, tile), bf16),
            pltpu.VMEM((2, 4 * rows, tile), bf16),
            pltpu.VMEM((4, rows, lanes), f32),
            pltpu.VMEM((4, rows, lanes), f32),
        ],
        limit=36,
        us=15,
    )(
        live, base, left, other_main, low, right, target, other_goal, all_quads,
        row_table, row_table_t, col_table, col_table_t,
    )
    second = moved(other, "col", paired)
    after = moved(mine, "col", lambda i: i - 1)
    before = moved(other, "col", lambda i: i + 2 if i % 2 == 0 else None)
    mixed, up, down = call(
        partial(returned_kernel, tile),
        (shape((2 * rows, width), bf16), shape((AMBIT, width), bf16), shape((AMBIT, width), bf16)),
        vmem(7),
        scratch=[pltpu.VMEM((2 * rows, width), f32)],
    )(mine, second, after, before, other, row_table_t, col_table)
    from_above = moved(down, "row", lambda i: i + 1)
    from_below = moved(up, "row", lambda i: i - 1)
    anywhere = pl.BlockSpec(memory_space=pl.ANY)
    whole, rims = shape((tile, width), f32), shape((2 * AMBIT, width), f32)
    updated, edges = pl.pallas_call(
        update_kernel,
        out_shape=(whole, rims),
        in_specs=vmem(3),
        out_specs=(anywhere, *vmem(1)),
        scratch_shapes=[pltpu.VMEM((tile, width), f32), pltpu.SemaphoreType.DMA],
        cost_estimate=pl.CostEstimate(flops=10**9, bytes_accessed=2 * 10**6, transcendentals=0),
        compiler_params=pltpu.CompilerParams(vmem_limit_bytes=16 * MIB),
    )(mask, mixed, row_table_t)
    return pl.pallas_call(
        rims_kernel,
        out_shape=whole,
        in_specs=[*vmem(3), anywhere],
        out_specs=anywhere,
        scratch_shapes=[pltpu.VMEM((2 * AMBIT, width), f32), pltpu.SemaphoreType.DMA((2,))],
        input_output_aliases={3: 0},
        compiler_params=pltpu.CompilerParams(vmem_limit_bytes=8 * MIB),
    )(from_above, from_below, edges, updated)


def solution(mesh):
    placed = (P("row", "col"), P("row", "col"), P("row", "col"), P(), P())
    return jax.shard_map(
        body, mesh=mesh, in_specs=placed, out_specs=P("row", "col"), check_vma=False
    )
```

```python
from functools import partial
import math

import jax
import jax.numpy as jnp
import numpy as np
from jax import lax
from jax.experimental import pallas as pl
from jax.experimental.pallas import tpu as pltpu
from jax.sharding import PartitionSpec as P


AMBIT = 128
LANE = 128

steepness = 4.0
threshold_level = 1.0
step_rate = 8.0

MIB = 1024 * 1024


def round_up(value, unit):
    return -(-value // unit) * unit


def stepped(block, axis, step):
    count = lax.axis_size(axis)
    pairs = [(i, i + step) for i in range(count) if 0 <= i + step < count]
    return lax.ppermute(block, axis, pairs)


def turned(block, axis, step):
    count = lax.axis_size(axis)
    return lax.ppermute(block, axis, [(i, (i + step) % count) for i in range(count)])


def dot(leading, trailing):
    return jnp.dot(leading, trailing, preferred_element_type=jnp.float32)


def half_tables(half, rows, extent):
    frequency = np.arange(half + 1, dtype=np.int64)
    pixels = np.arange(extent, dtype=np.int64)
    phases = np.mod(frequency[:, None] * pixels[None, :], extent).astype(np.float32)
    angles = phases * np.float32(2.0 * math.pi / extent)
    factor = np.float32(1.0 / math.sqrt(extent))
    table = np.zeros((2 * rows, extent), np.float32)
    table[: half + 1] = np.cos(angles) * factor
    table[rows : rows + half + 1] = np.sin(angles) * factor
    return table


def pick_tables(half, rows, lanes):
    size = 2 * half
    row_pick = np.zeros((2 * rows, size), np.float32)
    col_pick = np.zeros((size, 2 * lanes), np.float32)
    for index in range(half):
        row_pick[index, half + index] = 1.0
        col_pick[half + index, index] = 1.0
        row_pick[rows + half - index, index] = 1.0
        col_pick[index, lanes + half - index] = 1.0
    return row_pick, col_pick


def vmem(count):
    return [pl.BlockSpec(memory_space=pltpu.VMEM)] * count


def call(kernel, outs, specs, scratch=(), limit=16, us=1, **kwargs):
    return pl.pallas_call(
        kernel,
        out_shape=outs,
        in_specs=specs,
        out_specs=jax.tree.map(lambda _: pl.BlockSpec(memory_space=pltpu.VMEM), outs),
        scratch_shapes=list(scratch),
        cost_estimate=pl.CostEstimate(
            flops=int(us * 5e8), bytes_accessed=int(us * 1e6), transcendentals=0
        ),
        compiler_params=pltpu.CompilerParams(vmem_limit_bytes=limit * MIB),
        **kwargs,
    )


def pupil_steps(rows, lanes, first, last, pupils_ref, weights_ref, row_ref, col_ref, out_ref):
    for k in range(first, last):
        scale = jnp.sqrt(jnp.full((1, 1), weights_ref[k] * (0.5 * steepness), jnp.float32))
        for part in range(2):
            values = (pupils_ref[part, k - first] * scale).astype(jnp.bfloat16)
            columns = dot(values, col_ref[...]).astype(jnp.bfloat16)
            full = dot(row_ref[...], columns)
            pos_pos, pos_neg = full[:rows, :lanes], full[:rows, lanes:]
            neg_pos, neg_neg = full[rows:, :lanes], full[rows:, lanes:]
            out_ref[k, 0 + part] = (pos_pos + neg_neg).astype(jnp.bfloat16)
            out_ref[k, 2 + part] = (pos_pos - neg_neg).astype(jnp.bfloat16)
            out_ref[k, 4 + part] = (pos_neg + neg_pos).astype(jnp.bfloat16)
            out_ref[k, 6 + part] = (pos_neg - neg_pos).astype(jnp.bfloat16)


def edges_kernel(mask_ref, target_ref, first_ref, last_ref, goal_ref, stage_ref, sems):
    tile = mask_ref.shape[0]
    whole = pltpu.make_async_copy(target_ref.at[:, tile:], goal_ref, sems.at[2])
    copies = []
    for index, start in enumerate((0, tile - AMBIT)):
        copy = pltpu.make_async_copy(
            mask_ref.at[pl.ds(start, AMBIT)], stage_ref.at[index], sems.at[index]
        )
        copy.start()
        copies.append(copy)
    whole.start()
    for index, out_ref in enumerate((first_ref, last_ref)):
        copies[index].wait()
        out_ref[...] = stage_ref[index].astype(jnp.bfloat16)
    whole.wait()


def early_kernel(
    rows, lanes, count, mask_ref, pupils_ref, table_ref, weights_ref, row_ref, col_ref,
    mid_ref, out_ref, mask_stage, pupil_stage, sems,
):
    tile = mask_ref.shape[0]
    mask_copy = pltpu.make_async_copy(mask_ref, mask_stage, sems.at[0])
    mask_copy.start()
    pupil_copy = pltpu.make_async_copy(pupils_ref.at[:, pl.ds(0, count)], pupil_stage, sems.at[1])
    pupil_copy.start()
    mask_copy.wait()
    mid_ref[...] = dot(
        table_ref[:, AMBIT : AMBIT + tile], mask_stage[...].astype(jnp.bfloat16)
    )
    pupil_copy.wait()
    pupil_steps(rows, lanes, 0, count, pupil_stage, weights_ref, row_ref, col_ref, out_ref)


def partial_kernel(
    live_ref, mid_ref, top_ref, bottom_ref, table_ref, col_t_ref, own_ref, low_ref, sent_ref
):
    extent = table_ref.shape[1]
    width = mid_ref.shape[1]
    tile = extent - 2 * AMBIT
    total = mid_ref[...] + dot(table_ref[:, :AMBIT], top_ref[...])
    total = total + dot(table_ref[:, extent - AMBIT :], bottom_ref[...])
    total = total.astype(jnp.bfloat16)
    own_ref[...] = total[:, : tile + AMBIT]
    low_ref[...] = total[:, :AMBIT]
    sent_ref[:, :AMBIT] = total[:, width - AMBIT :]
    main = dot(total[:, tile - AMBIT :], col_t_ref[: tile + AMBIT])
    shape = main.shape
    flag = (lax.broadcasted_iota(jnp.int32, shape, 0) == shape[0] - 1) & (
        lax.broadcasted_iota(jnp.int32, shape, 1) == shape[1] - 1
    )
    live = live_ref[0, live_ref.shape[1] - 1].astype(jnp.float32)
    sent_ref[:, AMBIT:] = jnp.where(flag, live, main).astype(jnp.bfloat16)


def late_kernel(
    rows, lanes, first, last, pupils_ref, own_ref, col_t_ref, quads_ref, weights_ref, row_ref, col_ref,
    base_ref, out_ref, pupil_stage, sem,
):
    copy = pltpu.make_async_copy(pupils_ref.at[:, pl.ds(first, last - first)], pupil_stage, sem)
    copy.start()
    out_ref[:first] = quads_ref[...]
    base_ref[...] = dot(own_ref[...], col_t_ref[AMBIT:])
    copy.wait()
    pupil_steps(rows, lanes, first, last, pupil_stage, weights_ref, row_ref, col_ref, out_ref)


def core_kernel(
    rows,
    lanes,
    live_ref,
    base_ref,
    sent_ref,
    low_ref,
    goal_ref,
    other_ref,
    pupil_ref,
    row_ref,
    row_t_ref,
    col_ref,
    col_t_ref,
    out_ref,
    spec_ref,
    amp_ref,
    sec_ref,
    field_ref,
    total_ref,
    slope_ref,
    back_ref,
    sum_ref,
    ans_ref,
):
    tile = goal_ref.shape[0]
    extent = row_ref.shape[1]
    kernels = pupil_ref.shape[0]
    halves = [slice(start, start + 2 * LANE) for start in range(0, tile, 2 * LANE)]
    inner = slice(AMBIT, AMBIT + tile)
    outer = lax.axis_index("col") == 0
    left = sent_ref[:, :AMBIT]
    left = jnp.where(outer, jnp.zeros_like(left), left)
    spec_ref[0] = base_ref[...] + dot(left, col_t_ref[:AMBIT])
    right = low_ref[...]
    right = jnp.where(outer, jnp.zeros_like(right), right)
    spec_ref[1] = sent_ref[:, AMBIT:].astype(jnp.float32) + dot(right, col_t_ref[extent - AMBIT :])
    corner = sent_ref[2 * rows - 16 :, AMBIT + 2 * lanes - LANE :].astype(jnp.float32)
    other_live = jnp.max(corner[15:, LANE - 1 :])
    out_ref[...] = jnp.zeros_like(out_ref)

    def work(item, carry):
        live = jnp.where(item == 0, live_ref[0, 0].astype(jnp.float32), other_live) > 0.0

        @pl.when(live)
        def _():
            spec = spec_ref[item]
            cc, cs = spec[:rows, :lanes], spec[:rows, lanes:]
            sc, ss = spec[rows:, :lanes], spec[rows:, lanes:]
            sum_ref[0] = cc - ss
            sum_ref[1] = sc + cs
            sum_ref[2] = cc + ss
            sum_ref[3] = sc - cs

            def pupil(k, index):
                return pupil_ref[k, index].astype(jnp.float32)

            def section(k, buf):
                u, v, m, n = sum_ref[0], sum_ref[1], sum_ref[2], sum_ref[3]
                pr, pi, mr, mi = (pupil(k, index) for index in range(4))
                big_re = pr * u + mi * v
                big_im = pi * u - mr * v
                small_re = mr * u + pi * v
                small_im = mi * u - pr * v
                pr, pi, mr, mi = (pupil(k, index) for index in range(4, 8))
                big_re2 = pr * m + mi * n
                big_im2 = pi * m - mr * n
                small_re2 = mr * m + pi * n
                small_im2 = mi * m - pr * n

                def pair(place, left, right):
                    where = slice(place * rows, (place + 1) * rows)
                    amp_ref[buf, where, :lanes] = left.astype(jnp.bfloat16)
                    amp_ref[buf, where, lanes:] = right.astype(jnp.bfloat16)

                pair(0, big_re + big_re2, small_im2 - small_im)
                pair(1, -(small_im + small_im2), big_re2 - big_re)
                pair(2, big_im + big_im2, small_re - small_re2)
                pair(3, small_re + small_re2, big_im2 - big_im)
                sec_ref[buf] = dot(amp_ref[buf], col_ref[:, inner]).astype(jnp.bfloat16)

            def field(ks, bufs):
                for where in halves:
                    energy = None
                    for k, buf in zip(ks, bufs):
                        real = dot(row_t_ref[inner], sec_ref[buf, : 2 * rows, where])
                        imag = dot(row_t_ref[inner], sec_ref[buf, 2 * rows :, where])
                        field_ref[k, 0, :, where] = real.astype(jnp.bfloat16)
                        field_ref[k, 1, :, where] = imag.astype(jnp.bfloat16)
                        term = real * real + imag * imag
                        energy = term if energy is None else energy + term
                    total_ref[:, where] += energy

            section(0, 0)
            total_ref[...] = jnp.zeros_like(total_ref)

            def forward(i, carry):
                k = 2 * i
                field((k,), (0,))
                section(k + 1, 1)
                field((k + 1,), (1,))
                section(jnp.minimum(k + 2, kernels - 1), 0)
                return carry

            lax.fori_loop(0, kernels // 2, forward, 0)

            def slopes(ref):
                for where in halves:
                    level = jnp.tanh(total_ref[:, where] - 0.5 * steepness * threshold_level)
                    excess = 0.5 * level + 0.5 - ref[:, where].astype(jnp.float32)
                    slope_ref[:, where] = (excess * (1.0 - level * level)).astype(jnp.bfloat16)

            @pl.when(item == 0)
            def _():
                slopes(goal_ref)

            @pl.when(item > 0)
            def _():
                slopes(other_ref)

            def back(k, buf):
                for where in halves:
                    for part in range(2):
                        cotangent = slope_ref[:, where] * field_ref[k, part, :, where]
                        place = slice(part * 2 * rows, (part + 1) * 2 * rows)
                        back_ref[buf, place, where] = dot(row_ref[:, inner], cotangent).astype(
                            jnp.bfloat16
                        )

            def adjoint(k, buf):
                wave = dot(back_ref[buf], col_t_ref[inner])
                rcc, rcs = wave[:rows, :lanes], wave[:rows, lanes:]
                rsc, rss = wave[rows : 2 * rows, :lanes], wave[rows : 2 * rows, lanes:]
                icc, ics = wave[2 * rows : 3 * rows, :lanes], wave[2 * rows : 3 * rows, lanes:]
                isc, iss = wave[3 * rows :, :lanes], wave[3 * rows :, lanes:]
                ur, ui, vr, vi = rcc - rss, icc - iss, rsc + rcs, isc + ics
                pr, pi, mr, mi = (pupil(k, index) for index in range(4))
                ans_ref[0] += pr * ur + pi * ui + mr * vi - mi * vr
                ans_ref[1] += mr * ui - mi * ur - pr * vr - pi * vi
                ur, ui, vr, vi = rcc + rss, icc + iss, rsc - rcs, isc - ics
                pr, pi, mr, mi = (pupil(k, index) for index in range(4, 8))
                ans_ref[2] += pr * ur + pi * ui + mr * vi - mi * vr
                ans_ref[3] += mr * ui - mi * ur - pr * vr - pi * vi

            ans_ref[...] = jnp.zeros_like(ans_ref)
            back(0, 0)

            def backward(i, carry):
                k = 2 * i
                adjoint(k, 0)
                back(k + 1, 1)
                adjoint(k + 1, 1)
                back(jnp.minimum(k + 2, kernels - 1), 0)
                return carry

            lax.fori_loop(0, kernels // 2, backward, 0)

            def answer(first):
                left, right = slice(first, first + lanes), slice(first + lanes, first + 2 * lanes)
                out_ref[:rows, left] = (ans_ref[0] + ans_ref[2]).astype(jnp.bfloat16)
                out_ref[:rows, right] = (ans_ref[3] - ans_ref[1]).astype(jnp.bfloat16)
                out_ref[rows:, left] = (-(ans_ref[1] + ans_ref[3])).astype(jnp.bfloat16)
                out_ref[rows:, right] = (ans_ref[2] - ans_ref[0]).astype(jnp.bfloat16)

            @pl.when(item == 0)
            def _():
                answer(0)

            @pl.when(item > 0)
            def _():
                answer(2 * lanes)

        return carry

    lax.fori_loop(0, 2, work, 0)


def returned_kernel(tile, mine_ref, sent_ref, row_t_ref, col_ref, out_ref, up_ref, down_ref, sum_ref):
    width = out_ref.shape[1]
    extent = row_t_ref.shape[0]
    lanes = mine_ref.shape[1] // 2
    place = lax.axis_index("col")
    before, after = mine_ref[:, lanes:], sent_ref[:, :lanes]
    before = jnp.where(place == 0, jnp.zeros_like(before), before)
    after = jnp.where(place == lax.axis_size("col") - 1, jnp.zeros_like(after), after)
    sum_ref[...] = jnp.zeros_like(sum_ref)
    for place, value in zip(range(-1, 3), (before, mine_ref[:, :lanes], sent_ref[:, lanes:], after)):
        start = place * tile - AMBIT
        low, high = max(0, start), min(width, start + extent)
        sum_ref[:, low:high] += dot(value, col_ref[:, low - start : high - start])
    mixed = sum_ref[...].astype(jnp.bfloat16)
    out_ref[...] = mixed
    up_ref[...] = dot(row_t_ref[:AMBIT], mixed).astype(jnp.bfloat16)
    down_ref[...] = dot(row_t_ref[extent - AMBIT :], mixed).astype(jnp.bfloat16)


def update_kernel(mask_ref, mixed_ref, row_t_ref, out_ref, rims_ref, stage_ref, sems):
    tile = mask_ref.shape[0]
    copy = pltpu.make_async_copy(mask_ref, stage_ref, sems.at[0])
    copy.start()
    copy.wait()
    stage_ref[...] = stage_ref[...] - step_rate * dot(
        row_t_ref[AMBIT : AMBIT + tile], mixed_ref[...]
    )
    inner = pl.ds(AMBIT, tile - 2 * AMBIT)
    copy = pltpu.make_async_copy(stage_ref.at[inner], out_ref.at[inner], sems.at[1])
    copy.start()
    rims_ref[:AMBIT] = stage_ref[:AMBIT]
    rims_ref[AMBIT:] = stage_ref[tile - AMBIT :]
    copy.wait()


def rims_kernel(above_ref, below_ref, rims_ref, base_ref, out_ref, stage_ref, sems):
    tile = out_ref.shape[0]
    copies = []
    for index, (rim_ref, start) in enumerate(((above_ref, 0), (below_ref, tile - AMBIT))):
        where = pl.ds(index * AMBIT, AMBIT)
        stage_ref[where] = rims_ref[where] - step_rate * rim_ref[...].astype(jnp.float32)
        copy = pltpu.make_async_copy(
            stage_ref.at[where], out_ref.at[pl.ds(start, AMBIT)], sems.at[index]
        )
        copy.start()
        copies.append(copy)
    for copy in copies:
        copy.wait()


def body(mask, target, live, pupils, weights):
    tile, width = mask.shape
    kernels, size = pupils.shape[1], pupils.shape[2]
    half = size // 2
    rows, lanes = round_up(half + 1, 16), round_up(half + 2, LANE)
    extent = tile + 2 * AMBIT
    row_np = half_tables(half, rows, extent)
    col_np = half_tables(half, lanes, extent)
    row_pick, col_pick = (
        jnp.asarray(pick, jnp.bfloat16) for pick in pick_tables(half, rows, lanes)
    )
    row_table, row_table_t = jnp.asarray(row_np, jnp.bfloat16), jnp.asarray(row_np.T, jnp.bfloat16)
    col_table, col_table_t = jnp.asarray(col_np, jnp.bfloat16), jnp.asarray(col_np.T, jnp.bfloat16)
    bf16, f32 = jnp.bfloat16, jnp.float32
    shape = jax.ShapeDtypeStruct
    smem = pl.BlockSpec(memory_space=pltpu.SMEM)
    early = kernels // 2

    hbm = pl.BlockSpec(memory_space=pltpu.HBM)
    dma = pltpu.SemaphoreType.DMA
    edge = shape((AMBIT, width), bf16)
    first, last, goal = call(
        edges_kernel,
        (edge, edge, shape((tile, tile), bf16)),
        [hbm, hbm],
        scratch=[pltpu.VMEM((2, AMBIT, width), f32), dma((3,))],
        limit=52,
    )(mask, target)
    top = stepped(last, "row", 1)
    bottom = stepped(first, "row", -1)
    other_goal = turned(goal, "col", 1)
    middle, quads = call(
        partial(early_kernel, rows, lanes, early),
        (shape((2 * rows, width), f32), shape((early, 8, rows, lanes), bf16)),
        [hbm, hbm, *vmem(1), smem, *vmem(2)],
        scratch=[
            pltpu.VMEM((tile, width), f32), pltpu.VMEM((2, early, size, size), f32), dma((2,)),
        ],
        limit=50,
        us=4,
    )(mask, pupils, row_table, weights, row_pick, col_pick)
    own, low, sending = call(
        partial_kernel,
        (
            shape((2 * rows, tile + AMBIT), bf16),
            shape((2 * rows, AMBIT), bf16),
            shape((2 * rows, AMBIT + 2 * lanes), bf16),
        ),
        [smem, *vmem(5)],
    )(live, middle, top, bottom, row_table, col_table_t)
    sent = turned(sending, "col", 1)
    base, all_quads = call(
        partial(late_kernel, rows, lanes, early, kernels),
        (shape((2 * rows, 2 * lanes), f32), shape((kernels, 8, rows, lanes), bf16)),
        [hbm, *vmem(3), smem, *vmem(2)],
        scratch=[pltpu.VMEM((2, kernels - early, size, size), f32), dma],
        limit=48,
        us=4,
    )(pupils, own, col_table_t, quads, weights, row_pick, col_pick)
    answers = call(
        partial(core_kernel, rows, lanes),
        shape((2 * rows, 4 * lanes), bf16),
        [smem, *vmem(10)],
        scratch=[
            pltpu.VMEM((2, 2 * rows, 2 * lanes), f32),
            pltpu.VMEM((2, 4 * rows, 2 * lanes), bf16),
            pltpu.VMEM((2, 4 * rows, tile), bf16),
            pltpu.VMEM((kernels, 2, tile, tile), bf16),
            pltpu.VMEM((tile, tile), f32),
            pltpu.VMEM((tile, tile), bf16),
            pltpu.VMEM((2, 4 * rows, tile), bf16),
            pltpu.VMEM((4, rows, lanes), f32),
            pltpu.VMEM((4, rows, lanes), f32),
        ],
        limit=36,
        us=15,
    )(
        live, base, sent, low, target, other_goal, all_quads,
        row_table, row_table_t, col_table, col_table_t,
    )
    returned = turned(answers, "col", -1)
    mixed, up, down = call(
        partial(returned_kernel, tile),
        (shape((2 * rows, width), bf16), shape((AMBIT, width), bf16), shape((AMBIT, width), bf16)),
        vmem(4),
        scratch=[pltpu.VMEM((2 * rows, width), f32)],
    )(answers, returned, row_table_t, col_table)
    from_above = stepped(down, "row", 1)
    from_below = stepped(up, "row", -1)
    anywhere = pl.BlockSpec(memory_space=pl.ANY)
    whole, rims = shape((tile, width), f32), shape((2 * AMBIT, width), f32)
    updated, edges = pl.pallas_call(
        update_kernel,
        out_shape=(whole, rims),
        in_specs=[hbm, *vmem(2)],
        out_specs=(anywhere, *vmem(1)),
        scratch_shapes=[pltpu.VMEM((tile, width), f32), dma((2,))],
        cost_estimate=pl.CostEstimate(flops=10**9, bytes_accessed=2 * 10**6, transcendentals=0),
        compiler_params=pltpu.CompilerParams(vmem_limit_bytes=16 * MIB),
    )(mask, mixed, row_table_t)
    return pl.pallas_call(
        rims_kernel,
        out_shape=whole,
        in_specs=[*vmem(3), anywhere],
        out_specs=anywhere,
        scratch_shapes=[pltpu.VMEM((2 * AMBIT, width), f32), pltpu.SemaphoreType.DMA((2,))],
        input_output_aliases={3: 0},
        compiler_params=pltpu.CompilerParams(vmem_limit_bytes=8 * MIB),
    )(from_above, from_below, edges, updated)


def solution(mesh):
    placed = (P("row", "col"), P("row", "col"), P("row", "col"), P(), P())
    return jax.shard_map(
        body, mesh=mesh, in_specs=placed, out_specs=P("row", "col"), check_vma=False
    )
```

```python
from functools import partial
import math

import jax
import jax.numpy as jnp
import numpy as np
from jax import lax
from jax.experimental import pallas as pl
from jax.experimental.pallas import tpu as pltpu
from jax.sharding import PartitionSpec as P


AMBIT = 128
LANE = 128

steepness = 4.0
threshold_level = 1.0
step_rate = 8.0

MIB = 1024 * 1024


def round_up(value, unit):
    return -(-value // unit) * unit


def stepped(block, axis, step):
    count = lax.axis_size(axis)
    pairs = [(i, i + step) for i in range(count) if 0 <= i + step < count]
    return lax.ppermute(block, axis, pairs)


def turned(block, step):
    height, count = lax.axis_size("row"), lax.axis_size("col")
    pairs = [
        (row * count + col, row * count + (col + (step if row % 2 == 0 else -step)) % count)
        for row in range(height)
        for col in range(count)
    ]
    return lax.ppermute(block, ("row", "col"), pairs)


def row_parity():
    return lax.rem(lax.axis_index("row"), 2)


def dot(leading, trailing):
    return jnp.dot(leading, trailing, preferred_element_type=jnp.float32)


def half_tables(half, rows, extent):
    frequency = np.arange(half + 1, dtype=np.int64)
    pixels = np.arange(extent, dtype=np.int64)
    phases = np.mod(frequency[:, None] * pixels[None, :], extent).astype(np.float32)
    angles = phases * np.float32(2.0 * math.pi / extent)
    factor = np.float32(1.0 / math.sqrt(extent))
    table = np.zeros((2 * rows, extent), np.float32)
    table[: half + 1] = np.cos(angles) * factor
    table[rows : rows + half + 1] = np.sin(angles) * factor
    return table


def pick_tables(half, rows, lanes):
    size = 2 * half
    row_pick = np.zeros((2 * rows, size), np.float32)
    col_pick = np.zeros((size, 2 * lanes), np.float32)
    for index in range(half):
        row_pick[index, half + index] = 1.0
        col_pick[half + index, index] = 1.0
        row_pick[rows + half - index, index] = 1.0
        col_pick[index, lanes + half - index] = 1.0
    return row_pick, col_pick


def vmem(count):
    return [pl.BlockSpec(memory_space=pltpu.VMEM)] * count


def call(kernel, outs, specs, scratch=(), limit=16, us=1, **kwargs):
    return pl.pallas_call(
        kernel,
        out_shape=outs,
        in_specs=specs,
        out_specs=jax.tree.map(lambda _: pl.BlockSpec(memory_space=pltpu.VMEM), outs),
        scratch_shapes=list(scratch),
        cost_estimate=pl.CostEstimate(
            flops=int(us * 5e8), bytes_accessed=int(us * 1e6), transcendentals=0
        ),
        compiler_params=pltpu.CompilerParams(vmem_limit_bytes=limit * MIB),
        **kwargs,
    )


def pupil_steps(rows, lanes, first, last, pupils_ref, weights_ref, row_ref, col_ref, out_ref):
    for k in range(first, last):
        scale = jnp.sqrt(jnp.full((1, 1), weights_ref[k] * (0.5 * steepness), jnp.float32))
        for part in range(2):
            values = (pupils_ref[part, k - first] * scale).astype(jnp.bfloat16)
            columns = dot(values, col_ref[...]).astype(jnp.bfloat16)
            full = dot(row_ref[...], columns)
            pos_pos, pos_neg = full[:rows, :lanes], full[:rows, lanes:]
            neg_pos, neg_neg = full[rows:, :lanes], full[rows:, lanes:]
            out_ref[k, 0 + part] = (pos_pos + neg_neg).astype(jnp.bfloat16)
            out_ref[k, 2 + part] = (pos_pos - neg_neg).astype(jnp.bfloat16)
            out_ref[k, 4 + part] = (pos_neg + neg_pos).astype(jnp.bfloat16)
            out_ref[k, 6 + part] = (pos_neg - neg_pos).astype(jnp.bfloat16)


def edges_kernel(mask_ref, target_ref, first_ref, last_ref, goal_ref, stage_ref, sems):
    tile = mask_ref.shape[0]
    far = pl.multiple_of((1 - row_parity()) * tile, LANE)
    whole = pltpu.make_async_copy(target_ref.at[:, pl.ds(far, tile)], goal_ref, sems.at[2])
    copies = []
    for index, start in enumerate((0, tile - AMBIT)):
        copy = pltpu.make_async_copy(
            mask_ref.at[pl.ds(start, AMBIT)], stage_ref.at[index], sems.at[index]
        )
        copy.start()
        copies.append(copy)
    whole.start()
    for index, out_ref in enumerate((first_ref, last_ref)):
        copies[index].wait()
        out_ref[...] = stage_ref[index].astype(jnp.bfloat16)
    whole.wait()


def early_kernel(
    rows, lanes, count, mask_ref, pupils_ref, table_ref, weights_ref, row_ref, col_ref,
    mid_ref, out_ref, mask_stage, pupil_stage, sems,
):
    tile = mask_ref.shape[0]
    mask_copy = pltpu.make_async_copy(mask_ref, mask_stage, sems.at[0])
    mask_copy.start()
    pupil_copy = pltpu.make_async_copy(pupils_ref.at[:, pl.ds(0, count)], pupil_stage, sems.at[1])
    pupil_copy.start()
    mask_copy.wait()
    mid_ref[...] = dot(
        table_ref[:, AMBIT : AMBIT + tile], mask_stage[...].astype(jnp.bfloat16)
    )
    pupil_copy.wait()
    pupil_steps(rows, lanes, 0, count, pupil_stage, weights_ref, row_ref, col_ref, out_ref)


def partial_kernel(
    live_ref, mid_ref, top_ref, bottom_ref, table_ref, col_t_ref, own_ref, kept_ref, sent_ref
):
    extent = table_ref.shape[1]
    width = mid_ref.shape[1]
    tile = extent - 2 * AMBIT
    total = mid_ref[...] + dot(table_ref[:, :AMBIT], top_ref[...])
    total = total + dot(table_ref[:, extent - AMBIT :], bottom_ref[...])
    total = total.astype(jnp.bfloat16)
    parity = row_parity()
    live = live_ref[0, 1 - parity].astype(jnp.float32)

    def store(near, far, far_table, facing, kept):
        own_ref[...] = total[:, near]
        kept_ref[...] = total[:, kept]
        sent_ref[:, :AMBIT] = total[:, facing]
        main = dot(total[:, far], col_t_ref[far_table])
        shape = main.shape
        flag = (lax.broadcasted_iota(jnp.int32, shape, 0) == shape[0] - 1) & (
            lax.broadcasted_iota(jnp.int32, shape, 1) == shape[1] - 1
        )
        sent_ref[:, AMBIT:] = jnp.where(flag, live, main).astype(jnp.bfloat16)

    reach = tile + AMBIT
    first, last = slice(0, reach), slice(width - reach, width)
    low, high = slice(0, AMBIT), slice(width - AMBIT, width)

    @pl.when(parity == 0)
    def _():
        store(first, last, slice(0, reach), high, low)

    @pl.when(parity > 0)
    def _():
        store(last, first, slice(AMBIT, extent), low, high)


def late_kernel(
    rows, lanes, first, last, pupils_ref, own_ref, col_t_ref, quads_ref, weights_ref, row_ref, col_ref,
    base_ref, out_ref, pupil_stage, sem,
):
    copy = pltpu.make_async_copy(pupils_ref.at[:, pl.ds(first, last - first)], pupil_stage, sem)
    copy.start()
    out_ref[:first] = quads_ref[...]
    reach = own_ref.shape[1]
    start = pl.multiple_of((1 - row_parity()) * AMBIT, AMBIT)
    base_ref[...] = dot(own_ref[...], col_t_ref[pl.ds(start, reach)])
    copy.wait()
    pupil_steps(rows, lanes, first, last, pupil_stage, weights_ref, row_ref, col_ref, out_ref)


def core_kernel(
    rows,
    lanes,
    live_ref,
    base_ref,
    sent_ref,
    kept_ref,
    goal_ref,
    other_ref,
    pupil_ref,
    row_ref,
    row_t_ref,
    col_ref,
    col_t_ref,
    out_ref,
    spec_ref,
    amp_ref,
    sec_ref,
    field_ref,
    total_ref,
    slope_ref,
    back_ref,
    sum_ref,
    ans_ref,
):
    tile = goal_ref.shape[0]
    extent = row_ref.shape[1]
    kernels = pupil_ref.shape[0]
    halves = [slice(start, start + 2 * LANE) for start in range(0, tile, 2 * LANE)]
    inner = slice(AMBIT, AMBIT + tile)
    parity = row_parity()
    outer = lax.axis_index("col") == parity * (lax.axis_size("col") - 1)
    ends = [
        pl.multiple_of(side * (extent - AMBIT), AMBIT) for side in (parity, 1 - parity)
    ]
    facing = sent_ref[:, :AMBIT]
    facing = jnp.where(outer, jnp.zeros_like(facing), facing)
    spec_ref[0] = base_ref[...] + dot(facing, col_t_ref[pl.ds(ends[0], AMBIT)])
    kept = kept_ref[...]
    kept = jnp.where(outer, jnp.zeros_like(kept), kept)
    spec_ref[1] = sent_ref[:, AMBIT:].astype(jnp.float32) + dot(
        kept, col_t_ref[pl.ds(ends[1], AMBIT)]
    )
    corner = sent_ref[2 * rows - 16 :, AMBIT + 2 * lanes - LANE :].astype(jnp.float32)
    other_live = jnp.max(corner[15:, LANE - 1 :])
    out_ref[...] = jnp.zeros_like(out_ref)

    def work(item, carry):
        live = jnp.where(item == 0, live_ref[0, parity].astype(jnp.float32), other_live) > 0.0

        @pl.when(live)
        def _():
            spec = spec_ref[item]
            cc, cs = spec[:rows, :lanes], spec[:rows, lanes:]
            sc, ss = spec[rows:, :lanes], spec[rows:, lanes:]
            sum_ref[0] = cc - ss
            sum_ref[1] = sc + cs
            sum_ref[2] = cc + ss
            sum_ref[3] = sc - cs

            def pupil(k, index):
                return pupil_ref[k, index].astype(jnp.float32)

            def section(k, buf):
                u, v, m, n = sum_ref[0], sum_ref[1], sum_ref[2], sum_ref[3]
                pr, pi, mr, mi = (pupil(k, index) for index in range(4))
                big_re = pr * u + mi * v
                big_im = pi * u - mr * v
                small_re = mr * u + pi * v
                small_im = mi * u - pr * v
                pr, pi, mr, mi = (pupil(k, index) for index in range(4, 8))
                big_re2 = pr * m + mi * n
                big_im2 = pi * m - mr * n
                small_re2 = mr * m + pi * n
                small_im2 = mi * m - pr * n

                def pair(place, left, right):
                    where = slice(place * rows, (place + 1) * rows)
                    amp_ref[buf, where, :lanes] = left.astype(jnp.bfloat16)
                    amp_ref[buf, where, lanes:] = right.astype(jnp.bfloat16)

                pair(0, big_re + big_re2, small_im2 - small_im)
                pair(1, -(small_im + small_im2), big_re2 - big_re)
                pair(2, big_im + big_im2, small_re - small_re2)
                pair(3, small_re + small_re2, big_im2 - big_im)
                sec_ref[buf] = dot(amp_ref[buf], col_ref[:, inner]).astype(jnp.bfloat16)

            def field(ks, bufs):
                for where in halves:
                    energy = None
                    for k, buf in zip(ks, bufs):
                        real = dot(row_t_ref[inner], sec_ref[buf, : 2 * rows, where])
                        imag = dot(row_t_ref[inner], sec_ref[buf, 2 * rows :, where])
                        field_ref[k, 0, :, where] = real.astype(jnp.bfloat16)
                        field_ref[k, 1, :, where] = imag.astype(jnp.bfloat16)
                        term = real * real + imag * imag
                        energy = term if energy is None else energy + term
                    total_ref[:, where] += energy

            section(0, 0)
            total_ref[...] = jnp.zeros_like(total_ref)

            def forward(i, carry):
                k = 2 * i
                field((k,), (0,))
                section(k + 1, 1)
                field((k + 1,), (1,))
                section(jnp.minimum(k + 2, kernels - 1), 0)
                return carry

            lax.fori_loop(0, kernels // 2, forward, 0)

            def slopes(ref, first):
                for where in halves:
                    place = pl.ds(pl.multiple_of(first + where.start, LANE), 2 * LANE)
                    level = jnp.tanh(total_ref[:, where] - 0.5 * steepness * threshold_level)
                    excess = 0.5 * level + 0.5 - ref[:, place].astype(jnp.float32)
                    slope_ref[:, where] = (excess * (1.0 - level * level)).astype(jnp.bfloat16)

            @pl.when(item == 0)
            def _():
                slopes(goal_ref, parity * tile)

            @pl.when(item > 0)
            def _():
                slopes(other_ref, 0)

            def back(k, buf):
                for where in halves:
                    for part in range(2):
                        cotangent = slope_ref[:, where] * field_ref[k, part, :, where]
                        place = slice(part * 2 * rows, (part + 1) * 2 * rows)
                        back_ref[buf, place, where] = dot(row_ref[:, inner], cotangent).astype(
                            jnp.bfloat16
                        )

            def adjoint(k, buf):
                wave = dot(back_ref[buf], col_t_ref[inner])
                rcc, rcs = wave[:rows, :lanes], wave[:rows, lanes:]
                rsc, rss = wave[rows : 2 * rows, :lanes], wave[rows : 2 * rows, lanes:]
                icc, ics = wave[2 * rows : 3 * rows, :lanes], wave[2 * rows : 3 * rows, lanes:]
                isc, iss = wave[3 * rows :, :lanes], wave[3 * rows :, lanes:]
                ur, ui, vr, vi = rcc - rss, icc - iss, rsc + rcs, isc + ics
                pr, pi, mr, mi = (pupil(k, index) for index in range(4))
                ans_ref[0] += pr * ur + pi * ui + mr * vi - mi * vr
                ans_ref[1] += mr * ui - mi * ur - pr * vr - pi * vi
                ur, ui, vr, vi = rcc + rss, icc + iss, rsc - rcs, isc - ics
                pr, pi, mr, mi = (pupil(k, index) for index in range(4, 8))
                ans_ref[2] += pr * ur + pi * ui + mr * vi - mi * vr
                ans_ref[3] += mr * ui - mi * ur - pr * vr - pi * vi

            ans_ref[...] = jnp.zeros_like(ans_ref)
            back(0, 0)

            def backward(i, carry):
                k = 2 * i
                adjoint(k, 0)
                back(k + 1, 1)
                adjoint(k + 1, 1)
                back(jnp.minimum(k + 2, kernels - 1), 0)
                return carry

            lax.fori_loop(0, kernels // 2, backward, 0)

            def answer(first):
                left, right = slice(first, first + lanes), slice(first + lanes, first + 2 * lanes)
                out_ref[:rows, left] = (ans_ref[0] + ans_ref[2]).astype(jnp.bfloat16)
                out_ref[:rows, right] = (ans_ref[3] - ans_ref[1]).astype(jnp.bfloat16)
                out_ref[rows:, left] = (-(ans_ref[1] + ans_ref[3])).astype(jnp.bfloat16)
                out_ref[rows:, right] = (ans_ref[2] - ans_ref[0]).astype(jnp.bfloat16)

            @pl.when(item == 0)
            def _():
                answer(0)

            @pl.when(item > 0)
            def _():
                answer(2 * lanes)

        return carry

    lax.fori_loop(0, 2, work, 0)


def returned_kernel(tile, mine_ref, sent_ref, row_t_ref, col_ref, out_ref, up_ref, down_ref, sum_ref):
    width = out_ref.shape[1]
    extent = row_t_ref.shape[0]
    lanes = mine_ref.shape[1] // 2
    column = lax.axis_index("col")
    odd = row_parity() > 0
    mine, my_other = mine_ref[:, :lanes], mine_ref[:, lanes:]
    theirs, their_other = sent_ref[:, :lanes], sent_ref[:, lanes:]
    before = jnp.where(odd, theirs, my_other)
    before = jnp.where(column == 0, jnp.zeros_like(before), before)
    first = jnp.where(odd, their_other, mine)
    second = jnp.where(odd, mine, their_other)
    after = jnp.where(odd, my_other, theirs)
    after = jnp.where(column == lax.axis_size("col") - 1, jnp.zeros_like(after), after)
    sum_ref[...] = jnp.zeros_like(sum_ref)
    for place, value in zip(range(-1, 3), (before, first, second, after)):
        start = place * tile - AMBIT
        low, high = max(0, start), min(width, start + extent)
        sum_ref[:, low:high] += dot(value, col_ref[:, low - start : high - start])
    mixed = sum_ref[...].astype(jnp.bfloat16)
    out_ref[...] = mixed
    up_ref[...] = dot(row_t_ref[:AMBIT], mixed).astype(jnp.bfloat16)
    down_ref[...] = dot(row_t_ref[extent - AMBIT :], mixed).astype(jnp.bfloat16)


def update_kernel(mask_ref, mixed_ref, row_t_ref, out_ref, rims_ref, stage_ref, sems):
    tile = mask_ref.shape[0]
    copy = pltpu.make_async_copy(mask_ref, stage_ref, sems.at[0])
    copy.start()
    copy.wait()
    stage_ref[...] = stage_ref[...] - step_rate * dot(
        row_t_ref[AMBIT : AMBIT + tile], mixed_ref[...]
    )
    inner = pl.ds(AMBIT, tile - 2 * AMBIT)
    copy = pltpu.make_async_copy(stage_ref.at[inner], out_ref.at[inner], sems.at[1])
    copy.start()
    rims_ref[:AMBIT] = stage_ref[:AMBIT]
    rims_ref[AMBIT:] = stage_ref[tile - AMBIT :]
    copy.wait()


def rims_kernel(above_ref, below_ref, rims_ref, base_ref, out_ref, stage_ref, sems):
    tile = out_ref.shape[0]
    copies = []
    for index, (rim_ref, start) in enumerate(((above_ref, 0), (below_ref, tile - AMBIT))):
        where = pl.ds(index * AMBIT, AMBIT)
        stage_ref[where] = rims_ref[where] - step_rate * rim_ref[...].astype(jnp.float32)
        copy = pltpu.make_async_copy(
            stage_ref.at[where], out_ref.at[pl.ds(start, AMBIT)], sems.at[index]
        )
        copy.start()
        copies.append(copy)
    for copy in copies:
        copy.wait()


def body(mask, target, live, pupils, weights):
    tile, width = mask.shape
    kernels, size = pupils.shape[1], pupils.shape[2]
    half = size // 2
    rows, lanes = round_up(half + 1, 16), round_up(half + 2, LANE)
    extent = tile + 2 * AMBIT
    row_np = half_tables(half, rows, extent)
    col_np = half_tables(half, lanes, extent)
    row_pick, col_pick = (
        jnp.asarray(pick, jnp.bfloat16) for pick in pick_tables(half, rows, lanes)
    )
    row_table, row_table_t = jnp.asarray(row_np, jnp.bfloat16), jnp.asarray(row_np.T, jnp.bfloat16)
    col_table, col_table_t = jnp.asarray(col_np, jnp.bfloat16), jnp.asarray(col_np.T, jnp.bfloat16)
    bf16, f32 = jnp.bfloat16, jnp.float32
    shape = jax.ShapeDtypeStruct
    smem = pl.BlockSpec(memory_space=pltpu.SMEM)
    early = kernels // 2

    hbm = pl.BlockSpec(memory_space=pltpu.HBM)
    dma = pltpu.SemaphoreType.DMA
    edge = shape((AMBIT, width), bf16)
    first, last, goal = call(
        edges_kernel,
        (edge, edge, shape((tile, tile), bf16)),
        [hbm, hbm],
        scratch=[pltpu.VMEM((2, AMBIT, width), f32), dma((3,))],
        limit=52,
    )(mask, target)
    top = stepped(last, "row", 1)
    bottom = stepped(first, "row", -1)
    other_goal = turned(goal, 1)
    middle, quads = call(
        partial(early_kernel, rows, lanes, early),
        (shape((2 * rows, width), f32), shape((early, 8, rows, lanes), bf16)),
        [hbm, hbm, *vmem(1), smem, *vmem(2)],
        scratch=[
            pltpu.VMEM((tile, width), f32), pltpu.VMEM((2, early, size, size), f32), dma((2,)),
        ],
        limit=50,
        us=4,
    )(mask, pupils, row_table, weights, row_pick, col_pick)
    own, kept, sending = call(
        partial_kernel,
        (
            shape((2 * rows, tile + AMBIT), bf16),
            shape((2 * rows, AMBIT), bf16),
            shape((2 * rows, AMBIT + 2 * lanes), bf16),
        ),
        [smem, *vmem(5)],
    )(live, middle, top, bottom, row_table, col_table_t)
    sent = turned(sending, 1)
    base, all_quads = call(
        partial(late_kernel, rows, lanes, early, kernels),
        (shape((2 * rows, 2 * lanes), f32), shape((kernels, 8, rows, lanes), bf16)),
        [hbm, *vmem(3), smem, *vmem(2)],
        scratch=[pltpu.VMEM((2, kernels - early, size, size), f32), dma],
        limit=48,
        us=4,
    )(pupils, own, col_table_t, quads, weights, row_pick, col_pick)
    answers = call(
        partial(core_kernel, rows, lanes),
        shape((2 * rows, 4 * lanes), bf16),
        [smem, *vmem(10)],
        scratch=[
            pltpu.VMEM((2, 2 * rows, 2 * lanes), f32),
            pltpu.VMEM((2, 4 * rows, 2 * lanes), bf16),
            pltpu.VMEM((2, 4 * rows, tile), bf16),
            pltpu.VMEM((kernels, 2, tile, tile), bf16),
            pltpu.VMEM((tile, tile), f32),
            pltpu.VMEM((tile, tile), bf16),
            pltpu.VMEM((2, 4 * rows, tile), bf16),
            pltpu.VMEM((4, rows, lanes), f32),
            pltpu.VMEM((4, rows, lanes), f32),
        ],
        limit=36,
        us=15,
    )(
        live, base, sent, kept, target, other_goal, all_quads,
        row_table, row_table_t, col_table, col_table_t,
    )
    returned = turned(answers, -1)
    mixed, up, down = call(
        partial(returned_kernel, tile),
        (shape((2 * rows, width), bf16), shape((AMBIT, width), bf16), shape((AMBIT, width), bf16)),
        vmem(4),
        scratch=[pltpu.VMEM((2 * rows, width), f32)],
    )(answers, returned, row_table_t, col_table)
    from_above = stepped(down, "row", 1)
    from_below = stepped(up, "row", -1)
    anywhere = pl.BlockSpec(memory_space=pl.ANY)
    whole, rims = shape((tile, width), f32), shape((2 * AMBIT, width), f32)
    updated, edges = pl.pallas_call(
        update_kernel,
        out_shape=(whole, rims),
        in_specs=[hbm, *vmem(2)],
        out_specs=(anywhere, *vmem(1)),
        scratch_shapes=[pltpu.VMEM((tile, width), f32), dma((2,))],
        cost_estimate=pl.CostEstimate(flops=10**9, bytes_accessed=2 * 10**6, transcendentals=0),
        compiler_params=pltpu.CompilerParams(vmem_limit_bytes=16 * MIB),
    )(mask, mixed, row_table_t)
    return pl.pallas_call(
        rims_kernel,
        out_shape=whole,
        in_specs=[*vmem(3), anywhere],
        out_specs=anywhere,
        scratch_shapes=[pltpu.VMEM((2 * AMBIT, width), f32), pltpu.SemaphoreType.DMA((2,))],
        input_output_aliases={3: 0},
        compiler_params=pltpu.CompilerParams(vmem_limit_bytes=8 * MIB),
    )(from_above, from_below, edges, updated)


def solution(mesh):
    placed = (P("row", "col"), P("row", "col"), P("row", "col"), P(), P())
    return jax.shard_map(
        body, mesh=mesh, in_specs=placed, out_specs=P("row", "col"), check_vma=False
    )
```

```python
from functools import partial
import math

import jax
import jax.numpy as jnp
import numpy as np
from jax import lax
from jax.experimental import pallas as pl
from jax.experimental.pallas import tpu as pltpu
from jax.sharding import PartitionSpec as P


AMBIT = 128
LANE = 128

steepness = 4.0
threshold_level = 1.0
step_rate = 8.0

MIB = 1024 * 1024


def round_up(value, unit):
    return -(-value // unit) * unit


def swapped(block, axis, offset):
    count = lax.axis_size(axis)
    pairs = []
    for low in range(offset, count - 1, 2):
        pairs += [(low, low + 1), (low + 1, low)]
    return lax.ppermute(block, axis, pairs)


def sides(reach):
    odd = lax.rem(lax.axis_index("row"), 2)
    return [pl.multiple_of(side * reach, AMBIT) for side in (1 - odd, odd)]


def turned(block, axis, step):
    count = lax.axis_size(axis)
    return lax.ppermute(block, axis, [(i, (i + step) % count) for i in range(count)])


def dot(leading, trailing):
    return jnp.dot(leading, trailing, preferred_element_type=jnp.float32)


def half_tables(half, rows, extent):
    frequency = np.arange(half + 1, dtype=np.int64)
    pixels = np.arange(extent, dtype=np.int64)
    phases = np.mod(frequency[:, None] * pixels[None, :], extent).astype(np.float32)
    angles = phases * np.float32(2.0 * math.pi / extent)
    factor = np.float32(1.0 / math.sqrt(extent))
    table = np.zeros((2 * rows, extent), np.float32)
    table[: half + 1] = np.cos(angles) * factor
    table[rows : rows + half + 1] = np.sin(angles) * factor
    return table


def pick_tables(half, rows, lanes):
    size = 2 * half
    row_pick = np.zeros((2 * rows, size), np.float32)
    col_pick = np.zeros((size, 2 * lanes), np.float32)
    for index in range(half):
        row_pick[index, half + index] = 1.0
        col_pick[half + index, index] = 1.0
        row_pick[rows + half - index, index] = 1.0
        col_pick[index, lanes + half - index] = 1.0
    return row_pick, col_pick


def vmem(count):
    return [pl.BlockSpec(memory_space=pltpu.VMEM)] * count


def call(kernel, outs, specs, scratch=(), limit=16, us=1, **kwargs):
    return pl.pallas_call(
        kernel,
        out_shape=outs,
        in_specs=specs,
        out_specs=jax.tree.map(lambda _: pl.BlockSpec(memory_space=pltpu.VMEM), outs),
        scratch_shapes=list(scratch),
        cost_estimate=pl.CostEstimate(
            flops=int(us * 5e8), bytes_accessed=int(us * 1e6), transcendentals=0
        ),
        compiler_params=pltpu.CompilerParams(vmem_limit_bytes=limit * MIB),
        **kwargs,
    )


def pupil_steps(rows, lanes, first, last, pupils_ref, weights_ref, row_ref, col_ref, out_ref):
    for k in range(first, last):
        scale = jnp.sqrt(jnp.full((1, 1), weights_ref[k] * (0.5 * steepness), jnp.float32))
        for part in range(2):
            values = (pupils_ref[part, k - first] * scale).astype(jnp.bfloat16)
            columns = dot(values, col_ref[...]).astype(jnp.bfloat16)
            full = dot(row_ref[...], columns)
            pos_pos, pos_neg = full[:rows, :lanes], full[:rows, lanes:]
            neg_pos, neg_neg = full[rows:, :lanes], full[rows:, lanes:]
            out_ref[k, 0 + part] = (pos_pos + neg_neg).astype(jnp.bfloat16)
            out_ref[k, 2 + part] = (pos_pos - neg_neg).astype(jnp.bfloat16)
            out_ref[k, 4 + part] = (pos_neg + neg_pos).astype(jnp.bfloat16)
            out_ref[k, 6 + part] = (pos_neg - neg_pos).astype(jnp.bfloat16)


def edges_kernel(mask_ref, target_ref, near_ref, cross_ref, goal_ref, stage_ref, sems):
    tile = mask_ref.shape[0]
    whole = pltpu.make_async_copy(target_ref.at[:, tile:], goal_ref, sems.at[2])
    copies = []
    for index, start in enumerate(sides(tile - AMBIT)):
        copy = pltpu.make_async_copy(
            mask_ref.at[pl.ds(start, AMBIT)], stage_ref.at[index], sems.at[index]
        )
        copy.start()
        copies.append(copy)
    whole.start()
    for index, out_ref in enumerate((near_ref, cross_ref)):
        copies[index].wait()
        out_ref[...] = stage_ref[index].astype(jnp.bfloat16)
    whole.wait()


def early_kernel(
    rows, lanes, count, mask_ref, pupils_ref, table_ref, weights_ref, row_ref, col_ref,
    mid_ref, out_ref, mask_stage, pupil_stage, sems,
):
    tile = mask_ref.shape[0]
    mask_copy = pltpu.make_async_copy(mask_ref, mask_stage, sems.at[0])
    mask_copy.start()
    pupil_copy = pltpu.make_async_copy(pupils_ref.at[:, pl.ds(0, count)], pupil_stage, sems.at[1])
    pupil_copy.start()
    mask_copy.wait()
    mid_ref[...] = dot(
        table_ref[:, AMBIT : AMBIT + tile], mask_stage[...].astype(jnp.bfloat16)
    )
    pupil_copy.wait()
    pupil_steps(rows, lanes, 0, count, pupil_stage, weights_ref, row_ref, col_ref, out_ref)


def partial_kernel(
    live_ref, mid_ref, near_ref, cross_ref, table_ref, col_t_ref, own_ref, low_ref, sent_ref
):
    extent = table_ref.shape[1]
    width = mid_ref.shape[1]
    tile = extent - 2 * AMBIT
    total = mid_ref[...]
    for start, rim_ref in zip(sides(extent - AMBIT), (near_ref, cross_ref)):
        total = total + dot(table_ref[:, pl.ds(start, AMBIT)], rim_ref[...])
    total = total.astype(jnp.bfloat16)
    own_ref[...] = total[:, : tile + AMBIT]
    low_ref[...] = total[:, :AMBIT]
    sent_ref[:, :AMBIT] = total[:, width - AMBIT :]
    main = dot(total[:, tile - AMBIT :], col_t_ref[: tile + AMBIT])
    shape = main.shape
    flag = (lax.broadcasted_iota(jnp.int32, shape, 0) == shape[0] - 1) & (
        lax.broadcasted_iota(jnp.int32, shape, 1) == shape[1] - 1
    )
    live = live_ref[0, live_ref.shape[1] - 1].astype(jnp.float32)
    sent_ref[:, AMBIT:] = jnp.where(flag, live, main).astype(jnp.bfloat16)


def late_kernel(
    rows, lanes, first, last, pupils_ref, own_ref, col_t_ref, quads_ref, weights_ref, row_ref, col_ref,
    base_ref, out_ref, pupil_stage, sem,
):
    copy = pltpu.make_async_copy(pupils_ref.at[:, pl.ds(first, last - first)], pupil_stage, sem)
    copy.start()
    out_ref[:first] = quads_ref[...]
    base_ref[...] = dot(own_ref[...], col_t_ref[AMBIT:])
    copy.wait()
    pupil_steps(rows, lanes, first, last, pupil_stage, weights_ref, row_ref, col_ref, out_ref)


def core_kernel(
    rows,
    lanes,
    live_ref,
    base_ref,
    sent_ref,
    low_ref,
    goal_ref,
    other_ref,
    pupil_ref,
    row_ref,
    row_t_ref,
    col_ref,
    col_t_ref,
    out_ref,
    spec_ref,
    amp_ref,
    sec_ref,
    field_ref,
    total_ref,
    slope_ref,
    back_ref,
    sum_ref,
    ans_ref,
):
    tile = goal_ref.shape[0]
    extent = row_ref.shape[1]
    kernels = pupil_ref.shape[0]
    halves = [slice(start, start + 2 * LANE) for start in range(0, tile, 2 * LANE)]
    inner = slice(AMBIT, AMBIT + tile)
    outer = lax.axis_index("col") == 0
    left = sent_ref[:, :AMBIT]
    left = jnp.where(outer, jnp.zeros_like(left), left)
    spec_ref[0] = base_ref[...] + dot(left, col_t_ref[:AMBIT])
    right = low_ref[...]
    right = jnp.where(outer, jnp.zeros_like(right), right)
    spec_ref[1] = sent_ref[:, AMBIT:].astype(jnp.float32) + dot(right, col_t_ref[extent - AMBIT :])
    corner = sent_ref[2 * rows - 16 :, AMBIT + 2 * lanes - LANE :].astype(jnp.float32)
    other_live = jnp.max(corner[15:, LANE - 1 :])
    out_ref[...] = jnp.zeros_like(out_ref)

    def work(item, carry):
        live = jnp.where(item == 0, live_ref[0, 0].astype(jnp.float32), other_live) > 0.0

        @pl.when(live)
        def _():
            spec = spec_ref[item]
            cc, cs = spec[:rows, :lanes], spec[:rows, lanes:]
            sc, ss = spec[rows:, :lanes], spec[rows:, lanes:]
            sum_ref[0] = cc - ss
            sum_ref[1] = sc + cs
            sum_ref[2] = cc + ss
            sum_ref[3] = sc - cs

            def pupil(k, index):
                return pupil_ref[k, index].astype(jnp.float32)

            def section(k, buf):
                u, v, m, n = sum_ref[0], sum_ref[1], sum_ref[2], sum_ref[3]
                pr, pi, mr, mi = (pupil(k, index) for index in range(4))
                big_re = pr * u + mi * v
                big_im = pi * u - mr * v
                small_re = mr * u + pi * v
                small_im = mi * u - pr * v
                pr, pi, mr, mi = (pupil(k, index) for index in range(4, 8))
                big_re2 = pr * m + mi * n
                big_im2 = pi * m - mr * n
                small_re2 = mr * m + pi * n
                small_im2 = mi * m - pr * n

                def pair(place, left, right):
                    where = slice(place * rows, (place + 1) * rows)
                    amp_ref[buf, where, :lanes] = left.astype(jnp.bfloat16)
                    amp_ref[buf, where, lanes:] = right.astype(jnp.bfloat16)

                pair(0, big_re + big_re2, small_im2 - small_im)
                pair(1, -(small_im + small_im2), big_re2 - big_re)
                pair(2, big_im + big_im2, small_re - small_re2)
                pair(3, small_re + small_re2, big_im2 - big_im)
                sec_ref[buf] = dot(amp_ref[buf], col_ref[:, inner]).astype(jnp.bfloat16)

            def field(ks, bufs):
                for where in halves:
                    energy = None
                    for k, buf in zip(ks, bufs):
                        real = dot(row_t_ref[inner], sec_ref[buf, : 2 * rows, where])
                        imag = dot(row_t_ref[inner], sec_ref[buf, 2 * rows :, where])
                        field_ref[k, 0, :, where] = real.astype(jnp.bfloat16)
                        field_ref[k, 1, :, where] = imag.astype(jnp.bfloat16)
                        term = real * real + imag * imag
                        energy = term if energy is None else energy + term
                    total_ref[:, where] += energy

            section(0, 0)
            total_ref[...] = jnp.zeros_like(total_ref)

            def forward(i, carry):
                k = 2 * i
                field((k,), (0,))
                section(k + 1, 1)
                field((k + 1,), (1,))
                section(jnp.minimum(k + 2, kernels - 1), 0)
                return carry

            lax.fori_loop(0, kernels // 2, forward, 0)

            def slopes(ref):
                for where in halves:
                    level = jnp.tanh(total_ref[:, where] - 0.5 * steepness * threshold_level)
                    excess = 0.5 * level + 0.5 - ref[:, where].astype(jnp.float32)
                    slope_ref[:, where] = (excess * (1.0 - level * level)).astype(jnp.bfloat16)

            @pl.when(item == 0)
            def _():
                slopes(goal_ref)

            @pl.when(item > 0)
            def _():
                slopes(other_ref)

            def back(k, buf):
                for where in halves:
                    for part in range(2):
                        cotangent = slope_ref[:, where] * field_ref[k, part, :, where]
                        place = slice(part * 2 * rows, (part + 1) * 2 * rows)
                        back_ref[buf, place, where] = dot(row_ref[:, inner], cotangent).astype(
                            jnp.bfloat16
                        )

            def adjoint(k, buf):
                wave = dot(back_ref[buf], col_t_ref[inner])
                rcc, rcs = wave[:rows, :lanes], wave[:rows, lanes:]
                rsc, rss = wave[rows : 2 * rows, :lanes], wave[rows : 2 * rows, lanes:]
                icc, ics = wave[2 * rows : 3 * rows, :lanes], wave[2 * rows : 3 * rows, lanes:]
                isc, iss = wave[3 * rows :, :lanes], wave[3 * rows :, lanes:]
                ur, ui, vr, vi = rcc - rss, icc - iss, rsc + rcs, isc + ics
                pr, pi, mr, mi = (pupil(k, index) for index in range(4))
                ans_ref[0] += pr * ur + pi * ui + mr * vi - mi * vr
                ans_ref[1] += mr * ui - mi * ur - pr * vr - pi * vi
                ur, ui, vr, vi = rcc + rss, icc + iss, rsc - rcs, isc - ics
                pr, pi, mr, mi = (pupil(k, index) for index in range(4, 8))
                ans_ref[2] += pr * ur + pi * ui + mr * vi - mi * vr
                ans_ref[3] += mr * ui - mi * ur - pr * vr - pi * vi

            ans_ref[...] = jnp.zeros_like(ans_ref)
            back(0, 0)

            def backward(i, carry):
                k = 2 * i
                adjoint(k, 0)
                back(k + 1, 1)
                adjoint(k + 1, 1)
                back(jnp.minimum(k + 2, kernels - 1), 0)
                return carry

            lax.fori_loop(0, kernels // 2, backward, 0)

            def answer(first):
                left, right = slice(first, first + lanes), slice(first + lanes, first + 2 * lanes)
                out_ref[:rows, left] = (ans_ref[0] + ans_ref[2]).astype(jnp.bfloat16)
                out_ref[:rows, right] = (ans_ref[3] - ans_ref[1]).astype(jnp.bfloat16)
                out_ref[rows:, left] = (-(ans_ref[1] + ans_ref[3])).astype(jnp.bfloat16)
                out_ref[rows:, right] = (ans_ref[2] - ans_ref[0]).astype(jnp.bfloat16)

            @pl.when(item == 0)
            def _():
                answer(0)

            @pl.when(item > 0)
            def _():
                answer(2 * lanes)

        return carry

    lax.fori_loop(0, 2, work, 0)


def returned_kernel(tile, mine_ref, sent_ref, row_t_ref, col_ref, out_ref, near_ref, cross_ref, sum_ref):
    width = out_ref.shape[1]
    extent = row_t_ref.shape[0]
    lanes = mine_ref.shape[1] // 2
    place = lax.axis_index("col")
    before, after = mine_ref[:, lanes:], sent_ref[:, :lanes]
    before = jnp.where(place == 0, jnp.zeros_like(before), before)
    after = jnp.where(place == lax.axis_size("col") - 1, jnp.zeros_like(after), after)
    sum_ref[...] = jnp.zeros_like(sum_ref)
    for place, value in zip(range(-1, 3), (before, mine_ref[:, :lanes], sent_ref[:, lanes:], after)):
        start = place * tile - AMBIT
        low, high = max(0, start), min(width, start + extent)
        sum_ref[:, low:high] += dot(value, col_ref[:, low - start : high - start])
    mixed = sum_ref[...].astype(jnp.bfloat16)
    out_ref[...] = mixed
    for start, rim_ref in zip(sides(extent - AMBIT), (near_ref, cross_ref)):
        rim_ref[...] = dot(row_t_ref[pl.ds(start, AMBIT)], mixed).astype(jnp.bfloat16)


def update_kernel(mask_ref, mixed_ref, row_t_ref, out_ref, rims_ref, stage_ref, sems):
    tile = mask_ref.shape[0]
    copy = pltpu.make_async_copy(mask_ref, stage_ref, sems.at[0])
    copy.start()
    copy.wait()
    stage_ref[...] = stage_ref[...] - step_rate * dot(
        row_t_ref[AMBIT : AMBIT + tile], mixed_ref[...]
    )
    inner = pl.ds(AMBIT, tile - 2 * AMBIT)
    copy = pltpu.make_async_copy(stage_ref.at[inner], out_ref.at[inner], sems.at[1])
    copy.start()
    rims_ref[:AMBIT] = stage_ref[:AMBIT]
    rims_ref[AMBIT:] = stage_ref[tile - AMBIT :]
    copy.wait()


def rims_kernel(near_ref, cross_ref, rims_ref, base_ref, out_ref, stage_ref, sems):
    tile = out_ref.shape[0]
    copies = []
    places = zip((cross_ref, near_ref), sides(AMBIT)[::-1], sides(tile - AMBIT)[::-1])
    for index, (rim_ref, place, start) in enumerate(places):
        stage_ref[index] = rims_ref[pl.ds(place, AMBIT)] - step_rate * rim_ref[...].astype(
            jnp.float32
        )
        copy = pltpu.make_async_copy(
            stage_ref.at[index], out_ref.at[pl.ds(start, AMBIT)], sems.at[index]
        )
        copy.start()
        copies.append(copy)
    for copy in copies:
        copy.wait()


def body(mask, target, live, pupils, weights):
    tile, width = mask.shape
    kernels, size = pupils.shape[1], pupils.shape[2]
    half = size // 2
    rows, lanes = round_up(half + 1, 16), round_up(half + 2, LANE)
    extent = tile + 2 * AMBIT
    row_np = half_tables(half, rows, extent)
    col_np = half_tables(half, lanes, extent)
    row_pick, col_pick = (
        jnp.asarray(pick, jnp.bfloat16) for pick in pick_tables(half, rows, lanes)
    )
    row_table, row_table_t = jnp.asarray(row_np, jnp.bfloat16), jnp.asarray(row_np.T, jnp.bfloat16)
    col_table, col_table_t = jnp.asarray(col_np, jnp.bfloat16), jnp.asarray(col_np.T, jnp.bfloat16)
    bf16, f32 = jnp.bfloat16, jnp.float32
    shape = jax.ShapeDtypeStruct
    smem = pl.BlockSpec(memory_space=pltpu.SMEM)
    early = kernels // 2

    hbm = pl.BlockSpec(memory_space=pltpu.HBM)
    dma = pltpu.SemaphoreType.DMA
    edge = shape((AMBIT, width), bf16)
    near, cross, goal = call(
        edges_kernel,
        (edge, edge, shape((tile, tile), bf16)),
        [hbm, hbm],
        scratch=[pltpu.VMEM((2, AMBIT, width), f32), dma((3,))],
        limit=52,
    )(mask, target)
    other_goal = turned(goal, "col", 1)
    cross = swapped(cross, "row", 1)
    near = swapped(near, "row", 0)
    middle, quads = call(
        partial(early_kernel, rows, lanes, early),
        (shape((2 * rows, width), f32), shape((early, 8, rows, lanes), bf16)),
        [hbm, hbm, *vmem(1), smem, *vmem(2)],
        scratch=[
            pltpu.VMEM((tile, width), f32), pltpu.VMEM((2, early, size, size), f32), dma((2,)),
        ],
        limit=50,
        us=4,
    )(mask, pupils, row_table, weights, row_pick, col_pick)
    own, low, sending = call(
        partial_kernel,
        (
            shape((2 * rows, tile + AMBIT), bf16),
            shape((2 * rows, AMBIT), bf16),
            shape((2 * rows, AMBIT + 2 * lanes), bf16),
        ),
        [smem, *vmem(5)],
    )(live, middle, near, cross, row_table, col_table_t)
    sent = turned(sending, "col", 1)
    base, all_quads = call(
        partial(late_kernel, rows, lanes, early, kernels),
        (shape((2 * rows, 2 * lanes), f32), shape((kernels, 8, rows, lanes), bf16)),
        [hbm, *vmem(3), smem, *vmem(2)],
        scratch=[pltpu.VMEM((2, kernels - early, size, size), f32), dma],
        limit=48,
        us=4,
    )(pupils, own, col_table_t, quads, weights, row_pick, col_pick)
    answers = call(
        partial(core_kernel, rows, lanes),
        shape((2 * rows, 4 * lanes), bf16),
        [smem, *vmem(10)],
        scratch=[
            pltpu.VMEM((2, 2 * rows, 2 * lanes), f32),
            pltpu.VMEM((2, 4 * rows, 2 * lanes), bf16),
            pltpu.VMEM((2, 4 * rows, tile), bf16),
            pltpu.VMEM((kernels, 2, tile, tile), bf16),
            pltpu.VMEM((tile, tile), f32),
            pltpu.VMEM((tile, tile), bf16),
            pltpu.VMEM((2, 4 * rows, tile), bf16),
            pltpu.VMEM((4, rows, lanes), f32),
            pltpu.VMEM((4, rows, lanes), f32),
        ],
        limit=36,
        us=15,
    )(
        live, base, sent, low, target, other_goal, all_quads,
        row_table, row_table_t, col_table, col_table_t,
    )
    returned = turned(answers, "col", -1)
    mixed, near, cross = call(
        partial(returned_kernel, tile),
        (shape((2 * rows, width), bf16), shape((AMBIT, width), bf16), shape((AMBIT, width), bf16)),
        vmem(4),
        scratch=[pltpu.VMEM((2 * rows, width), f32)],
    )(answers, returned, row_table_t, col_table)
    cross = swapped(cross, "row", 1)
    near = swapped(near, "row", 0)
    anywhere = pl.BlockSpec(memory_space=pl.ANY)
    whole, rims = shape((tile, width), f32), shape((2 * AMBIT, width), f32)
    updated, edges = pl.pallas_call(
        update_kernel,
        out_shape=(whole, rims),
        in_specs=[hbm, *vmem(2)],
        out_specs=(anywhere, *vmem(1)),
        scratch_shapes=[pltpu.VMEM((tile, width), f32), dma((2,))],
        cost_estimate=pl.CostEstimate(flops=10**9, bytes_accessed=2 * 10**6, transcendentals=0),
        compiler_params=pltpu.CompilerParams(vmem_limit_bytes=16 * MIB),
    )(mask, mixed, row_table_t)
    return pl.pallas_call(
        rims_kernel,
        out_shape=whole,
        in_specs=[*vmem(3), anywhere],
        out_specs=anywhere,
        scratch_shapes=[pltpu.VMEM((2, AMBIT, width), f32), pltpu.SemaphoreType.DMA((2,))],
        input_output_aliases={3: 0},
        compiler_params=pltpu.CompilerParams(vmem_limit_bytes=8 * MIB),
    )(near, cross, edges, updated)


def solution(mesh):
    placed = (P("row", "col"), P("row", "col"), P("row", "col"), P(), P())
    return jax.shard_map(
        body, mesh=mesh, in_specs=placed, out_specs=P("row", "col"), check_vma=False
    )
```

```python
from functools import partial
import math

import jax
import jax.numpy as jnp
import numpy as np
from jax import lax
from jax.experimental import pallas as pl
from jax.experimental.pallas import tpu as pltpu
from jax.sharding import PartitionSpec as P


AMBIT = 128
LANE = 128

steepness = 4.0
threshold_level = 1.0
step_rate = 8.0

MIB = 1024 * 1024


def round_up(value, unit):
    return -(-value // unit) * unit


def swapped(block, axis, offset):
    count = lax.axis_size(axis)
    pairs = []
    for low in range(offset, count - 1, 2):
        pairs += [(low, low + 1), (low + 1, low)]
    return lax.ppermute(block, axis, pairs)


def sides(reach):
    odd = lax.rem(lax.axis_index("row"), 2)
    return [pl.multiple_of(side * reach, AMBIT) for side in (1 - odd, odd)]


def turned(block, axis, step):
    count = lax.axis_size(axis)
    return lax.ppermute(block, axis, [(i, (i + step) % count) for i in range(count)])


def dot(leading, trailing):
    return jnp.dot(leading, trailing, preferred_element_type=jnp.float32)


def half_tables(half, rows, extent):
    frequency = np.arange(half + 1, dtype=np.int64)
    pixels = np.arange(extent, dtype=np.int64)
    phases = np.mod(frequency[:, None] * pixels[None, :], extent).astype(np.float32)
    angles = phases * np.float32(2.0 * math.pi / extent)
    factor = np.float32(1.0 / math.sqrt(extent))
    table = np.zeros((2 * rows, extent), np.float32)
    table[: half + 1] = np.cos(angles) * factor
    table[rows : rows + half + 1] = np.sin(angles) * factor
    return table


def pick_tables(half, rows, lanes):
    size = 2 * half
    row_pick = np.zeros((2 * rows, size), np.float32)
    col_pick = np.zeros((size, 2 * lanes), np.float32)
    for index in range(half):
        row_pick[index, half + index] = 1.0
        col_pick[half + index, index] = 1.0
        row_pick[rows + half - index, index] = 1.0
        col_pick[index, lanes + half - index] = 1.0
    return row_pick, col_pick


def vmem(count):
    return [pl.BlockSpec(memory_space=pltpu.VMEM)] * count


def call(kernel, outs, specs, scratch=(), limit=16, us=1, **kwargs):
    return pl.pallas_call(
        kernel,
        out_shape=outs,
        in_specs=specs,
        out_specs=jax.tree.map(lambda _: pl.BlockSpec(memory_space=pltpu.VMEM), outs),
        scratch_shapes=list(scratch),
        cost_estimate=pl.CostEstimate(
            flops=int(us * 5e8), bytes_accessed=int(us * 1e6), transcendentals=0
        ),
        compiler_params=pltpu.CompilerParams(vmem_limit_bytes=limit * MIB),
        **kwargs,
    )


def pupil_steps(rows, lanes, first, last, pupils_ref, weights_ref, row_ref, col_ref, out_ref):
    for k in range(first, last):
        scale = jnp.sqrt(jnp.full((1, 1), weights_ref[k] * (0.5 * steepness), jnp.float32))
        for part in range(2):
            values = (pupils_ref[part, k - first] * scale).astype(jnp.bfloat16)
            columns = dot(values, col_ref[...]).astype(jnp.bfloat16)
            full = dot(row_ref[...], columns)
            pos_pos, pos_neg = full[:rows, :lanes], full[:rows, lanes:]
            neg_pos, neg_neg = full[rows:, :lanes], full[rows:, lanes:]
            out_ref[k, 0 + part] = (pos_pos + neg_neg).astype(jnp.bfloat16)
            out_ref[k, 2 + part] = (pos_pos - neg_neg).astype(jnp.bfloat16)
            out_ref[k, 4 + part] = (pos_neg + neg_pos).astype(jnp.bfloat16)
            out_ref[k, 6 + part] = (pos_neg - neg_pos).astype(jnp.bfloat16)


def edges_kernel(mask_ref, target_ref, near_ref, cross_ref, goal_ref, stage_ref, sems):
    tile = mask_ref.shape[0]
    whole = pltpu.make_async_copy(target_ref.at[:, tile:], goal_ref, sems.at[2])
    copies = []
    for index, start in enumerate(sides(tile - AMBIT)):
        copy = pltpu.make_async_copy(
            mask_ref.at[pl.ds(start, AMBIT)], stage_ref.at[index], sems.at[index]
        )
        copy.start()
        copies.append(copy)
    whole.start()
    for index, out_ref in enumerate((near_ref, cross_ref)):
        copies[index].wait()
        out_ref[...] = stage_ref[index].astype(jnp.bfloat16)
    whole.wait()


def early_kernel(
    rows, lanes, count, mask_ref, pupils_ref, table_ref, weights_ref, row_ref, col_ref,
    mid_ref, out_ref, rest_ref, pupil_stage, sems,
):
    tile = mask_ref.shape[0]
    pupil_copy = pltpu.make_async_copy(pupils_ref.at[:, pl.ds(0, count)], pupil_stage, sems.at[0])
    pupil_copy.start()
    rest = pupils_ref.shape[1] - count
    rest_copy = pltpu.make_async_copy(pupils_ref.at[:, pl.ds(count, rest)], rest_ref, sems.at[1])
    rest_copy.start()
    mid_ref[...] = dot(
        table_ref[:, AMBIT : AMBIT + tile], mask_ref[...].astype(jnp.bfloat16)
    )
    pupil_copy.wait()
    pupil_steps(rows, lanes, 0, count, pupil_stage, weights_ref, row_ref, col_ref, out_ref)
    rest_copy.wait()


def partial_kernel(
    live_ref, mid_ref, near_ref, cross_ref, table_ref, col_t_ref, own_ref, low_ref, sent_ref
):
    extent = table_ref.shape[1]
    width = mid_ref.shape[1]
    tile = extent - 2 * AMBIT
    total = mid_ref[...]
    for start, rim_ref in zip(sides(extent - AMBIT), (near_ref, cross_ref)):
        total = total + dot(table_ref[:, pl.ds(start, AMBIT)], rim_ref[...])
    total = total.astype(jnp.bfloat16)
    own_ref[...] = total[:, : tile + AMBIT]
    low_ref[...] = total[:, :AMBIT]
    sent_ref[:, :AMBIT] = total[:, width - AMBIT :]
    main = dot(total[:, tile - AMBIT :], col_t_ref[: tile + AMBIT])
    shape = main.shape
    flag = (lax.broadcasted_iota(jnp.int32, shape, 0) == shape[0] - 1) & (
        lax.broadcasted_iota(jnp.int32, shape, 1) == shape[1] - 1
    )
    live = live_ref[0, live_ref.shape[1] - 1].astype(jnp.float32)
    sent_ref[:, AMBIT:] = jnp.where(flag, live, main).astype(jnp.bfloat16)


def late_kernel(
    rows, lanes, first, last, pupils_ref, own_ref, col_t_ref, quads_ref, weights_ref, row_ref, col_ref,
    base_ref, out_ref,
):
    out_ref[:first] = quads_ref[...]
    base_ref[...] = dot(own_ref[...], col_t_ref[AMBIT:])
    pupil_steps(rows, lanes, first, last, pupils_ref, weights_ref, row_ref, col_ref, out_ref)


def in_groups(count, group, run):
    def one(index, carry):
        run(index * group, False)
        return carry

    if count > group:
        lax.fori_loop(0, count // group - 1, one, 0)
    run(count - group, True)


def core_kernel(
    rows,
    lanes,
    live_ref,
    base_ref,
    sent_ref,
    low_ref,
    goal_ref,
    other_ref,
    pupil_ref,
    row_ref,
    row_t_ref,
    col_ref,
    col_t_ref,
    out_ref,
    spec_ref,
    amp_ref,
    sec_ref,
    field_ref,
    total_ref,
    slope_ref,
    back_ref,
    sum_ref,
    ans_ref,
):
    tile = goal_ref.shape[0]
    extent = row_ref.shape[1]
    kernels = pupil_ref.shape[0]
    halves = [slice(start, start + 2 * LANE) for start in range(0, tile, 2 * LANE)]
    inner = slice(AMBIT, AMBIT + tile)
    outer = lax.axis_index("col") == 0
    left = sent_ref[:, :AMBIT]
    left = jnp.where(outer, jnp.zeros_like(left), left)
    spec_ref[0] = base_ref[...] + dot(left, col_t_ref[:AMBIT])
    right = low_ref[...]
    right = jnp.where(outer, jnp.zeros_like(right), right)
    spec_ref[1] = sent_ref[:, AMBIT:].astype(jnp.float32) + dot(right, col_t_ref[extent - AMBIT :])
    corner = sent_ref[2 * rows - 16 :, AMBIT + 2 * lanes - LANE :].astype(jnp.float32)
    other_live = jnp.max(corner[15:, LANE - 1 :])
    out_ref[...] = jnp.zeros_like(out_ref)

    def work(item, carry):
        live = jnp.where(item == 0, live_ref[0, 0].astype(jnp.float32), other_live) > 0.0

        @pl.when(live)
        def _():
            spec = spec_ref[item]
            cc, cs = spec[:rows, :lanes], spec[:rows, lanes:]
            sc, ss = spec[rows:, :lanes], spec[rows:, lanes:]
            sum_ref[0] = cc - ss
            sum_ref[1] = sc + cs
            sum_ref[2] = cc + ss
            sum_ref[3] = sc - cs

            def pupil(k, index):
                return pupil_ref[k, index].astype(jnp.float32)

            def section(k, buf):
                u, v, m, n = sum_ref[0], sum_ref[1], sum_ref[2], sum_ref[3]
                pr, pi, mr, mi = (pupil(k, index) for index in range(4))
                big_re = pr * u + mi * v
                big_im = pi * u - mr * v
                small_re = mr * u + pi * v
                small_im = mi * u - pr * v
                pr, pi, mr, mi = (pupil(k, index) for index in range(4, 8))
                big_re2 = pr * m + mi * n
                big_im2 = pi * m - mr * n
                small_re2 = mr * m + pi * n
                small_im2 = mi * m - pr * n

                def pair(place, left, right):
                    where = slice(place * rows, (place + 1) * rows)
                    amp_ref[buf, where, :lanes] = left.astype(jnp.bfloat16)
                    amp_ref[buf, where, lanes:] = right.astype(jnp.bfloat16)

                pair(0, big_re + big_re2, small_im2 - small_im)
                pair(1, -(small_im + small_im2), big_re2 - big_re)
                pair(2, big_im + big_im2, small_re - small_re2)
                pair(3, small_re + small_re2, big_im2 - big_im)
                sec_ref[buf] = dot(amp_ref[buf], col_ref[:, inner]).astype(jnp.bfloat16)

            def field(ks, bufs):
                for where in halves:
                    energy = None
                    for k, buf in zip(ks, bufs):
                        real = dot(row_t_ref[inner], sec_ref[buf, : 2 * rows, where])
                        imag = dot(row_t_ref[inner], sec_ref[buf, 2 * rows :, where])
                        field_ref[k, 0, :, where] = real.astype(jnp.bfloat16)
                        field_ref[k, 1, :, where] = imag.astype(jnp.bfloat16)
                        term = real * real + imag * imag
                        energy = term if energy is None else energy + term
                    total_ref[:, where] += energy

            section(0, 0)
            section(1, 1)
            total_ref[...] = jnp.zeros_like(total_ref)

            def forward(first, last_group):
                for step in range(0, 4, 2):
                    bufs, nexts = (0, 1), (2, 3)
                    if step:
                        bufs, nexts = nexts, bufs
                    k = first + step
                    more = step == 0 or not last_group
                    field((k, k + 1), bufs)
                    if more:
                        section(k + 2, nexts[0])
                        section(k + 3, nexts[1])

            in_groups(kernels, 4, forward)

            def back(ks, bufs):
                for where in halves:
                    for k, buf in zip(ks, bufs):
                        for part in range(2):
                            cotangent = slope_ref[:, where] * field_ref[k, part, :, where]
                            place = slice(part * 2 * rows, (part + 1) * 2 * rows)
                            back_ref[buf, place, where] = dot(
                                row_ref[:, inner], cotangent
                            ).astype(jnp.bfloat16)

            def adjoint(k, buf):
                wave = dot(back_ref[buf], col_t_ref[inner])
                rcc, rcs = wave[:rows, :lanes], wave[:rows, lanes:]
                rsc, rss = wave[rows : 2 * rows, :lanes], wave[rows : 2 * rows, lanes:]
                icc, ics = wave[2 * rows : 3 * rows, :lanes], wave[2 * rows : 3 * rows, lanes:]
                isc, iss = wave[3 * rows :, :lanes], wave[3 * rows :, lanes:]
                ur, ui, vr, vi = rcc - rss, icc - iss, rsc + rcs, isc + ics
                pr, pi, mr, mi = (pupil(k, index) for index in range(4))
                ans_ref[0] += pr * ur + pi * ui + mr * vi - mi * vr
                ans_ref[1] += mr * ui - mi * ur - pr * vr - pi * vi
                ur, ui, vr, vi = rcc + rss, icc + iss, rsc - rcs, isc - ics
                pr, pi, mr, mi = (pupil(k, index) for index in range(4, 8))
                ans_ref[2] += pr * ur + pi * ui + mr * vi - mi * vr
                ans_ref[3] += mr * ui - mi * ur - pr * vr - pi * vi

            ans_ref[...] = jnp.zeros_like(ans_ref)

            def slopes(ref):
                for where in halves:
                    level = jnp.tanh(total_ref[:, where] - 0.5 * steepness * threshold_level)
                    excess = 0.5 * level + 0.5 - ref[:, where].astype(jnp.float32)
                    slope_ref[:, where] = (excess * (1.0 - level * level)).astype(jnp.bfloat16)
                back((0, 1), (0, 1))

            @pl.when(item == 0)
            def _():
                slopes(goal_ref)

            @pl.when(item > 0)
            def _():
                slopes(other_ref)

            def backward(first, last_group):
                for step in range(0, 4, 2):
                    bufs, nexts = (0, 1), (2, 3)
                    if step:
                        bufs, nexts = nexts, bufs
                    k = first + step
                    adjoint(k, bufs[0])
                    adjoint(k + 1, bufs[1])
                    if step == 0 or not last_group:
                        back((k + 2, k + 3), nexts)

            in_groups(kernels, 4, backward)

            def answer(first):
                left, right = slice(first, first + lanes), slice(first + lanes, first + 2 * lanes)
                out_ref[:rows, left] = (ans_ref[0] + ans_ref[2]).astype(jnp.bfloat16)
                out_ref[:rows, right] = (ans_ref[3] - ans_ref[1]).astype(jnp.bfloat16)
                out_ref[rows:, left] = (-(ans_ref[1] + ans_ref[3])).astype(jnp.bfloat16)
                out_ref[rows:, right] = (ans_ref[2] - ans_ref[0]).astype(jnp.bfloat16)

            @pl.when(item == 0)
            def _():
                answer(0)

            @pl.when(item > 0)
            def _():
                answer(2 * lanes)

        return carry

    lax.fori_loop(0, 2, work, 0)


def returned_kernel(tile, mine_ref, sent_ref, row_t_ref, col_ref, out_ref, near_ref, cross_ref, sum_ref):
    width = out_ref.shape[1]
    extent = row_t_ref.shape[0]
    lanes = mine_ref.shape[1] // 2
    place = lax.axis_index("col")
    before, after = mine_ref[:, lanes:], sent_ref[:, :lanes]
    before = jnp.where(place == 0, jnp.zeros_like(before), before)
    after = jnp.where(place == lax.axis_size("col") - 1, jnp.zeros_like(after), after)
    sum_ref[...] = jnp.zeros_like(sum_ref)
    for place, value in zip(range(-1, 3), (before, mine_ref[:, :lanes], sent_ref[:, lanes:], after)):
        start = place * tile - AMBIT
        low, high = max(0, start), min(width, start + extent)
        sum_ref[:, low:high] += dot(value, col_ref[:, low - start : high - start])
    mixed = sum_ref[...].astype(jnp.bfloat16)
    out_ref[...] = mixed
    for start, rim_ref in zip(sides(extent - AMBIT), (near_ref, cross_ref)):
        rim_ref[...] = dot(row_t_ref[pl.ds(start, AMBIT)], mixed).astype(jnp.bfloat16)


def update_kernel(mask_ref, mixed_ref, row_t_ref, out_ref, rims_ref, stage_ref, sem):
    tile = mask_ref.shape[0]
    stage_ref[...] = mask_ref[...] - step_rate * dot(
        row_t_ref[AMBIT : AMBIT + tile], mixed_ref[...]
    )
    inner = pl.ds(AMBIT, tile - 2 * AMBIT)
    copy = pltpu.make_async_copy(stage_ref.at[inner], out_ref.at[inner], sem)
    copy.start()
    rims_ref[:AMBIT] = stage_ref[:AMBIT]
    rims_ref[AMBIT:] = stage_ref[tile - AMBIT :]
    copy.wait()


def rims_kernel(near_ref, cross_ref, rims_ref, base_ref, out_ref, stage_ref, sems):
    tile = out_ref.shape[0]
    copies = []
    places = zip((cross_ref, near_ref), sides(AMBIT)[::-1], sides(tile - AMBIT)[::-1])
    for index, (rim_ref, place, start) in enumerate(places):
        stage_ref[index] = rims_ref[pl.ds(place, AMBIT)] - step_rate * rim_ref[...].astype(
            jnp.float32
        )
        copy = pltpu.make_async_copy(
            stage_ref.at[index], out_ref.at[pl.ds(start, AMBIT)], sems.at[index]
        )
        copy.start()
        copies.append(copy)
    for copy in copies:
        copy.wait()


def body(mask, target, live, pupils, weights):
    tile, width = mask.shape
    kernels, size = pupils.shape[1], pupils.shape[2]
    half = size // 2
    rows, lanes = round_up(half + 1, 16), round_up(half + 2, LANE)
    extent = tile + 2 * AMBIT
    row_np = half_tables(half, rows, extent)
    col_np = half_tables(half, lanes, extent)
    row_pick, col_pick = (
        jnp.asarray(pick, jnp.bfloat16) for pick in pick_tables(half, rows, lanes)
    )
    row_table, row_table_t = jnp.asarray(row_np, jnp.bfloat16), jnp.asarray(row_np.T, jnp.bfloat16)
    col_table, col_table_t = jnp.asarray(col_np, jnp.bfloat16), jnp.asarray(col_np.T, jnp.bfloat16)
    bf16, f32 = jnp.bfloat16, jnp.float32
    shape = jax.ShapeDtypeStruct
    smem = pl.BlockSpec(memory_space=pltpu.SMEM)
    early = kernels // 2

    hbm = pl.BlockSpec(memory_space=pltpu.HBM)
    dma = pltpu.SemaphoreType.DMA
    edge = shape((AMBIT, width), bf16)
    near, cross, goal = call(
        edges_kernel,
        (edge, edge, shape((tile, tile), bf16)),
        [hbm, hbm],
        scratch=[pltpu.VMEM((2, AMBIT, width), f32), dma((3,))],
        limit=52,
    )(mask, target)
    other_goal = turned(goal, "col", 1)
    cross = swapped(cross, "row", 1)
    near = swapped(near, "row", 0)
    middle, quads, rest = call(
        partial(early_kernel, rows, lanes, early),
        (
            shape((2 * rows, width), f32),
            shape((early, 8, rows, lanes), bf16),
            shape((2, kernels - early, size, size), f32),
        ),
        [*vmem(1), hbm, *vmem(1), smem, *vmem(2)],
        scratch=[pltpu.VMEM((2, early, size, size), f32), dma((2,))],
        limit=48,
        us=4,
    )(mask, pupils, row_table, weights, row_pick, col_pick)
    own, low, sending = call(
        partial_kernel,
        (
            shape((2 * rows, tile + AMBIT), bf16),
            shape((2 * rows, AMBIT), bf16),
            shape((2 * rows, AMBIT + 2 * lanes), bf16),
        ),
        [smem, *vmem(5)],
    )(live, middle, near, cross, row_table, col_table_t)
    sent = turned(sending, "col", 1)
    base, all_quads = call(
        partial(late_kernel, rows, lanes, early, kernels),
        (shape((2 * rows, 2 * lanes), f32), shape((kernels, 8, rows, lanes), bf16)),
        [*vmem(4), smem, *vmem(2)],
        limit=16,
        us=4,
    )(rest, own, col_table_t, quads, weights, row_pick, col_pick)
    answers = call(
        partial(core_kernel, rows, lanes),
        shape((2 * rows, 4 * lanes), bf16),
        [smem, *vmem(10)],
        scratch=[
            pltpu.VMEM((2, 2 * rows, 2 * lanes), f32),
            pltpu.VMEM((4, 4 * rows, 2 * lanes), bf16),
            pltpu.VMEM((4, 4 * rows, tile), bf16),
            pltpu.VMEM((kernels, 2, tile, tile), bf16),
            pltpu.VMEM((tile, tile), f32),
            pltpu.VMEM((tile, tile), bf16),
            pltpu.VMEM((4, 4 * rows, tile), bf16),
            pltpu.VMEM((4, rows, lanes), f32),
            pltpu.VMEM((4, rows, lanes), f32),
        ],
        limit=36,
        us=15,
    )(
        live, base, sent, low, target, other_goal, all_quads,
        row_table, row_table_t, col_table, col_table_t,
    )
    returned = turned(answers, "col", -1)
    mixed, near, cross = call(
        partial(returned_kernel, tile),
        (shape((2 * rows, width), bf16), shape((AMBIT, width), bf16), shape((AMBIT, width), bf16)),
        vmem(4),
        scratch=[pltpu.VMEM((2 * rows, width), f32)],
    )(answers, returned, row_table_t, col_table)
    cross = swapped(cross, "row", 1)
    near = swapped(near, "row", 0)
    anywhere = pl.BlockSpec(memory_space=pl.ANY)
    whole, rims = shape((tile, width), f32), shape((2 * AMBIT, width), f32)
    updated, edges = pl.pallas_call(
        update_kernel,
        out_shape=(whole, rims),
        in_specs=vmem(3),
        out_specs=(anywhere, *vmem(1)),
        scratch_shapes=[pltpu.VMEM((tile, width), f32), dma],
        cost_estimate=pl.CostEstimate(flops=10**9, bytes_accessed=2 * 10**6, transcendentals=0),
        compiler_params=pltpu.CompilerParams(vmem_limit_bytes=16 * MIB),
    )(mask, mixed, row_table_t)
    return pl.pallas_call(
        rims_kernel,
        out_shape=whole,
        in_specs=[*vmem(3), anywhere],
        out_specs=anywhere,
        scratch_shapes=[pltpu.VMEM((2, AMBIT, width), f32), pltpu.SemaphoreType.DMA((2,))],
        input_output_aliases={3: 0},
        compiler_params=pltpu.CompilerParams(vmem_limit_bytes=8 * MIB),
    )(near, cross, edges, updated)


def solution(mesh):
    placed = (P("row", "col"), P("row", "col"), P("row", "col"), P(), P())
    return jax.shard_map(
        body, mesh=mesh, in_specs=placed, out_specs=P("row", "col"), check_vma=False
    )
```

```python
from functools import partial
import math

import jax
import jax.numpy as jnp
import numpy as np
from jax import lax
from jax.experimental import pallas as pl
from jax.experimental.pallas import tpu as pltpu
from jax.sharding import PartitionSpec as P


AMBIT = 128
LANE = 128

steepness = 4.0
threshold_level = 1.0
step_rate = 8.0

MIB = 1024 * 1024


def round_up(value, unit):
    return -(-value // unit) * unit


def swapped(block, axis, offset):
    count = lax.axis_size(axis)
    pairs = []
    for low in range(offset, count - 1, 2):
        pairs += [(low, low + 1), (low + 1, low)]
    return lax.ppermute(block, axis, pairs)


def sides(reach):
    odd = lax.rem(lax.axis_index("row"), 2)
    return [pl.multiple_of(side * reach, AMBIT) for side in (1 - odd, odd)]


def col_parity():
    return lax.rem(lax.axis_index("col"), 2)


def dot(leading, trailing):
    return jnp.dot(leading, trailing, preferred_element_type=jnp.float32)


def half_tables(half, rows, extent):
    frequency = np.arange(half + 1, dtype=np.int64)
    pixels = np.arange(extent, dtype=np.int64)
    phases = np.mod(frequency[:, None] * pixels[None, :], extent).astype(np.float32)
    angles = phases * np.float32(2.0 * math.pi / extent)
    factor = np.float32(1.0 / math.sqrt(extent))
    table = np.zeros((2 * rows, extent), np.float32)
    table[: half + 1] = np.cos(angles) * factor
    table[rows : rows + half + 1] = np.sin(angles) * factor
    return table


def pick_tables(half, rows, lanes):
    size = 2 * half
    row_pick = np.zeros((2 * rows, size), np.float32)
    col_pick = np.zeros((size, 2 * lanes), np.float32)
    for index in range(half):
        row_pick[index, half + index] = 1.0
        col_pick[half + index, index] = 1.0
        row_pick[rows + half - index, index] = 1.0
        col_pick[index, lanes + half - index] = 1.0
    return row_pick, col_pick


def vmem(count):
    return [pl.BlockSpec(memory_space=pltpu.VMEM)] * count


def call(kernel, outs, specs, scratch=(), limit=16, us=1, **kwargs):
    return pl.pallas_call(
        kernel,
        out_shape=outs,
        in_specs=specs,
        out_specs=jax.tree.map(lambda _: pl.BlockSpec(memory_space=pltpu.VMEM), outs),
        scratch_shapes=list(scratch),
        cost_estimate=pl.CostEstimate(
            flops=int(us * 5e8), bytes_accessed=int(us * 1e6), transcendentals=0
        ),
        compiler_params=pltpu.CompilerParams(vmem_limit_bytes=limit * MIB),
        **kwargs,
    )


def pupil_steps(rows, lanes, first, last, pupils_ref, weights_ref, row_ref, col_ref, out_ref):
    for k in range(first, last):
        scale = jnp.sqrt(jnp.full((1, 1), weights_ref[k] * (0.5 * steepness), jnp.float32))
        for part in range(2):
            values = (pupils_ref[part, k - first] * scale).astype(jnp.bfloat16)
            columns = dot(values, col_ref[...]).astype(jnp.bfloat16)
            full = dot(row_ref[...], columns)
            pos_pos, pos_neg = full[:rows, :lanes], full[:rows, lanes:]
            neg_pos, neg_neg = full[rows:, :lanes], full[rows:, lanes:]
            out_ref[k, 0 + part] = (pos_pos + neg_neg).astype(jnp.bfloat16)
            out_ref[k, 2 + part] = (pos_pos - neg_neg).astype(jnp.bfloat16)
            out_ref[k, 4 + part] = (pos_neg + neg_pos).astype(jnp.bfloat16)
            out_ref[k, 6 + part] = (pos_neg - neg_pos).astype(jnp.bfloat16)


def edges_kernel(mask_ref, target_ref, near_ref, cross_ref, goal_ref, stage_ref, sems):
    tile = mask_ref.shape[0]
    far = pl.multiple_of((1 - col_parity()) * tile, LANE)
    whole = pltpu.make_async_copy(target_ref.at[:, pl.ds(far, tile)], goal_ref, sems.at[2])
    copies = []
    for index, start in enumerate(sides(tile - AMBIT)):
        copy = pltpu.make_async_copy(
            mask_ref.at[pl.ds(start, AMBIT)], stage_ref.at[index], sems.at[index]
        )
        copy.start()
        copies.append(copy)
    whole.start()
    for index, out_ref in enumerate((near_ref, cross_ref)):
        copies[index].wait()
        out_ref[...] = stage_ref[index].astype(jnp.bfloat16)
    whole.wait()


def early_kernel(
    rows, lanes, count, mask_ref, pupils_ref, table_ref, weights_ref, row_ref, col_ref,
    mid_ref, out_ref, rest_ref, pupil_stage, sems,
):
    tile = mask_ref.shape[0]
    pupil_copy = pltpu.make_async_copy(pupils_ref.at[:, pl.ds(0, count)], pupil_stage, sems.at[0])
    pupil_copy.start()
    rest = pupils_ref.shape[1] - count
    rest_copy = pltpu.make_async_copy(pupils_ref.at[:, pl.ds(count, rest)], rest_ref, sems.at[1])
    rest_copy.start()
    mid_ref[...] = dot(
        table_ref[:, AMBIT : AMBIT + tile], mask_ref[...].astype(jnp.bfloat16)
    )
    pupil_copy.wait()
    pupil_steps(rows, lanes, 0, count, pupil_stage, weights_ref, row_ref, col_ref, out_ref)
    rest_copy.wait()


def partial_kernel(
    live_ref, mid_ref, near_ref, cross_ref, table_ref, col_t_ref, own_ref, kept_ref, facing_ref, sent_ref
):
    extent = table_ref.shape[1]
    width = mid_ref.shape[1]
    tile = extent - 2 * AMBIT
    total = mid_ref[...]
    for start, rim_ref in zip(sides(extent - AMBIT), (near_ref, cross_ref)):
        total = total + dot(table_ref[:, pl.ds(start, AMBIT)], rim_ref[...])
    total = total.astype(jnp.bfloat16)
    parity = col_parity()
    live = live_ref[0, 1 - parity].astype(jnp.float32)

    def store(near, far, far_table, facing, kept):
        own_ref[...] = total[:, near]
        kept_ref[...] = total[:, kept]
        facing_ref[...] = total[:, facing]
        main = dot(total[:, far], col_t_ref[far_table])
        shape = main.shape
        flag = (lax.broadcasted_iota(jnp.int32, shape, 0) == shape[0] - 1) & (
            lax.broadcasted_iota(jnp.int32, shape, 1) == shape[1] - 1
        )
        sent_ref[...] = jnp.where(flag, live, main).astype(jnp.bfloat16)

    reach = tile + AMBIT
    first, last = slice(0, reach), slice(width - reach, width)
    low, high = slice(0, AMBIT), slice(width - AMBIT, width)

    @pl.when(parity == 0)
    def _():
        store(first, last, slice(0, reach), low, high)

    @pl.when(parity > 0)
    def _():
        store(last, first, slice(AMBIT, extent), high, low)


def late_kernel(
    rows, lanes, first, last, pupils_ref, own_ref, col_t_ref, quads_ref, weights_ref, row_ref, col_ref,
    base_ref, out_ref,
):
    out_ref[:first] = quads_ref[...]
    reach = own_ref.shape[1]
    start = pl.multiple_of((1 - col_parity()) * AMBIT, AMBIT)
    base_ref[...] = dot(own_ref[...], col_t_ref[pl.ds(start, reach)])
    pupil_steps(rows, lanes, first, last, pupils_ref, weights_ref, row_ref, col_ref, out_ref)


def in_groups(count, group, run):
    def one(index, carry):
        run(index * group, False)
        return carry

    if count > group:
        lax.fori_loop(0, count // group - 1, one, 0)
    run(count - group, True)


def core_kernel(
    rows,
    lanes,
    live_ref,
    base_ref,
    facing_ref,
    sent_ref,
    kept_ref,
    goal_ref,
    other_ref,
    pupil_ref,
    row_ref,
    row_t_ref,
    col_ref,
    col_t_ref,
    out_ref,
    other_out_ref,
    spec_ref,
    amp_ref,
    sec_ref,
    field_ref,
    total_ref,
    slope_ref,
    back_ref,
    sum_ref,
    ans_ref,
):
    tile = goal_ref.shape[0]
    extent = row_ref.shape[1]
    kernels = pupil_ref.shape[0]
    halves = [slice(start, start + 2 * LANE) for start in range(0, tile, 2 * LANE)]
    inner = slice(AMBIT, AMBIT + tile)
    parity = col_parity()
    end = col_t_ref[pl.ds(pl.multiple_of(parity * (extent - AMBIT), AMBIT), AMBIT)]
    spec_ref[0] = base_ref[...] + dot(facing_ref[...], end)
    spec_ref[1] = sent_ref[...].astype(jnp.float32) + dot(kept_ref[...], end)
    corner = sent_ref[2 * rows - 16 :, 2 * lanes - LANE :].astype(jnp.float32)
    other_live = jnp.max(corner[15:, LANE - 1 :])
    out_ref[...] = jnp.zeros_like(out_ref)
    other_out_ref[...] = jnp.zeros_like(other_out_ref)

    def work(item, carry):
        live = jnp.where(item == 0, live_ref[0, parity].astype(jnp.float32), other_live) > 0.0

        @pl.when(live)
        def _():
            spec = spec_ref[item]
            cc, cs = spec[:rows, :lanes], spec[:rows, lanes:]
            sc, ss = spec[rows:, :lanes], spec[rows:, lanes:]
            sum_ref[0] = cc - ss
            sum_ref[1] = sc + cs
            sum_ref[2] = cc + ss
            sum_ref[3] = sc - cs

            def pupil(k, index):
                return pupil_ref[k, index].astype(jnp.float32)

            def section(k, buf):
                u, v, m, n = sum_ref[0], sum_ref[1], sum_ref[2], sum_ref[3]
                pr, pi, mr, mi = (pupil(k, index) for index in range(4))
                big_re = pr * u + mi * v
                big_im = pi * u - mr * v
                small_re = mr * u + pi * v
                small_im = mi * u - pr * v
                pr, pi, mr, mi = (pupil(k, index) for index in range(4, 8))
                big_re2 = pr * m + mi * n
                big_im2 = pi * m - mr * n
                small_re2 = mr * m + pi * n
                small_im2 = mi * m - pr * n

                def pair(place, left, right):
                    where = slice(place * rows, (place + 1) * rows)
                    amp_ref[buf, where, :lanes] = left.astype(jnp.bfloat16)
                    amp_ref[buf, where, lanes:] = right.astype(jnp.bfloat16)

                pair(0, big_re + big_re2, small_im2 - small_im)
                pair(1, -(small_im + small_im2), big_re2 - big_re)
                pair(2, big_im + big_im2, small_re - small_re2)
                pair(3, small_re + small_re2, big_im2 - big_im)
                sec_ref[buf] = dot(amp_ref[buf], col_ref[:, inner]).astype(jnp.bfloat16)

            def field(ks, bufs):
                for where in halves:
                    energy = None
                    for k, buf in zip(ks, bufs):
                        real = dot(row_t_ref[inner], sec_ref[buf, : 2 * rows, where])
                        imag = dot(row_t_ref[inner], sec_ref[buf, 2 * rows :, where])
                        field_ref[k, 0, :, where] = real.astype(jnp.bfloat16)
                        field_ref[k, 1, :, where] = imag.astype(jnp.bfloat16)
                        term = real * real + imag * imag
                        energy = term if energy is None else energy + term
                    total_ref[:, where] += energy

            section(0, 0)
            section(1, 1)
            total_ref[...] = jnp.zeros_like(total_ref)

            def forward(first, last_group):
                for step in range(0, 4, 2):
                    bufs, nexts = (0, 1), (2, 3)
                    if step:
                        bufs, nexts = nexts, bufs
                    k = first + step
                    more = step == 0 or not last_group
                    field((k, k + 1), bufs)
                    if more:
                        section(k + 2, nexts[0])
                        section(k + 3, nexts[1])

            in_groups(kernels, 4, forward)

            def back(ks, bufs):
                for where in halves:
                    for k, buf in zip(ks, bufs):
                        for part in range(2):
                            cotangent = slope_ref[:, where] * field_ref[k, part, :, where]
                            place = slice(part * 2 * rows, (part + 1) * 2 * rows)
                            back_ref[buf, place, where] = dot(
                                row_ref[:, inner], cotangent
                            ).astype(jnp.bfloat16)

            def adjoint(k, buf):
                wave = dot(back_ref[buf], col_t_ref[inner])
                rcc, rcs = wave[:rows, :lanes], wave[:rows, lanes:]
                rsc, rss = wave[rows : 2 * rows, :lanes], wave[rows : 2 * rows, lanes:]
                icc, ics = wave[2 * rows : 3 * rows, :lanes], wave[2 * rows : 3 * rows, lanes:]
                isc, iss = wave[3 * rows :, :lanes], wave[3 * rows :, lanes:]
                ur, ui, vr, vi = rcc - rss, icc - iss, rsc + rcs, isc + ics
                pr, pi, mr, mi = (pupil(k, index) for index in range(4))
                ans_ref[0] += pr * ur + pi * ui + mr * vi - mi * vr
                ans_ref[1] += mr * ui - mi * ur - pr * vr - pi * vi
                ur, ui, vr, vi = rcc + rss, icc + iss, rsc - rcs, isc - ics
                pr, pi, mr, mi = (pupil(k, index) for index in range(4, 8))
                ans_ref[2] += pr * ur + pi * ui + mr * vi - mi * vr
                ans_ref[3] += mr * ui - mi * ur - pr * vr - pi * vi

            ans_ref[...] = jnp.zeros_like(ans_ref)

            def slopes(ref, first):
                for where in halves:
                    place = pl.ds(pl.multiple_of(first + where.start, LANE), 2 * LANE)
                    level = jnp.tanh(total_ref[:, where] - 0.5 * steepness * threshold_level)
                    excess = 0.5 * level + 0.5 - ref[:, place].astype(jnp.float32)
                    slope_ref[:, where] = (excess * (1.0 - level * level)).astype(jnp.bfloat16)
                back((0, 1), (0, 1))

            @pl.when(item == 0)
            def _():
                slopes(goal_ref, parity * tile)

            @pl.when(item > 0)
            def _():
                slopes(other_ref, 0)

            def backward(first, last_group):
                for step in range(0, 4, 2):
                    bufs, nexts = (0, 1), (2, 3)
                    if step:
                        bufs, nexts = nexts, bufs
                    k = first + step
                    adjoint(k, bufs[0])
                    adjoint(k + 1, bufs[1])
                    if step == 0 or not last_group:
                        back((k + 2, k + 3), nexts)

            in_groups(kernels, 4, backward)

            def answer(ref):
                ref[:rows, :lanes] = (ans_ref[0] + ans_ref[2]).astype(jnp.bfloat16)
                ref[:rows, lanes:] = (ans_ref[3] - ans_ref[1]).astype(jnp.bfloat16)
                ref[rows:, :lanes] = (-(ans_ref[1] + ans_ref[3])).astype(jnp.bfloat16)
                ref[rows:, lanes:] = (ans_ref[2] - ans_ref[0]).astype(jnp.bfloat16)

            @pl.when(item == 0)
            def _():
                answer(out_ref)

            @pl.when(item > 0)
            def _():
                answer(other_out_ref)

        return carry

    lax.fori_loop(0, 2, work, 0)


def returned_kernel(
    tile, mine_ref, other_ref, paired_ref, facing_ref, row_t_ref, col_ref, out_ref, near_ref, cross_ref, sum_ref
):
    width = out_ref.shape[1]
    extent = row_t_ref.shape[0]
    odd = col_parity() > 0
    mine, other, paired, facing = (
        ref[...] for ref in (mine_ref, other_ref, paired_ref, facing_ref)
    )
    values = (
        jnp.where(odd, other, facing),
        jnp.where(odd, paired, mine),
        jnp.where(odd, mine, paired),
        jnp.where(odd, facing, other),
    )
    sum_ref[...] = jnp.zeros_like(sum_ref)
    for place, value in zip(range(-1, 3), values):
        start = place * tile - AMBIT
        low, high = max(0, start), min(width, start + extent)
        sum_ref[:, low:high] += dot(value, col_ref[:, low - start : high - start])
    mixed = sum_ref[...].astype(jnp.bfloat16)
    out_ref[...] = mixed
    for start, rim_ref in zip(sides(extent - AMBIT), (near_ref, cross_ref)):
        rim_ref[...] = dot(row_t_ref[pl.ds(start, AMBIT)], mixed).astype(jnp.bfloat16)


def update_kernel(mask_ref, mixed_ref, row_t_ref, out_ref, rims_ref, stage_ref, sem):
    tile = mask_ref.shape[0]
    stage_ref[...] = mask_ref[...] - step_rate * dot(
        row_t_ref[AMBIT : AMBIT + tile], mixed_ref[...]
    )
    inner = pl.ds(AMBIT, tile - 2 * AMBIT)
    copy = pltpu.make_async_copy(stage_ref.at[inner], out_ref.at[inner], sem)
    copy.start()
    rims_ref[:AMBIT] = stage_ref[:AMBIT]
    rims_ref[AMBIT:] = stage_ref[tile - AMBIT :]
    copy.wait()


def rims_kernel(near_ref, cross_ref, rims_ref, base_ref, out_ref, stage_ref, sems):
    tile = out_ref.shape[0]
    copies = []
    places = zip((cross_ref, near_ref), sides(AMBIT)[::-1], sides(tile - AMBIT)[::-1])
    for index, (rim_ref, place, start) in enumerate(places):
        stage_ref[index] = rims_ref[pl.ds(place, AMBIT)] - step_rate * rim_ref[...].astype(
            jnp.float32
        )
        copy = pltpu.make_async_copy(
            stage_ref.at[index], out_ref.at[pl.ds(start, AMBIT)], sems.at[index]
        )
        copy.start()
        copies.append(copy)
    for copy in copies:
        copy.wait()


def body(mask, target, live, pupils, weights):
    tile, width = mask.shape
    kernels, size = pupils.shape[1], pupils.shape[2]
    half = size // 2
    rows, lanes = round_up(half + 1, 16), round_up(half + 2, LANE)
    extent = tile + 2 * AMBIT
    row_np = half_tables(half, rows, extent)
    col_np = half_tables(half, lanes, extent)
    row_pick, col_pick = (
        jnp.asarray(pick, jnp.bfloat16) for pick in pick_tables(half, rows, lanes)
    )
    row_table, row_table_t = jnp.asarray(row_np, jnp.bfloat16), jnp.asarray(row_np.T, jnp.bfloat16)
    col_table, col_table_t = jnp.asarray(col_np, jnp.bfloat16), jnp.asarray(col_np.T, jnp.bfloat16)
    bf16, f32 = jnp.bfloat16, jnp.float32
    shape = jax.ShapeDtypeStruct
    smem = pl.BlockSpec(memory_space=pltpu.SMEM)
    early = kernels // 2

    hbm = pl.BlockSpec(memory_space=pltpu.HBM)
    dma = pltpu.SemaphoreType.DMA
    edge = shape((AMBIT, width), bf16)
    near, cross, goal = call(
        edges_kernel,
        (edge, edge, shape((tile, tile), bf16)),
        [hbm, hbm],
        scratch=[pltpu.VMEM((2, AMBIT, width), f32), dma((3,))],
        limit=52,
    )(mask, target)
    other_goal = swapped(goal, "col", 0)
    cross = swapped(cross, "row", 1)
    near = swapped(near, "row", 0)
    middle, quads, rest = call(
        partial(early_kernel, rows, lanes, early),
        (
            shape((2 * rows, width), f32),
            shape((early, 8, rows, lanes), bf16),
            shape((2, kernels - early, size, size), f32),
        ),
        [*vmem(1), hbm, *vmem(1), smem, *vmem(2)],
        scratch=[pltpu.VMEM((2, early, size, size), f32), dma((2,))],
        limit=48,
        us=4,
    )(mask, pupils, row_table, weights, row_pick, col_pick)
    own, kept, facing, sending = call(
        partial_kernel,
        (
            shape((2 * rows, tile + AMBIT), bf16),
            shape((2 * rows, AMBIT), bf16),
            shape((2 * rows, AMBIT), bf16),
            shape((2 * rows, 2 * lanes), bf16),
        ),
        [smem, *vmem(5)],
    )(live, middle, near, cross, row_table, col_table_t)
    sent = swapped(sending, "col", 0)
    faced = swapped(facing, "col", 1)
    base, all_quads = call(
        partial(late_kernel, rows, lanes, early, kernels),
        (shape((2 * rows, 2 * lanes), f32), shape((kernels, 8, rows, lanes), bf16)),
        [*vmem(4), smem, *vmem(2)],
        limit=16,
        us=4,
    )(rest, own, col_table_t, quads, weights, row_pick, col_pick)
    answer = shape((2 * rows, 2 * lanes), bf16)
    mine, other = call(
        partial(core_kernel, rows, lanes),
        (answer, answer),
        [smem, *vmem(11)],
        scratch=[
            pltpu.VMEM((2, 2 * rows, 2 * lanes), f32),
            pltpu.VMEM((4, 4 * rows, 2 * lanes), bf16),
            pltpu.VMEM((4, 4 * rows, tile), bf16),
            pltpu.VMEM((kernels, 2, tile, tile), bf16),
            pltpu.VMEM((tile, tile), f32),
            pltpu.VMEM((tile, tile), bf16),
            pltpu.VMEM((4, 4 * rows, tile), bf16),
            pltpu.VMEM((4, rows, lanes), f32),
            pltpu.VMEM((4, rows, lanes), f32),
        ],
        limit=36,
        us=15,
    )(
        live, base, faced, sent, kept, target, other_goal, all_quads,
        row_table, row_table_t, col_table, col_table_t,
    )
    paired = swapped(other, "col", 0)
    returned = swapped(mine, "col", 1)
    mixed, near, cross = call(
        partial(returned_kernel, tile),
        (shape((2 * rows, width), bf16), shape((AMBIT, width), bf16), shape((AMBIT, width), bf16)),
        vmem(6),
        scratch=[pltpu.VMEM((2 * rows, width), f32)],
    )(mine, other, paired, returned, row_table_t, col_table)
    cross = swapped(cross, "row", 1)
    near = swapped(near, "row", 0)
    anywhere = pl.BlockSpec(memory_space=pl.ANY)
    whole, rims = shape((tile, width), f32), shape((2 * AMBIT, width), f32)
    updated, edges = pl.pallas_call(
        update_kernel,
        out_shape=(whole, rims),
        in_specs=vmem(3),
        out_specs=(anywhere, *vmem(1)),
        scratch_shapes=[pltpu.VMEM((tile, width), f32), dma],
        cost_estimate=pl.CostEstimate(flops=10**9, bytes_accessed=2 * 10**6, transcendentals=0),
        compiler_params=pltpu.CompilerParams(vmem_limit_bytes=16 * MIB),
    )(mask, mixed, row_table_t)
    return pl.pallas_call(
        rims_kernel,
        out_shape=whole,
        in_specs=[*vmem(3), anywhere],
        out_specs=anywhere,
        scratch_shapes=[pltpu.VMEM((2, AMBIT, width), f32), pltpu.SemaphoreType.DMA((2,))],
        input_output_aliases={3: 0},
        compiler_params=pltpu.CompilerParams(vmem_limit_bytes=8 * MIB),
    )(near, cross, edges, updated)


def solution(mesh):
    placed = (P("row", "col"), P("row", "col"), P("row", "col"), P(), P())
    return jax.shard_map(
        body, mesh=mesh, in_specs=placed, out_specs=P("row", "col"), check_vma=False
    )
```

```python
from functools import partial
import math

import jax
import jax.numpy as jnp
import numpy as np
from jax import lax
from jax.experimental import pallas as pl
from jax.experimental.pallas import tpu as pltpu
from jax.sharding import PartitionSpec as P


AMBIT = 128
LANE = 128

steepness = 4.0
threshold_level = 1.0
step_rate = 8.0

MIB = 1024 * 1024


def round_up(value, unit):
    return -(-value // unit) * unit


def swapped(block, axis, offset):
    count = lax.axis_size(axis)
    pairs = []
    for low in range(offset, count - 1, 2):
        pairs += [(low, low + 1), (low + 1, low)]
    return lax.ppermute(block, axis, pairs)


def sides(reach):
    odd = lax.rem(lax.axis_index("row"), 2)
    return [pl.multiple_of(side * reach, AMBIT) for side in (1 - odd, odd)]


def turned(block, axis, step):
    count = lax.axis_size(axis)
    return lax.ppermute(block, axis, [(i, (i + step) % count) for i in range(count)])


def dot(leading, trailing):
    return jnp.dot(leading, trailing, preferred_element_type=jnp.float32)


def half_tables(half, rows, extent):
    frequency = np.arange(half + 1, dtype=np.int64)
    pixels = np.arange(extent, dtype=np.int64)
    phases = np.mod(frequency[:, None] * pixels[None, :], extent).astype(np.float32)
    angles = phases * np.float32(2.0 * math.pi / extent)
    factor = np.float32(1.0 / math.sqrt(extent))
    table = np.zeros((2 * rows, extent), np.float32)
    table[: half + 1] = np.cos(angles) * factor
    table[rows : rows + half + 1] = np.sin(angles) * factor
    return table


def pick_tables(half, rows, lanes):
    size = 2 * half
    row_pick = np.zeros((2 * rows, size), np.float32)
    col_pick = np.zeros((size, 2 * lanes), np.float32)
    for index in range(half):
        row_pick[index, half + index] = 1.0
        col_pick[half + index, index] = 1.0
        row_pick[rows + half - index, index] = 1.0
        col_pick[index, lanes + half - index] = 1.0
    return row_pick, col_pick


def vmem(count):
    return [pl.BlockSpec(memory_space=pltpu.VMEM)] * count


def call(kernel, outs, specs, scratch=(), limit=16, us=1, **kwargs):
    return pl.pallas_call(
        kernel,
        out_shape=outs,
        in_specs=specs,
        out_specs=jax.tree.map(lambda _: pl.BlockSpec(memory_space=pltpu.VMEM), outs),
        scratch_shapes=list(scratch),
        cost_estimate=pl.CostEstimate(
            flops=int(us * 5e8), bytes_accessed=int(us * 1e6), transcendentals=0
        ),
        compiler_params=pltpu.CompilerParams(vmem_limit_bytes=limit * MIB),
        **kwargs,
    )


def pupil_steps(rows, lanes, first, last, pupils_ref, weights_ref, row_ref, col_ref, out_ref):
    for k in range(first, last):
        scale = jnp.sqrt(jnp.full((1, 1), weights_ref[k] * (0.5 * steepness), jnp.float32))
        for part in range(2):
            values = (pupils_ref[part, k - first] * scale).astype(jnp.bfloat16)
            columns = dot(values, col_ref[...]).astype(jnp.bfloat16)
            full = dot(row_ref[...], columns)
            pos_pos, pos_neg = full[:rows, :lanes], full[:rows, lanes:]
            neg_pos, neg_neg = full[rows:, :lanes], full[rows:, lanes:]
            out_ref[k, 0 + part] = (pos_pos + neg_neg).astype(jnp.bfloat16)
            out_ref[k, 2 + part] = (pos_pos - neg_neg).astype(jnp.bfloat16)
            out_ref[k, 4 + part] = (pos_neg + neg_pos).astype(jnp.bfloat16)
            out_ref[k, 6 + part] = (pos_neg - neg_pos).astype(jnp.bfloat16)


def edges_kernel(mask_ref, target_ref, near_ref, cross_ref, goal_ref, stage_ref, sems):
    tile = mask_ref.shape[0]
    whole = pltpu.make_async_copy(target_ref.at[:, tile:], goal_ref, sems.at[2])
    copies = []
    for index, start in enumerate(sides(tile - AMBIT)):
        copy = pltpu.make_async_copy(
            mask_ref.at[pl.ds(start, AMBIT)], stage_ref.at[index], sems.at[index]
        )
        copy.start()
        copies.append(copy)
    whole.start()
    for index, out_ref in enumerate((near_ref, cross_ref)):
        copies[index].wait()
        out_ref[...] = stage_ref[index].astype(jnp.bfloat16)
    whole.wait()


def early_kernel(
    rows, lanes, count, mask_ref, pupils_ref, table_ref, weights_ref, row_ref, col_ref,
    mid_ref, out_ref, rest_ref, pupil_stage, sems,
):
    tile = mask_ref.shape[0]
    pupil_copy = pltpu.make_async_copy(pupils_ref.at[:, pl.ds(0, count)], pupil_stage, sems.at[0])
    pupil_copy.start()
    rest = pupils_ref.shape[1] - count
    rest_copy = pltpu.make_async_copy(pupils_ref.at[:, pl.ds(count, rest)], rest_ref, sems.at[1])
    rest_copy.start()
    mid_ref[...] = dot(
        table_ref[:, AMBIT : AMBIT + tile], mask_ref[...].astype(jnp.bfloat16)
    )
    pupil_copy.wait()
    pupil_steps(rows, lanes, 0, count, pupil_stage, weights_ref, row_ref, col_ref, out_ref)
    rest_copy.wait()


def partial_kernel(
    live_ref, mid_ref, near_ref, cross_ref, table_ref, col_t_ref, own_ref, low_ref, sent_ref
):
    extent = table_ref.shape[1]
    width = mid_ref.shape[1]
    tile = extent - 2 * AMBIT
    total = mid_ref[...]
    for start, rim_ref in zip(sides(extent - AMBIT), (near_ref, cross_ref)):
        total = total + dot(table_ref[:, pl.ds(start, AMBIT)], rim_ref[...])
    total = total.astype(jnp.bfloat16)
    own_ref[...] = total[:, : tile + AMBIT]
    low_ref[...] = total[:, :AMBIT]
    sent_ref[:, :AMBIT] = total[:, width - AMBIT :]
    main = dot(total[:, tile - AMBIT :], col_t_ref[: tile + AMBIT])
    shape = main.shape
    flag = (lax.broadcasted_iota(jnp.int32, shape, 0) == shape[0] - 1) & (
        lax.broadcasted_iota(jnp.int32, shape, 1) == shape[1] - 1
    )
    live = live_ref[0, live_ref.shape[1] - 1].astype(jnp.float32)
    sent_ref[:, AMBIT:] = jnp.where(flag, live, main).astype(jnp.bfloat16)


def late_kernel(
    rows, lanes, first, last, pupils_ref, own_ref, col_t_ref, quads_ref, weights_ref, row_ref, col_ref,
    base_ref, out_ref,
):
    out_ref[:first] = quads_ref[...]
    base_ref[...] = dot(own_ref[...], col_t_ref[AMBIT:])
    pupil_steps(rows, lanes, first, last, pupils_ref, weights_ref, row_ref, col_ref, out_ref)


def in_groups(count, group, run):
    def one(index, carry):
        run(index * group, False)
        return carry

    if count > group:
        lax.fori_loop(0, count // group - 1, one, 0)
    run(count - group, True)


def core_kernel(
    rows,
    lanes,
    live_ref,
    base_ref,
    sent_ref,
    low_ref,
    goal_ref,
    other_ref,
    pupil_ref,
    row_ref,
    row_t_ref,
    col_ref,
    col_t_ref,
    out_ref,
    spec_ref,
    amp_ref,
    sec_ref,
    field_ref,
    total_ref,
    slope_ref,
    back_ref,
    sum_ref,
    ans_ref,
):
    tile = goal_ref.shape[0]
    extent = row_ref.shape[1]
    kernels = pupil_ref.shape[0]
    halves = [slice(start, start + 2 * LANE) for start in range(0, tile, 2 * LANE)]
    inner = slice(AMBIT, AMBIT + tile)
    outer = lax.axis_index("col") == 0
    left = sent_ref[:, :AMBIT]
    left = jnp.where(outer, jnp.zeros_like(left), left)
    spec_ref[0] = base_ref[...] + dot(left, col_t_ref[:AMBIT])
    right = low_ref[...]
    right = jnp.where(outer, jnp.zeros_like(right), right)
    spec_ref[1] = sent_ref[:, AMBIT:].astype(jnp.float32) + dot(right, col_t_ref[extent - AMBIT :])
    corner = sent_ref[2 * rows - 16 :, AMBIT + 2 * lanes - LANE :].astype(jnp.float32)
    other_live = jnp.max(corner[15:, LANE - 1 :])
    out_ref[...] = jnp.zeros_like(out_ref)

    def work(item, carry):
        live = jnp.where(item == 0, live_ref[0, 0].astype(jnp.float32), other_live) > 0.0

        @pl.when(live)
        def _():
            spec = spec_ref[item]
            cc, cs = spec[:rows, :lanes], spec[:rows, lanes:]
            sc, ss = spec[rows:, :lanes], spec[rows:, lanes:]
            sum_ref[0] = cc - ss
            sum_ref[1] = sc + cs
            sum_ref[2] = cc + ss
            sum_ref[3] = sc - cs

            def pupil(k, index):
                return pupil_ref[k, index].astype(jnp.float32)

            def section(k, buf):
                u, v, m, n = sum_ref[0], sum_ref[1], sum_ref[2], sum_ref[3]
                pr, pi, mr, mi = (pupil(k, index) for index in range(4))
                big_re = pr * u + mi * v
                big_im = pi * u - mr * v
                small_re = mr * u + pi * v
                small_im = mi * u - pr * v
                pr, pi, mr, mi = (pupil(k, index) for index in range(4, 8))
                big_re2 = pr * m + mi * n
                big_im2 = pi * m - mr * n
                small_re2 = mr * m + pi * n
                small_im2 = mi * m - pr * n

                def pair(place, left, right):
                    where = slice(place * rows, (place + 1) * rows)
                    amp_ref[buf, where, :lanes] = left.astype(jnp.bfloat16)
                    amp_ref[buf, where, lanes:] = right.astype(jnp.bfloat16)

                pair(0, big_re + big_re2, small_im2 - small_im)
                pair(1, -(small_im + small_im2), big_re2 - big_re)
                pair(2, big_im + big_im2, small_re - small_re2)
                pair(3, small_re + small_re2, big_im2 - big_im)
                sec_ref[buf] = dot(amp_ref[buf], col_ref[:, inner]).astype(jnp.bfloat16)

            def field(ks, bufs):
                for where in halves:
                    energy = None
                    for k, buf in zip(ks, bufs):
                        real = dot(row_t_ref[inner], sec_ref[buf, : 2 * rows, where])
                        imag = dot(row_t_ref[inner], sec_ref[buf, 2 * rows :, where])
                        field_ref[k, 0, :, where] = real.astype(jnp.bfloat16)
                        field_ref[k, 1, :, where] = imag.astype(jnp.bfloat16)
                        term = real * real + imag * imag
                        energy = term if energy is None else energy + term
                    total_ref[:, where] += energy

            section(0, 0)
            section(1, 1)
            total_ref[...] = jnp.full_like(total_ref, -0.5 * steepness * threshold_level)

            def forward(first, last_group):
                for step in range(0, 4, 2):
                    bufs, nexts = (0, 1), (2, 3)
                    if step:
                        bufs, nexts = nexts, bufs
                    k = first + step
                    more = step == 0 or not last_group
                    field((k, k + 1), bufs)
                    if more:
                        section(k + 2, nexts[0])
                        section(k + 3, nexts[1])

            in_groups(kernels, 4, forward)

            def back(ks, bufs):
                for where in halves:
                    for k, buf in zip(ks, bufs):
                        for part in range(2):
                            cotangent = slope_ref[:, where] * field_ref[k, part, :, where]
                            place = slice(part * 2 * rows, (part + 1) * 2 * rows)
                            back_ref[buf, place, where] = dot(
                                row_ref[:, inner], cotangent
                            ).astype(jnp.bfloat16)

            def adjoint(k, buf):
                wave = dot(back_ref[buf], col_t_ref[inner])
                rcc, rcs = wave[:rows, :lanes], wave[:rows, lanes:]
                rsc, rss = wave[rows : 2 * rows, :lanes], wave[rows : 2 * rows, lanes:]
                icc, ics = wave[2 * rows : 3 * rows, :lanes], wave[2 * rows : 3 * rows, lanes:]
                isc, iss = wave[3 * rows :, :lanes], wave[3 * rows :, lanes:]
                ur, ui, vr, vi = rcc - rss, icc - iss, rsc + rcs, isc + ics
                pr, pi, mr, mi = (pupil(k, index) for index in range(4))
                ans_ref[0] += pr * ur + pi * ui + mr * vi - mi * vr
                ans_ref[1] += mr * ui - mi * ur - pr * vr - pi * vi
                ur, ui, vr, vi = rcc + rss, icc + iss, rsc - rcs, isc - ics
                pr, pi, mr, mi = (pupil(k, index) for index in range(4, 8))
                ans_ref[2] += pr * ur + pi * ui + mr * vi - mi * vr
                ans_ref[3] += mr * ui - mi * ur - pr * vr - pi * vi

            ans_ref[...] = jnp.zeros_like(ans_ref)

            def slopes(ref):
                for where in halves:
                    level = jnp.tanh(total_ref[:, where])
                    excess = 0.5 * level + 0.5 - ref[:, where].astype(jnp.float32)
                    slope_ref[:, where] = (excess * (1.0 - level * level)).astype(jnp.bfloat16)
                back((0, 1), (0, 1))

            @pl.when(item == 0)
            def _():
                slopes(goal_ref)

            @pl.when(item > 0)
            def _():
                slopes(other_ref)

            def backward(first, last_group):
                for step in range(0, 4, 2):
                    bufs, nexts = (0, 1), (2, 3)
                    if step:
                        bufs, nexts = nexts, bufs
                    k = first + step
                    adjoint(k, bufs[0])
                    adjoint(k + 1, bufs[1])
                    if step == 0 or not last_group:
                        back((k + 2, k + 3), nexts)

            in_groups(kernels, 4, backward)

            def answer(first):
                left, right = slice(first, first + lanes), slice(first + lanes, first + 2 * lanes)
                out_ref[:rows, left] = (ans_ref[0] + ans_ref[2]).astype(jnp.bfloat16)
                out_ref[:rows, right] = (ans_ref[3] - ans_ref[1]).astype(jnp.bfloat16)
                out_ref[rows:, left] = (-(ans_ref[1] + ans_ref[3])).astype(jnp.bfloat16)
                out_ref[rows:, right] = (ans_ref[2] - ans_ref[0]).astype(jnp.bfloat16)

            @pl.when(item == 0)
            def _():
                answer(0)

            @pl.when(item > 0)
            def _():
                answer(2 * lanes)

        return carry

    lax.fori_loop(0, 2, work, 0)


def returned_kernel(tile, mine_ref, sent_ref, row_t_ref, col_ref, out_ref, near_ref, cross_ref, sum_ref):
    width = out_ref.shape[1]
    extent = row_t_ref.shape[0]
    lanes = mine_ref.shape[1] // 2
    place = lax.axis_index("col")
    before, after = mine_ref[:, lanes:], sent_ref[:, :lanes]
    before = jnp.where(place == 0, jnp.zeros_like(before), before)
    after = jnp.where(place == lax.axis_size("col") - 1, jnp.zeros_like(after), after)
    sum_ref[...] = jnp.zeros_like(sum_ref)
    for place, value in zip(range(-1, 3), (before, mine_ref[:, :lanes], sent_ref[:, lanes:], after)):
        start = place * tile - AMBIT
        low, high = max(0, start), min(width, start + extent)
        sum_ref[:, low:high] += dot(value, col_ref[:, low - start : high - start])
    mixed = sum_ref[...].astype(jnp.bfloat16)
    out_ref[...] = mixed
    for start, rim_ref in zip(sides(extent - AMBIT), (near_ref, cross_ref)):
        rim_ref[...] = dot(row_t_ref[pl.ds(start, AMBIT)], mixed).astype(jnp.bfloat16)


def update_kernel(mask_ref, mixed_ref, near_ref, row_t_ref, out_ref, rim_ref, stage_ref, sem):
    tile = mask_ref.shape[0]
    stage_ref[...] = mask_ref[...] - step_rate * dot(
        row_t_ref[AMBIT : AMBIT + tile], mixed_ref[...]
    )
    near, cross = (pl.ds(start, AMBIT) for start in sides(tile - AMBIT))
    stage_ref[near] = stage_ref[near] - step_rate * near_ref[...].astype(jnp.float32)
    kept = pl.ds(pl.multiple_of((1 - lax.rem(lax.axis_index("row"), 2)) * AMBIT, AMBIT), tile - AMBIT)
    copy = pltpu.make_async_copy(stage_ref.at[kept], out_ref.at[kept], sem)
    copy.start()
    rim_ref[...] = stage_ref[cross]
    copy.wait()


def rim_kernel(cross_ref, rim_ref, base_ref, out_ref, stage_ref, sem):
    start = sides(out_ref.shape[0] - AMBIT)[1]
    stage_ref[...] = rim_ref[...] - step_rate * cross_ref[...].astype(jnp.float32)
    copy = pltpu.make_async_copy(stage_ref, out_ref.at[pl.ds(start, AMBIT)], sem)
    copy.start()
    copy.wait()


def body(mask, target, live, pupils, weights):
    tile, width = mask.shape
    kernels, size = pupils.shape[1], pupils.shape[2]
    half = size // 2
    rows, lanes = round_up(half + 1, 16), round_up(half + 2, LANE)
    extent = tile + 2 * AMBIT
    row_np = half_tables(half, rows, extent)
    col_np = half_tables(half, lanes, extent)
    row_pick, col_pick = (
        jnp.asarray(pick, jnp.bfloat16) for pick in pick_tables(half, rows, lanes)
    )
    row_table, row_table_t = jnp.asarray(row_np, jnp.bfloat16), jnp.asarray(row_np.T, jnp.bfloat16)
    col_table, col_table_t = jnp.asarray(col_np, jnp.bfloat16), jnp.asarray(col_np.T, jnp.bfloat16)
    bf16, f32 = jnp.bfloat16, jnp.float32
    shape = jax.ShapeDtypeStruct
    smem = pl.BlockSpec(memory_space=pltpu.SMEM)
    early = kernels // 2

    hbm = pl.BlockSpec(memory_space=pltpu.HBM)
    dma = pltpu.SemaphoreType.DMA
    edge = shape((AMBIT, width), bf16)
    near, cross, goal = call(
        edges_kernel,
        (edge, edge, shape((tile, tile), bf16)),
        [hbm, hbm],
        scratch=[pltpu.VMEM((2, AMBIT, width), f32), dma((3,))],
        limit=52,
    )(mask, target)
    other_goal = turned(goal, "col", 1)
    cross = swapped(cross, "row", 1)
    near = swapped(near, "row", 0)
    middle, quads, rest = call(
        partial(early_kernel, rows, lanes, early),
        (
            shape((2 * rows, width), f32),
            shape((early, 8, rows, lanes), bf16),
            shape((2, kernels - early, size, size), f32),
        ),
        [*vmem(1), hbm, *vmem(1), smem, *vmem(2)],
        scratch=[pltpu.VMEM((2, early, size, size), f32), dma((2,))],
        limit=48,
        us=4,
    )(mask, pupils, row_table, weights, row_pick, col_pick)
    own, low, sending = call(
        partial_kernel,
        (
            shape((2 * rows, tile + AMBIT), bf16),
            shape((2 * rows, AMBIT), bf16),
            shape((2 * rows, AMBIT + 2 * lanes), bf16),
        ),
        [smem, *vmem(5)],
    )(live, middle, near, cross, row_table, col_table_t)
    sent = turned(sending, "col", 1)
    base, all_quads = call(
        partial(late_kernel, rows, lanes, early, kernels),
        (shape((2 * rows, 2 * lanes), f32), shape((kernels, 8, rows, lanes), bf16)),
        [*vmem(4), smem, *vmem(2)],
        limit=16,
        us=4,
    )(rest, own, col_table_t, quads, weights, row_pick, col_pick)
    answers = call(
        partial(core_kernel, rows, lanes),
        shape((2 * rows, 4 * lanes), bf16),
        [smem, *vmem(10)],
        scratch=[
            pltpu.VMEM((2, 2 * rows, 2 * lanes), f32),
            pltpu.VMEM((4, 4 * rows, 2 * lanes), bf16),
            pltpu.VMEM((4, 4 * rows, tile), bf16),
            pltpu.VMEM((kernels, 2, tile, tile), bf16),
            pltpu.VMEM((tile, tile), f32),
            pltpu.VMEM((tile, tile), bf16),
            pltpu.VMEM((4, 4 * rows, tile), bf16),
            pltpu.VMEM((4, rows, lanes), f32),
            pltpu.VMEM((4, rows, lanes), f32),
        ],
        limit=36,
        us=15,
    )(
        live, base, sent, low, target, other_goal, all_quads,
        row_table, row_table_t, col_table, col_table_t,
    )
    returned = turned(answers, "col", -1)
    mixed, near, cross = call(
        partial(returned_kernel, tile),
        (shape((2 * rows, width), bf16), shape((AMBIT, width), bf16), shape((AMBIT, width), bf16)),
        vmem(4),
        scratch=[pltpu.VMEM((2 * rows, width), f32)],
    )(answers, returned, row_table_t, col_table)
    cross = swapped(cross, "row", 1)
    near = swapped(near, "row", 0)
    anywhere = pl.BlockSpec(memory_space=pl.ANY)
    whole, rim = shape((tile, width), f32), shape((AMBIT, width), f32)
    updated, rim = pl.pallas_call(
        update_kernel,
        out_shape=(whole, rim),
        in_specs=vmem(4),
        out_specs=(anywhere, *vmem(1)),
        scratch_shapes=[pltpu.VMEM((tile, width), f32), dma],
        cost_estimate=pl.CostEstimate(flops=10**9, bytes_accessed=2 * 10**6, transcendentals=0),
        compiler_params=pltpu.CompilerParams(vmem_limit_bytes=16 * MIB),
    )(mask, mixed, near, row_table_t)
    return pl.pallas_call(
        rim_kernel,
        out_shape=whole,
        in_specs=[*vmem(2), anywhere],
        out_specs=anywhere,
        scratch_shapes=[pltpu.VMEM((AMBIT, width), f32), dma],
        input_output_aliases={2: 0},
        compiler_params=pltpu.CompilerParams(vmem_limit_bytes=8 * MIB),
    )(cross, rim, updated)


def solution(mesh):
    placed = (P("row", "col"), P("row", "col"), P("row", "col"), P(), P())
    return jax.shard_map(
        body, mesh=mesh, in_specs=placed, out_specs=P("row", "col"), check_vma=False
    )
```

```python
from functools import partial
import math

import jax
import jax.numpy as jnp
import numpy as np
from jax import lax
from jax.experimental import pallas as pl
from jax.experimental.pallas import tpu as pltpu
from jax.sharding import PartitionSpec as P


AMBIT = 128
LANE = 128

steepness = 4.0
threshold_level = 1.0
step_rate = 8.0

MIB = 1024 * 1024


def round_up(value, unit):
    return -(-value // unit) * unit


def swapped(block, axis, offset):
    count = lax.axis_size(axis)
    pairs = []
    for low in range(offset, count - 1, 2):
        pairs += [(low, low + 1), (low + 1, low)]
    return lax.ppermute(block, axis, pairs)


def sides(reach):
    odd = lax.rem(lax.axis_index("row"), 2)
    return [pl.multiple_of(side * reach, AMBIT) for side in (1 - odd, odd)]


def turned(block, axis, step):
    count = lax.axis_size(axis)
    return lax.ppermute(block, axis, [(i, (i + step) % count) for i in range(count)])


def dot(leading, trailing):
    return jnp.dot(leading, trailing, preferred_element_type=jnp.float32)


def half_tables(half, rows, extent):
    frequency = np.arange(half + 1, dtype=np.int64)
    pixels = np.arange(extent, dtype=np.int64)
    phases = np.mod(frequency[:, None] * pixels[None, :], extent).astype(np.float32)
    angles = phases * np.float32(2.0 * math.pi / extent)
    factor = np.float32(1.0 / math.sqrt(extent))
    table = np.zeros((2 * rows, extent), np.float32)
    table[: half + 1] = np.cos(angles) * factor
    table[rows : rows + half + 1] = np.sin(angles) * factor
    return table


def pick_tables(half, rows, lanes):
    size = 2 * half
    row_pick = np.zeros((2 * rows, size), np.float32)
    col_pick = np.zeros((size, 2 * lanes), np.float32)
    for index in range(half):
        row_pick[index, half + index] = 1.0
        col_pick[half + index, index] = 1.0
        row_pick[rows + half - index, index] = 1.0
        col_pick[index, lanes + half - index] = 1.0
    return row_pick, col_pick


def vmem(count):
    return [pl.BlockSpec(memory_space=pltpu.VMEM)] * count


def call(kernel, outs, specs, scratch=(), limit=16, us=1, **kwargs):
    return pl.pallas_call(
        kernel,
        out_shape=outs,
        in_specs=specs,
        out_specs=jax.tree.map(lambda _: pl.BlockSpec(memory_space=pltpu.VMEM), outs),
        scratch_shapes=list(scratch),
        cost_estimate=pl.CostEstimate(
            flops=int(us * 5e8), bytes_accessed=int(us * 1e6), transcendentals=0
        ),
        compiler_params=pltpu.CompilerParams(vmem_limit_bytes=limit * MIB),
        **kwargs,
    )


def pupil_steps(rows, lanes, first, last, pupils_ref, weights_ref, row_ref, col_ref, out_ref):
    for k in range(first, last):
        scale = jnp.sqrt(weights_ref[:, k : k + 1] * (0.5 * steepness))
        for part in range(2):
            values = (pupils_ref[part, k - first] * scale).astype(jnp.bfloat16)
            columns = dot(values, col_ref[...]).astype(jnp.bfloat16)
            full = dot(row_ref[...], columns)
            pos_pos, pos_neg = full[:rows, :lanes], full[:rows, lanes:]
            neg_pos, neg_neg = full[rows:, :lanes], full[rows:, lanes:]
            out_ref[k, 0 + part] = (pos_pos + neg_neg).astype(jnp.bfloat16)
            out_ref[k, 2 + part] = (pos_pos - neg_neg).astype(jnp.bfloat16)
            out_ref[k, 4 + part] = (pos_neg + neg_pos).astype(jnp.bfloat16)
            out_ref[k, 6 + part] = (pos_neg - neg_pos).astype(jnp.bfloat16)


def edges_kernel(mask_ref, target_ref, near_ref, cross_ref, goal_ref, stage_ref, sems):
    tile = mask_ref.shape[0]
    whole = pltpu.make_async_copy(target_ref.at[:, tile:], goal_ref, sems.at[2])
    copies = []
    for index, start in enumerate(sides(tile - AMBIT)):
        copy = pltpu.make_async_copy(
            mask_ref.at[pl.ds(start, AMBIT)], stage_ref.at[index], sems.at[index]
        )
        copy.start()
        copies.append(copy)
    whole.start()
    for index, out_ref in enumerate((near_ref, cross_ref)):
        copies[index].wait()
        out_ref[...] = stage_ref[index].astype(jnp.bfloat16)
    whole.wait()


def early_kernel(
    rows, lanes, count, mask_ref, pupils_ref, table_ref, weights_ref, row_ref, col_ref,
    mid_ref, out_ref, rest_ref, pupil_stage, sems,
):
    tile = mask_ref.shape[0]
    pupil_copy = pltpu.make_async_copy(pupils_ref.at[:, pl.ds(0, count)], pupil_stage, sems.at[0])
    pupil_copy.start()
    rest = pupils_ref.shape[1] - count
    rest_copy = pltpu.make_async_copy(pupils_ref.at[:, pl.ds(count, rest)], rest_ref, sems.at[1])
    rest_copy.start()
    mid_ref[...] = dot(
        table_ref[:, AMBIT : AMBIT + tile], mask_ref[...].astype(jnp.bfloat16)
    )
    pupil_copy.wait()
    pupil_steps(rows, lanes, 0, count, pupil_stage, weights_ref, row_ref, col_ref, out_ref)
    rest_copy.wait()


def partial_kernel(
    live_ref, mid_ref, near_ref, cross_ref, table_ref, col_t_ref, own_ref, low_ref, sent_ref
):
    extent = table_ref.shape[1]
    width = mid_ref.shape[1]
    tile = extent - 2 * AMBIT
    total = mid_ref[...]
    for start, rim_ref in zip(sides(extent - AMBIT), (near_ref, cross_ref)):
        total = total + dot(table_ref[:, pl.ds(start, AMBIT)], rim_ref[...])
    total = total.astype(jnp.bfloat16)
    own_ref[...] = total[:, : tile + AMBIT]
    low_ref[...] = total[:, :AMBIT]
    sent_ref[:, :AMBIT] = total[:, width - AMBIT :]
    main = dot(total[:, tile - AMBIT :], col_t_ref[: tile + AMBIT])
    shape = main.shape
    flag = (lax.broadcasted_iota(jnp.int32, shape, 0) == shape[0] - 1) & (
        lax.broadcasted_iota(jnp.int32, shape, 1) == shape[1] - 1
    )
    live = live_ref[:, live_ref.shape[1] - 1 :].astype(jnp.float32)
    sent_ref[:, AMBIT:] = jnp.where(flag, live, main).astype(jnp.bfloat16)


def late_kernel(
    rows, lanes, first, last, pupils_ref, own_ref, col_t_ref, quads_ref, weights_ref, row_ref, col_ref,
    base_ref, out_ref,
):
    out_ref[:first] = quads_ref[...]
    base_ref[...] = dot(own_ref[...], col_t_ref[AMBIT:])
    pupil_steps(rows, lanes, first, last, pupils_ref, weights_ref, row_ref, col_ref, out_ref)


def in_groups(count, group, run):
    def one(index, carry):
        run(index * group, False)
        return carry

    if count > group:
        lax.fori_loop(0, count // group - 1, one, 0)
    run(count - group, True)


def core_kernel(
    rows,
    lanes,
    live_ref,
    base_ref,
    sent_ref,
    low_ref,
    goal_ref,
    other_ref,
    pupil_ref,
    row_ref,
    row_t_ref,
    col_ref,
    col_t_ref,
    out_ref,
    spec_ref,
    amp_ref,
    sec_ref,
    field_ref,
    total_ref,
    slope_ref,
    back_ref,
    sum_ref,
    ans_ref,
):
    tile = goal_ref.shape[0]
    extent = row_ref.shape[1]
    kernels = pupil_ref.shape[0]
    halves = [slice(start, start + 2 * LANE) for start in range(0, tile, 2 * LANE)]
    inner = slice(AMBIT, AMBIT + tile)
    outer = lax.axis_index("col") == 0
    left = sent_ref[:, :AMBIT]
    left = jnp.where(outer, jnp.zeros_like(left), left)
    spec_ref[0] = base_ref[...] + dot(left, col_t_ref[:AMBIT])
    right = low_ref[...]
    right = jnp.where(outer, jnp.zeros_like(right), right)
    spec_ref[1] = sent_ref[:, AMBIT:].astype(jnp.float32) + dot(right, col_t_ref[extent - AMBIT :])
    corner = sent_ref[2 * rows - 16 :, AMBIT + 2 * lanes - LANE :].astype(jnp.float32)
    other_live = jnp.max(corner[15:, LANE - 1 :])
    own_live = jnp.max(live_ref[:, :1].astype(jnp.float32))
    out_ref[...] = jnp.zeros_like(out_ref)

    def work(item, carry):
        live = jnp.where(item == 0, own_live, other_live) > 0.0

        @pl.when(live)
        def _():
            spec = spec_ref[item]
            cc, cs = spec[:rows, :lanes], spec[:rows, lanes:]
            sc, ss = spec[rows:, :lanes], spec[rows:, lanes:]
            sum_ref[0] = cc - ss
            sum_ref[1] = sc + cs
            sum_ref[2] = cc + ss
            sum_ref[3] = sc - cs

            def pupil(k, index):
                return pupil_ref[k, index].astype(jnp.float32)

            def section(k, buf):
                u, v, m, n = sum_ref[0], sum_ref[1], sum_ref[2], sum_ref[3]
                pr, pi, mr, mi = (pupil(k, index) for index in range(4))
                big_re = pr * u + mi * v
                big_im = pi * u - mr * v
                small_re = mr * u + pi * v
                small_im = mi * u - pr * v
                pr, pi, mr, mi = (pupil(k, index) for index in range(4, 8))
                big_re2 = pr * m + mi * n
                big_im2 = pi * m - mr * n
                small_re2 = mr * m + pi * n
                small_im2 = mi * m - pr * n

                def pair(place, left, right):
                    where = slice(place * rows, (place + 1) * rows)
                    amp_ref[buf, where, :lanes] = left.astype(jnp.bfloat16)
                    amp_ref[buf, where, lanes:] = right.astype(jnp.bfloat16)

                pair(0, big_re + big_re2, small_im2 - small_im)
                pair(1, -(small_im + small_im2), big_re2 - big_re)
                pair(2, big_im + big_im2, small_re - small_re2)
                pair(3, small_re + small_re2, big_im2 - big_im)
                sec_ref[buf] = dot(amp_ref[buf], col_ref[:, inner]).astype(jnp.bfloat16)

            def field(ks, bufs):
                for where in halves:
                    energy = None
                    for k, buf in zip(ks, bufs):
                        real = dot(row_t_ref[inner], sec_ref[buf, : 2 * rows, where])
                        imag = dot(row_t_ref[inner], sec_ref[buf, 2 * rows :, where])
                        field_ref[k, 0, :, where] = real.astype(jnp.bfloat16)
                        field_ref[k, 1, :, where] = imag.astype(jnp.bfloat16)
                        term = real * real + imag * imag
                        energy = term if energy is None else energy + term
                    total_ref[:, where] += energy

            section(0, 0)
            section(1, 1)
            total_ref[...] = jnp.full_like(total_ref, -0.5 * steepness * threshold_level)

            def forward(first, last_group):
                for step in range(0, 4, 2):
                    bufs, nexts = (0, 1), (2, 3)
                    if step:
                        bufs, nexts = nexts, bufs
                    k = first + step
                    more = step == 0 or not last_group
                    field((k, k + 1), bufs)
                    if more:
                        section(k + 2, nexts[0])
                        section(k + 3, nexts[1])

            in_groups(kernels, 4, forward)

            def back(ks, bufs):
                for where in halves:
                    for k, buf in zip(ks, bufs):
                        for part in range(2):
                            cotangent = slope_ref[:, where] * field_ref[k, part, :, where]
                            place = slice(part * 2 * rows, (part + 1) * 2 * rows)
                            back_ref[buf, place, where] = dot(
                                row_ref[:, inner], cotangent
                            ).astype(jnp.bfloat16)

            def adjoint(k, buf):
                wave = dot(back_ref[buf], col_t_ref[inner])
                rcc, rcs = wave[:rows, :lanes], wave[:rows, lanes:]
                rsc, rss = wave[rows : 2 * rows, :lanes], wave[rows : 2 * rows, lanes:]
                icc, ics = wave[2 * rows : 3 * rows, :lanes], wave[2 * rows : 3 * rows, lanes:]
                isc, iss = wave[3 * rows :, :lanes], wave[3 * rows :, lanes:]
                ur, ui, vr, vi = rcc - rss, icc - iss, rsc + rcs, isc + ics
                pr, pi, mr, mi = (pupil(k, index) for index in range(4))
                ans_ref[0] += pr * ur + pi * ui + mr * vi - mi * vr
                ans_ref[1] += mr * ui - mi * ur - pr * vr - pi * vi
                ur, ui, vr, vi = rcc + rss, icc + iss, rsc - rcs, isc - ics
                pr, pi, mr, mi = (pupil(k, index) for index in range(4, 8))
                ans_ref[2] += pr * ur + pi * ui + mr * vi - mi * vr
                ans_ref[3] += mr * ui - mi * ur - pr * vr - pi * vi

            ans_ref[...] = jnp.zeros_like(ans_ref)

            def slopes(ref):
                for where in halves:
                    level = jnp.tanh(total_ref[:, where])
                    excess = 0.5 * level + 0.5 - ref[:, where].astype(jnp.float32)
                    slope_ref[:, where] = (excess * (1.0 - level * level)).astype(jnp.bfloat16)
                back((0, 1), (0, 1))

            @pl.when(item == 0)
            def _():
                slopes(goal_ref)

            @pl.when(item > 0)
            def _():
                slopes(other_ref)

            def backward(first, last_group):
                for step in range(0, 4, 2):
                    bufs, nexts = (0, 1), (2, 3)
                    if step:
                        bufs, nexts = nexts, bufs
                    k = first + step
                    adjoint(k, bufs[0])
                    adjoint(k + 1, bufs[1])
                    if step == 0 or not last_group:
                        back((k + 2, k + 3), nexts)

            in_groups(kernels, 4, backward)

            def answer(first):
                left, right = slice(first, first + lanes), slice(first + lanes, first + 2 * lanes)
                out_ref[:rows, left] = (ans_ref[0] + ans_ref[2]).astype(jnp.bfloat16)
                out_ref[:rows, right] = (ans_ref[3] - ans_ref[1]).astype(jnp.bfloat16)
                out_ref[rows:, left] = (-(ans_ref[1] + ans_ref[3])).astype(jnp.bfloat16)
                out_ref[rows:, right] = (ans_ref[2] - ans_ref[0]).astype(jnp.bfloat16)

            @pl.when(item == 0)
            def _():
                answer(0)

            @pl.when(item > 0)
            def _():
                answer(2 * lanes)

        return carry

    lax.fori_loop(0, 2, work, 0)


def returned_kernel(tile, mine_ref, sent_ref, row_t_ref, col_ref, out_ref, near_ref, cross_ref, sum_ref):
    width = out_ref.shape[1]
    extent = row_t_ref.shape[0]
    lanes = mine_ref.shape[1] // 2
    place = lax.axis_index("col")
    before, after = mine_ref[:, lanes:], sent_ref[:, :lanes]
    before = jnp.where(place == 0, jnp.zeros_like(before), before)
    after = jnp.where(place == lax.axis_size("col") - 1, jnp.zeros_like(after), after)
    sum_ref[...] = jnp.zeros_like(sum_ref)
    for place, value in zip(range(-1, 3), (before, mine_ref[:, :lanes], sent_ref[:, lanes:], after)):
        start = place * tile - AMBIT
        low, high = max(0, start), min(width, start + extent)
        sum_ref[:, low:high] += dot(value, col_ref[:, low - start : high - start])
    mixed = sum_ref[...].astype(jnp.bfloat16)
    out_ref[...] = mixed
    for start, rim_ref in zip(sides(extent - AMBIT), (near_ref, cross_ref)):
        rim_ref[...] = dot(row_t_ref[pl.ds(start, AMBIT)], mixed).astype(jnp.bfloat16)


def update_kernel(mask_ref, mixed_ref, near_ref, row_t_ref, out_ref, rim_ref, stage_ref, sem):
    tile = mask_ref.shape[0]
    stage_ref[...] = mask_ref[...] - step_rate * dot(
        row_t_ref[AMBIT : AMBIT + tile], mixed_ref[...]
    )
    near, cross = (pl.ds(start, AMBIT) for start in sides(tile - AMBIT))
    stage_ref[near] = stage_ref[near] - step_rate * near_ref[...].astype(jnp.float32)
    kept = pl.ds(pl.multiple_of((1 - lax.rem(lax.axis_index("row"), 2)) * AMBIT, AMBIT), tile - AMBIT)
    copy = pltpu.make_async_copy(stage_ref.at[kept], out_ref.at[kept], sem)
    copy.start()
    rim_ref[...] = stage_ref[cross]
    copy.wait()


def rim_kernel(cross_ref, rim_ref, base_ref, out_ref, stage_ref, sem):
    start = sides(out_ref.shape[0] - AMBIT)[1]
    stage_ref[...] = rim_ref[...] - step_rate * cross_ref[...].astype(jnp.float32)
    copy = pltpu.make_async_copy(stage_ref, out_ref.at[pl.ds(start, AMBIT)], sem)
    copy.start()
    copy.wait()


def body(mask, target, live, pupils, weights):
    tile, width = mask.shape
    kernels, size = pupils.shape[1], pupils.shape[2]
    half = size // 2
    rows, lanes = round_up(half + 1, 16), round_up(half + 2, LANE)
    extent = tile + 2 * AMBIT
    row_np = half_tables(half, rows, extent)
    col_np = half_tables(half, lanes, extent)
    row_pick, col_pick = (
        jnp.asarray(pick, jnp.bfloat16) for pick in pick_tables(half, rows, lanes)
    )
    row_table, row_table_t = jnp.asarray(row_np, jnp.bfloat16), jnp.asarray(row_np.T, jnp.bfloat16)
    col_table, col_table_t = jnp.asarray(col_np, jnp.bfloat16), jnp.asarray(col_np.T, jnp.bfloat16)
    bf16, f32 = jnp.bfloat16, jnp.float32
    shape = jax.ShapeDtypeStruct
    weights = weights.reshape(1, kernels)
    early = kernels // 2

    hbm = pl.BlockSpec(memory_space=pltpu.HBM)
    dma = pltpu.SemaphoreType.DMA
    edge = shape((AMBIT, width), bf16)
    near, cross, goal = call(
        edges_kernel,
        (edge, edge, shape((tile, tile), bf16)),
        [hbm, hbm],
        scratch=[pltpu.VMEM((2, AMBIT, width), f32), dma((3,))],
        limit=52,
    )(mask, target)
    other_goal = turned(goal, "col", 1)
    cross = swapped(cross, "row", 1)
    near = swapped(near, "row", 0)
    middle, quads, rest = call(
        partial(early_kernel, rows, lanes, early),
        (
            shape((2 * rows, width), f32),
            shape((early, 8, rows, lanes), bf16),
            shape((2, kernels - early, size, size), f32),
        ),
        [*vmem(1), hbm, *vmem(4)],
        scratch=[pltpu.VMEM((2, early, size, size), f32), dma((2,))],
        limit=48,
        us=4,
    )(mask, pupils, row_table, weights, row_pick, col_pick)
    own, low, sending = call(
        partial_kernel,
        (
            shape((2 * rows, tile + AMBIT), bf16),
            shape((2 * rows, AMBIT), bf16),
            shape((2 * rows, AMBIT + 2 * lanes), bf16),
        ),
        vmem(6),
    )(live, middle, near, cross, row_table, col_table_t)
    sent = turned(sending, "col", 1)
    base, all_quads = call(
        partial(late_kernel, rows, lanes, early, kernels),
        (shape((2 * rows, 2 * lanes), f32), shape((kernels, 8, rows, lanes), bf16)),
        vmem(7),
        limit=16,
        us=4,
    )(rest, own, col_table_t, quads, weights, row_pick, col_pick)
    answers = call(
        partial(core_kernel, rows, lanes),
        shape((2 * rows, 4 * lanes), bf16),
        vmem(11),
        scratch=[
            pltpu.VMEM((2, 2 * rows, 2 * lanes), f32),
            pltpu.VMEM((4, 4 * rows, 2 * lanes), bf16),
            pltpu.VMEM((4, 4 * rows, tile), bf16),
            pltpu.VMEM((kernels, 2, tile, tile), bf16),
            pltpu.VMEM((tile, tile), f32),
            pltpu.VMEM((tile, tile), bf16),
            pltpu.VMEM((4, 4 * rows, tile), bf16),
            pltpu.VMEM((4, rows, lanes), f32),
            pltpu.VMEM((4, rows, lanes), f32),
        ],
        limit=36,
        us=15,
    )(
        live, base, sent, low, target, other_goal, all_quads,
        row_table, row_table_t, col_table, col_table_t,
    )
    returned = turned(answers, "col", -1)
    mixed, near, cross = call(
        partial(returned_kernel, tile),
        (shape((2 * rows, width), bf16), shape((AMBIT, width), bf16), shape((AMBIT, width), bf16)),
        vmem(4),
        scratch=[pltpu.VMEM((2 * rows, width), f32)],
    )(answers, returned, row_table_t, col_table)
    cross = swapped(cross, "row", 1)
    near = swapped(near, "row", 0)
    anywhere = pl.BlockSpec(memory_space=pl.ANY)
    whole, rim = shape((tile, width), f32), shape((AMBIT, width), f32)
    updated, rim = pl.pallas_call(
        update_kernel,
        out_shape=(whole, rim),
        in_specs=vmem(4),
        out_specs=(anywhere, *vmem(1)),
        scratch_shapes=[pltpu.VMEM((tile, width), f32), dma],
        cost_estimate=pl.CostEstimate(flops=10**9, bytes_accessed=2 * 10**6, transcendentals=0),
        compiler_params=pltpu.CompilerParams(vmem_limit_bytes=16 * MIB),
    )(mask, mixed, near, row_table_t)
    return pl.pallas_call(
        rim_kernel,
        out_shape=whole,
        in_specs=[*vmem(2), anywhere],
        out_specs=anywhere,
        scratch_shapes=[pltpu.VMEM((AMBIT, width), f32), dma],
        input_output_aliases={2: 0},
        compiler_params=pltpu.CompilerParams(vmem_limit_bytes=8 * MIB),
    )(cross, rim, updated)


def solution(mesh):
    placed = (P("row", "col"), P("row", "col"), P("row", "col"), P(), P())
    return jax.shard_map(
        body, mesh=mesh, in_specs=placed, out_specs=P("row", "col"), check_vma=False
    )
```

```python
from functools import partial
import math

import jax
import jax.numpy as jnp
import numpy as np
from jax import lax
from jax.experimental import pallas as pl
from jax.experimental.pallas import tpu as pltpu
from jax.sharding import PartitionSpec as P


AMBIT = 128
LANE = 128

steepness = 4.0
threshold_level = 1.0
step_rate = 8.0

MIB = 1024 * 1024


def round_up(value, unit):
    return -(-value // unit) * unit


def swapped(block, axis, offset):
    count = lax.axis_size(axis)
    pairs = []
    for low in range(offset, count - 1, 2):
        pairs += [(low, low + 1), (low + 1, low)]
    return lax.ppermute(block, axis, pairs)


def sides(reach):
    odd = lax.rem(lax.axis_index("row"), 2)
    return [pl.multiple_of(side * reach, AMBIT) for side in (1 - odd, odd)]


def turned(block, axis, step):
    count = lax.axis_size(axis)
    return lax.ppermute(block, axis, [(i, (i + step) % count) for i in range(count)])


def dot(leading, trailing):
    return jnp.dot(leading, trailing, preferred_element_type=jnp.float32)


def half_tables(half, rows, extent):
    frequency = np.arange(half + 1, dtype=np.int64)
    pixels = np.arange(extent, dtype=np.int64)
    phases = np.mod(frequency[:, None] * pixels[None, :], extent).astype(np.float32)
    angles = phases * np.float32(2.0 * math.pi / extent)
    factor = np.float32(1.0 / math.sqrt(extent))
    table = np.zeros((2 * rows, extent), np.float32)
    table[: half + 1] = np.cos(angles) * factor
    table[rows : rows + half + 1] = np.sin(angles) * factor
    return table


def pick_tables(half, rows, lanes):
    size = 2 * half
    row_pick = np.zeros((2 * rows, size), np.float32)
    col_pick = np.zeros((size, 2 * lanes), np.float32)
    for index in range(half):
        row_pick[index, half + index] = 1.0
        col_pick[half + index, index] = 1.0
        row_pick[rows + half - index, index] = 1.0
        col_pick[index, lanes + half - index] = 1.0
    return row_pick, col_pick


def vmem(count):
    return [pl.BlockSpec(memory_space=pltpu.VMEM)] * count


def call(kernel, outs, specs, scratch=(), limit=16, us=1, **kwargs):
    return pl.pallas_call(
        kernel,
        out_shape=outs,
        in_specs=specs,
        out_specs=jax.tree.map(lambda _: pl.BlockSpec(memory_space=pltpu.VMEM), outs),
        scratch_shapes=list(scratch),
        cost_estimate=pl.CostEstimate(
            flops=int(us * 5e8), bytes_accessed=int(us * 1e6), transcendentals=0
        ),
        compiler_params=pltpu.CompilerParams(vmem_limit_bytes=limit * MIB),
        **kwargs,
    )


def pupil_steps(rows, lanes, first, last, pupils_ref, weights_ref, row_ref, col_ref, out_ref):
    for k in range(first, last):
        scale = jnp.sqrt(weights_ref[:, k : k + 1] * (0.5 * steepness))
        for part in range(2):
            values = (pupils_ref[part, k - first] * scale).astype(jnp.bfloat16)
            columns = dot(values, col_ref[...]).astype(jnp.bfloat16)
            full = dot(row_ref[...], columns)
            pos_pos, pos_neg = full[:rows, :lanes], full[:rows, lanes:]
            neg_pos, neg_neg = full[rows:, :lanes], full[rows:, lanes:]
            out_ref[k, 0 + part] = (pos_pos + neg_neg).astype(jnp.bfloat16)
            out_ref[k, 2 + part] = (pos_pos - neg_neg).astype(jnp.bfloat16)
            out_ref[k, 4 + part] = (pos_neg + neg_pos).astype(jnp.bfloat16)
            out_ref[k, 6 + part] = (pos_neg - neg_pos).astype(jnp.bfloat16)


def edges_kernel(mask_ref, target_ref, near_ref, cross_ref, goal_ref, stage_ref, sems):
    tile = mask_ref.shape[0]
    whole = pltpu.make_async_copy(target_ref.at[:, tile:], goal_ref, sems.at[2])
    copies = []
    for index, start in enumerate(sides(tile - AMBIT)):
        copy = pltpu.make_async_copy(
            mask_ref.at[pl.ds(start, AMBIT)], stage_ref.at[index], sems.at[index]
        )
        copy.start()
        copies.append(copy)
    whole.start()
    for index, out_ref in enumerate((near_ref, cross_ref)):
        copies[index].wait()
        out_ref[...] = stage_ref[index].astype(jnp.bfloat16)
    whole.wait()


def early_kernel(
    rows, lanes, count, mask_ref, pupils_ref, table_ref, weights_ref, row_ref, col_ref,
    mid_ref, out_ref, rest_ref, pupil_stage, sems,
):
    tile = mask_ref.shape[0]
    pupil_copy = pltpu.make_async_copy(pupils_ref.at[:, pl.ds(0, count)], pupil_stage, sems.at[0])
    pupil_copy.start()
    rest = pupils_ref.shape[1] - count
    rest_copy = pltpu.make_async_copy(pupils_ref.at[:, pl.ds(count, rest)], rest_ref, sems.at[1])
    rest_copy.start()
    mid_ref[...] = dot(
        table_ref[:, AMBIT : AMBIT + tile], mask_ref[...].astype(jnp.bfloat16)
    )
    pupil_copy.wait()
    pupil_steps(rows, lanes, 0, count, pupil_stage, weights_ref, row_ref, col_ref, out_ref)
    rest_copy.wait()


def partial_kernel(
    live_ref, mid_ref, near_ref, cross_ref, table_ref, col_t_ref, own_ref, low_ref, sent_ref
):
    extent = table_ref.shape[1]
    width = mid_ref.shape[1]
    tile = extent - 2 * AMBIT
    total = mid_ref[...]
    for start, rim_ref in zip(sides(extent - AMBIT), (near_ref, cross_ref)):
        total = total + dot(table_ref[:, pl.ds(start, AMBIT)], rim_ref[...])
    total = total.astype(jnp.bfloat16)
    own_ref[...] = total[:, : tile + AMBIT]
    low_ref[...] = total[:, :AMBIT]
    sent_ref[:, :AMBIT] = total[:, width - AMBIT :]
    main = dot(total[:, tile - AMBIT :], col_t_ref[: tile + AMBIT])
    shape = main.shape
    flag = (lax.broadcasted_iota(jnp.int32, shape, 0) == shape[0] - 1) & (
        lax.broadcasted_iota(jnp.int32, shape, 1) == shape[1] - 1
    )
    live = live_ref[:, live_ref.shape[1] - 1 :].astype(jnp.float32)
    sent_ref[:, AMBIT:] = jnp.where(flag, live, main).astype(jnp.bfloat16)


def late_kernel(
    rows, lanes, first, last, pupils_ref, own_ref, col_t_ref, quads_ref, weights_ref, row_ref, col_ref,
    base_ref, out_ref,
):
    out_ref[:first] = quads_ref[...]
    base_ref[...] = dot(own_ref[...], col_t_ref[AMBIT:])
    pupil_steps(rows, lanes, first, last, pupils_ref, weights_ref, row_ref, col_ref, out_ref)


def in_groups(count, group, run):
    def one(index, carry):
        run(index * group, False)
        return carry

    if count > group:
        lax.fori_loop(0, count // group - 1, one, 0)
    run(count - group, True)


def core_kernel(
    rows,
    lanes,
    live_ref,
    base_ref,
    sent_ref,
    low_ref,
    goal_ref,
    other_ref,
    pupil_ref,
    row_ref,
    row_t_ref,
    col_ref,
    col_t_ref,
    out_ref,
    spec_ref,
    amp_ref,
    sec_ref,
    field_ref,
    total_ref,
    slope_ref,
    back_ref,
    sum_ref,
    ans_ref,
):
    tile = goal_ref.shape[0]
    extent = row_ref.shape[1]
    kernels = pupil_ref.shape[0]
    halves = [slice(start, start + 2 * LANE) for start in range(0, tile, 2 * LANE)]
    inner = slice(AMBIT, AMBIT + tile)
    outer = lax.axis_index("col") == 0
    left = sent_ref[:, :AMBIT]
    left = jnp.where(outer, jnp.zeros_like(left), left)
    spec_ref[0] = base_ref[...] + dot(left, col_t_ref[:AMBIT])
    right = low_ref[...]
    right = jnp.where(outer, jnp.zeros_like(right), right)
    spec_ref[1] = sent_ref[:, AMBIT:].astype(jnp.float32) + dot(right, col_t_ref[extent - AMBIT :])
    corner = sent_ref[2 * rows - 16 :, AMBIT + 2 * lanes - LANE :].astype(jnp.float32)
    other_live = jnp.max(corner[15:, LANE - 1 :])
    own_live = jnp.max(live_ref[:, :1].astype(jnp.float32))
    out_ref[...] = jnp.zeros_like(out_ref)

    def work(item, carry):
        live = jnp.where(item == 0, own_live, other_live) > 0.0

        @pl.when(live)
        def _():
            spec = spec_ref[item]
            cc, cs = spec[:rows, :lanes], spec[:rows, lanes:]
            sc, ss = spec[rows:, :lanes], spec[rows:, lanes:]
            sum_ref[0] = cc - ss
            sum_ref[1] = sc + cs
            sum_ref[2] = cc + ss
            sum_ref[3] = sc - cs

            def pupil(k, index):
                return pupil_ref[k, index].astype(jnp.float32)

            def section(k, buf):
                u, v, m, n = sum_ref[0], sum_ref[1], sum_ref[2], sum_ref[3]
                pr, pi, mr, mi = (pupil(k, index) for index in range(4))
                big_re = pr * u + mi * v
                big_im = pi * u - mr * v
                small_re = mr * u + pi * v
                small_im = mi * u - pr * v
                pr, pi, mr, mi = (pupil(k, index) for index in range(4, 8))
                big_re2 = pr * m + mi * n
                big_im2 = pi * m - mr * n
                small_re2 = mr * m + pi * n
                small_im2 = mi * m - pr * n

                def pair(place, left, right):
                    where = slice(place * rows, (place + 1) * rows)
                    amp_ref[buf, where, :lanes] = left.astype(jnp.bfloat16)
                    amp_ref[buf, where, lanes:] = right.astype(jnp.bfloat16)

                pair(0, big_re + big_re2, small_im2 - small_im)
                pair(1, -(small_im + small_im2), big_re2 - big_re)
                pair(2, big_im + big_im2, small_re - small_re2)
                pair(3, small_re + small_re2, big_im2 - big_im)
                sec_ref[buf] = dot(amp_ref[buf], col_ref[:, inner]).astype(jnp.bfloat16)

            def field(ks, bufs):
                for where in halves:
                    energy = None
                    for k, buf in zip(ks, bufs):
                        real = dot(row_t_ref[inner], sec_ref[buf, : 2 * rows, where])
                        imag = dot(row_t_ref[inner], sec_ref[buf, 2 * rows :, where])
                        field_ref[k, 0, :, where] = real.astype(jnp.bfloat16)
                        field_ref[k, 1, :, where] = imag.astype(jnp.bfloat16)
                        term = real * real + imag * imag
                        energy = term if energy is None else energy + term
                    total_ref[:, where] += energy

            section(0, 0)
            section(1, 1)
            total_ref[...] = jnp.full_like(total_ref, -0.5 * steepness * threshold_level)

            def forward(first, last_group):
                for step in range(0, 4, 2):
                    bufs, nexts = (0, 1), (2, 3)
                    if step:
                        bufs, nexts = nexts, bufs
                    k = first + step
                    more = step == 0 or not last_group
                    field((k, k + 1), bufs)
                    if more:
                        section(k + 2, nexts[0])
                        section(k + 3, nexts[1])

            in_groups(kernels, 4, forward)

            def back(ks, bufs):
                for where in halves:
                    for k, buf in zip(ks, bufs):
                        for part in range(2):
                            cotangent = slope_ref[:, where] * field_ref[k, part, :, where]
                            place = slice(part * 2 * rows, (part + 1) * 2 * rows)
                            back_ref[buf, place, where] = dot(
                                row_ref[:, inner], cotangent
                            ).astype(jnp.bfloat16)

            def adjoint(k, buf):
                wave = dot(back_ref[buf], col_t_ref[inner])
                rcc, rcs = wave[:rows, :lanes], wave[:rows, lanes:]
                rsc, rss = wave[rows : 2 * rows, :lanes], wave[rows : 2 * rows, lanes:]
                icc, ics = wave[2 * rows : 3 * rows, :lanes], wave[2 * rows : 3 * rows, lanes:]
                isc, iss = wave[3 * rows :, :lanes], wave[3 * rows :, lanes:]
                ur, ui, vr, vi = rcc - rss, icc - iss, rsc + rcs, isc + ics
                pr, pi, mr, mi = (pupil(k, index) for index in range(4))
                ans_ref[0] += pr * ur + pi * ui + mr * vi - mi * vr
                ans_ref[1] += mr * ui - mi * ur - pr * vr - pi * vi
                ur, ui, vr, vi = rcc + rss, icc + iss, rsc - rcs, isc - ics
                pr, pi, mr, mi = (pupil(k, index) for index in range(4, 8))
                ans_ref[2] += pr * ur + pi * ui + mr * vi - mi * vr
                ans_ref[3] += mr * ui - mi * ur - pr * vr - pi * vi

            ans_ref[...] = jnp.zeros_like(ans_ref)

            def slopes(ref):
                for where in halves:
                    level = jnp.tanh(total_ref[:, where])
                    excess = 0.5 * level + 0.5 - ref[:, where].astype(jnp.float32)
                    slope_ref[:, where] = (excess * (1.0 - level * level)).astype(jnp.bfloat16)
                back((0, 1), (0, 1))

            @pl.when(item == 0)
            def _():
                slopes(goal_ref)

            @pl.when(item > 0)
            def _():
                slopes(other_ref)

            def backward(first, last_group):
                for step in range(0, 4, 2):
                    bufs, nexts = (0, 1), (2, 3)
                    if step:
                        bufs, nexts = nexts, bufs
                    k = first + step
                    adjoint(k, bufs[0])
                    adjoint(k + 1, bufs[1])
                    if step == 0 or not last_group:
                        back((k + 2, k + 3), nexts)

            in_groups(kernels, 4, backward)

            def answer(first):
                left, right = slice(first, first + lanes), slice(first + lanes, first + 2 * lanes)
                out_ref[:rows, left] = (ans_ref[0] + ans_ref[2]).astype(jnp.bfloat16)
                out_ref[:rows, right] = (ans_ref[3] - ans_ref[1]).astype(jnp.bfloat16)
                out_ref[rows:, left] = (-(ans_ref[1] + ans_ref[3])).astype(jnp.bfloat16)
                out_ref[rows:, right] = (ans_ref[2] - ans_ref[0]).astype(jnp.bfloat16)

            @pl.when(item == 0)
            def _():
                answer(0)

            @pl.when(item > 0)
            def _():
                answer(2 * lanes)

        return carry

    lax.fori_loop(0, 2, work, 0)


def returned_kernel(tile, mine_ref, sent_ref, row_t_ref, col_ref, out_ref, near_ref, cross_ref, sum_ref):
    width = out_ref.shape[1]
    extent = row_t_ref.shape[0]
    lanes = mine_ref.shape[1] // 2
    place = lax.axis_index("col")
    before, after = mine_ref[:, lanes:], sent_ref[:, :lanes]
    before = jnp.where(place == 0, jnp.zeros_like(before), before)
    after = jnp.where(place == lax.axis_size("col") - 1, jnp.zeros_like(after), after)
    sum_ref[...] = jnp.zeros_like(sum_ref)
    for place, value in zip(range(-1, 3), (before, mine_ref[:, :lanes], sent_ref[:, lanes:], after)):
        start = place * tile - AMBIT
        low, high = max(0, start), min(width, start + extent)
        sum_ref[:, low:high] += dot(value, col_ref[:, low - start : high - start])
    mixed = sum_ref[...].astype(jnp.bfloat16)
    out_ref[...] = mixed
    for start, rim_ref in zip(sides(extent - AMBIT), (near_ref, cross_ref)):
        rim_ref[...] = dot(row_t_ref[pl.ds(start, AMBIT)], mixed).astype(jnp.bfloat16)


def update_kernel(mask_ref, mixed_ref, near_ref, row_t_ref, out_ref, rim_ref, stage_ref, sem):
    tile = mask_ref.shape[0]
    stage_ref[...] = mask_ref[...] - step_rate * dot(
        row_t_ref[AMBIT : AMBIT + tile], mixed_ref[...]
    )
    near, cross = (pl.ds(start, AMBIT) for start in sides(tile - AMBIT))
    stage_ref[near] = stage_ref[near] - step_rate * near_ref[...].astype(jnp.float32)
    kept = pl.ds(pl.multiple_of((1 - lax.rem(lax.axis_index("row"), 2)) * AMBIT, AMBIT), tile - AMBIT)
    copy = pltpu.make_async_copy(stage_ref.at[kept], out_ref.at[kept], sem)
    copy.start()
    rim_ref[...] = stage_ref[cross]
    copy.wait()


def rim_kernel(cross_ref, rim_ref, base_ref, out_ref, stage_ref, sem):
    start = sides(out_ref.shape[0] - AMBIT)[1]
    step = AMBIT // 2
    copies = []
    for index in range(2):
        where = pl.ds(index * step, step)
        stage_ref[where] = rim_ref[where] - step_rate * cross_ref[where].astype(jnp.float32)
        copy = pltpu.make_async_copy(
            stage_ref.at[where],
            out_ref.at[pl.ds(pl.multiple_of(start + index * step, step), step)],
            sem.at[index],
        )
        copy.start()
        copies.append(copy)
    for copy in copies:
        copy.wait()


def body(mask, target, live, pupils, weights):
    tile, width = mask.shape
    kernels, size = pupils.shape[1], pupils.shape[2]
    half = size // 2
    rows, lanes = round_up(half + 1, 16), round_up(half + 2, LANE)
    extent = tile + 2 * AMBIT
    row_np = half_tables(half, rows, extent)
    col_np = half_tables(half, lanes, extent)
    row_pick, col_pick = (
        jnp.asarray(pick, jnp.bfloat16) for pick in pick_tables(half, rows, lanes)
    )
    row_table, row_table_t = jnp.asarray(row_np, jnp.bfloat16), jnp.asarray(row_np.T, jnp.bfloat16)
    col_table, col_table_t = jnp.asarray(col_np, jnp.bfloat16), jnp.asarray(col_np.T, jnp.bfloat16)
    bf16, f32 = jnp.bfloat16, jnp.float32
    shape = jax.ShapeDtypeStruct
    weights = weights.reshape(1, kernels)
    early = kernels // 2

    hbm = pl.BlockSpec(memory_space=pltpu.HBM)
    dma = pltpu.SemaphoreType.DMA
    edge = shape((AMBIT, width), bf16)
    near, cross, goal = call(
        edges_kernel,
        (edge, edge, shape((tile, tile), bf16)),
        [hbm, hbm],
        scratch=[pltpu.VMEM((2, AMBIT, width), f32), dma((3,))],
        limit=52,
    )(mask, target)
    other_goal = turned(goal, "col", 1)
    cross = swapped(cross, "row", 1)
    near = swapped(near, "row", 0)
    middle, quads, rest = call(
        partial(early_kernel, rows, lanes, early),
        (
            shape((2 * rows, width), f32),
            shape((early, 8, rows, lanes), bf16),
            shape((2, kernels - early, size, size), f32),
        ),
        [*vmem(1), hbm, *vmem(4)],
        scratch=[pltpu.VMEM((2, early, size, size), f32), dma((2,))],
        limit=48,
        us=4,
    )(mask, pupils, row_table, weights, row_pick, col_pick)
    own, low, sending = call(
        partial_kernel,
        (
            shape((2 * rows, tile + AMBIT), bf16),
            shape((2 * rows, AMBIT), bf16),
            shape((2 * rows, AMBIT + 2 * lanes), bf16),
        ),
        vmem(6),
    )(live, middle, near, cross, row_table, col_table_t)
    sent = turned(sending, "col", 1)
    base, all_quads = call(
        partial(late_kernel, rows, lanes, early, kernels),
        (shape((2 * rows, 2 * lanes), f32), shape((kernels, 8, rows, lanes), bf16)),
        vmem(7),
        limit=16,
        us=4,
    )(rest, own, col_table_t, quads, weights, row_pick, col_pick)
    answers = call(
        partial(core_kernel, rows, lanes),
        shape((2 * rows, 4 * lanes), bf16),
        vmem(11),
        scratch=[
            pltpu.VMEM((2, 2 * rows, 2 * lanes), f32),
            pltpu.VMEM((4, 4 * rows, 2 * lanes), bf16),
            pltpu.VMEM((4, 4 * rows, tile), bf16),
            pltpu.VMEM((kernels, 2, tile, tile), bf16),
            pltpu.VMEM((tile, tile), f32),
            pltpu.VMEM((tile, tile), bf16),
            pltpu.VMEM((4, 4 * rows, tile), bf16),
            pltpu.VMEM((4, rows, lanes), f32),
            pltpu.VMEM((4, rows, lanes), f32),
        ],
        limit=36,
        us=15,
    )(
        live, base, sent, low, target, other_goal, all_quads,
        row_table, row_table_t, col_table, col_table_t,
    )
    returned = turned(answers, "col", -1)
    mixed, near, cross = call(
        partial(returned_kernel, tile),
        (shape((2 * rows, width), bf16), shape((AMBIT, width), bf16), shape((AMBIT, width), bf16)),
        vmem(4),
        scratch=[pltpu.VMEM((2 * rows, width), f32)],
    )(answers, returned, row_table_t, col_table)
    cross = swapped(cross, "row", 1)
    near = swapped(near, "row", 0)
    anywhere = pl.BlockSpec(memory_space=pl.ANY)
    whole, rim = shape((tile, width), f32), shape((AMBIT, width), f32)
    updated, rim = pl.pallas_call(
        update_kernel,
        out_shape=(whole, rim),
        in_specs=vmem(4),
        out_specs=(anywhere, *vmem(1)),
        scratch_shapes=[pltpu.VMEM((tile, width), f32), dma],
        cost_estimate=pl.CostEstimate(flops=10**9, bytes_accessed=2 * 10**6, transcendentals=0),
        compiler_params=pltpu.CompilerParams(vmem_limit_bytes=16 * MIB),
    )(mask, mixed, near, row_table_t)
    return pl.pallas_call(
        rim_kernel,
        out_shape=whole,
        in_specs=[*vmem(2), anywhere],
        out_specs=anywhere,
        scratch_shapes=[pltpu.VMEM((AMBIT, width), f32), dma((2,))],
        input_output_aliases={2: 0},
        compiler_params=pltpu.CompilerParams(vmem_limit_bytes=8 * MIB),
    )(cross, rim, updated)


def solution(mesh):
    placed = (P("row", "col"), P("row", "col"), P("row", "col"), P(), P())
    return jax.shard_map(
        body, mesh=mesh, in_specs=placed, out_specs=P("row", "col"), check_vma=False
    )
```
